32 devices in a mesh: ctx: 16 (over z, x, core), fsdp: 2 (over y).
Axes of the slice: x: 2, y: 2, z: 4, core: 2. Of those that a mesh axis runs over, the one named last changes fastest.
Arguments:
- tokens: bfloat16 [2, 4096, 768], P('fsdp', 'ctx'), may hold values from -6 to 6
- timestep: int32 [2, 16], P('fsdp', 'ctx'), may hold values from 0 to 1023
- time_table: float32 [1024, 768], replicated, may hold values from -2 to 2
- w_qkv: bfloat16 [768, 2304], P('fsdp'), may hold values from -0.21875 to 0.21875
- w_out: bfloat16 [768, 768], P('fsdp'), may hold values from -2.5 to 2.5
- w_up: bfloat16 [768, 3072], P('fsdp'), may hold values from -0.21875 to 0.21875
- w_down: bfloat16 [3072, 768], P('fsdp'), may hold values from -0.3125 to 0.3125
- w_ada: bfloat16 [768, 3072], P('fsdp'), may hold values from -0.21875 to 0.21875
- cotangent: bfloat16 [2, 4096, 768], P('fsdp', 'ctx'), may hold values from -6 to 6
Outputs:
- output: float32 [2, 4096, 768], P('fsdp', 'ctx')
- input_grad: float32 [2, 4096, 768], P('fsdp', 'ctx')
- grad_qkv: float32 [768, 2304], P('fsdp')
- grad_out: float32 [768, 768], P('fsdp')
- grad_up: float32 [768, 3072], P('fsdp')
- grad_down: float32 [3072, 768], P('fsdp')
- grad_ada: float32 [768, 3072], P('fsdp')
The draws below stay inside these ranges and needn't reach their ends.
All inputs are finite; a program needn't handle non-finite values.
Results may differ from the reference program's by a relative error of at most 0.04.
Values may be sent and summed in bfloat16 or wider, within the bound.
A program may use at most 512 MiB of HBM per device.

```python
import math
import jax
import jax.numpy as jnp
from jax import lax

D = 768
HD = 64
FF = 3072
BLOCK = 256
NT = 1024
LENGTH = 4096
SEQS = 2
NBLK = 16


def set_ends(array, key, low, largest):
    spot = [jax.random.randint(jax.random.fold_in(key, axis), (), 0, length) for axis, length in enumerate(array.shape)]
    widest = array.shape.index(max(array.shape))
    next_to = spot[:widest] + [(spot[widest] + 1) % array.shape[widest]] + spot[widest + 1:]
    return array.at[tuple(spot)].set(low).at[tuple(next_to)].set(largest)


def shard_levels(rng, extent, cuts, low, high):
    gain = 1.0
    for position, parts in cuts:
        steps = jax.random.uniform(jax.random.fold_in(jax.random.fold_in(rng, 6), position), (parts,), jnp.float32, low / len(cuts), high / len(cuts))
        gain = gain * jnp.repeat(jnp.exp(steps), extent[position] // parts).reshape((-1,) + (1,) * (len(extent) - 1 - position))
    return gain


def normal_values(stream_key, shape, spread, bound, pieces=(), kind=jnp.bfloat16):
    values = spread * jax.random.normal(stream_key, shape, jnp.float32)
    if pieces:
        values = values * shard_levels(stream_key, shape, pieces, -0.22, 0.18)
    return jnp.clip(values, -bound, bound).astype(kind)


def setup_inputs(seed: int = 0) -> dict:
    key_list = jax.random.split(jax.random.key(seed), 10)
    tokens = normal_values(key_list[0], (SEQS, LENGTH, D), 1.0, 6.0, ((0, 2), (1, 16)))
    timestep = set_ends(jax.random.randint(key_list[1], (SEQS, NBLK), 0, NT), jax.random.fold_in(key_list[1], 1), 0, NT - 1).astype(jnp.int32)
    time_table = normal_values(key_list[2], (NT, D), 0.3, 2.0, (), jnp.float32)
    w_qkv = normal_values(key_list[3], (D, 3 * D), D ** -0.5, 0.21875, ((0, 2),))
    w_out = normal_values(key_list[4], (D, D), (max(D // 128, 1)) ** -0.5, 2.5, ((0, 2),))
    w_up = normal_values(key_list[5], (D, FF), D ** -0.5, 0.21875, ((0, 2),))
    w_down = normal_values(key_list[6], (FF, D), (max(FF // 8, 1)) ** -0.5, 0.3125, ((0, 2),))
    w_ada = normal_values(key_list[7], (D, 4 * D), D ** -0.5, 0.21875, ((0, 2),))
    cotangent = normal_values(key_list[8], (SEQS, LENGTH, D), 1.0, 6.0, ((0, 2), (1, 16)))
    return dict(tokens=tokens, timestep=timestep, time_table=time_table, w_qkv=w_qkv, w_out=w_out, w_up=w_up, w_down=w_down, w_ada=w_ada, cotangent=cotangent)


@jax.custom_vjp
def lowered_cast(v):
    return lax.optimization_barrier(v.astype(jnp.bfloat16)).astype(jnp.float32)

@jax.custom_vjp
def lowered_cast_backward(v):
    return v

def low_keep(v):
    return (lowered_cast(v), None)

def low_pass(kept, grad):
    return (grad,)

def back_keep(v):
    return (v, None)

def back_low(kept, grad):
    return (lowered_cast(grad),)
lowered_cast.defvjp(low_keep, low_pass)
lowered_cast_backward.defvjp(back_keep, back_low)
norm_eps = 1e-06
masked_score = -1e+30
rope_base = 10000.0

def layer_norm(values):
    center = values - lax.optimization_barrier(jnp.mean(values, axis=-1, keepdims=True))
    return center * lax.rsqrt(lax.optimization_barrier(jnp.mean(center * center, axis=-1, keepdims=True)) + norm_eps)

def rope_tables(positions, head_size):
    half_size = head_size // 2
    frequency = jnp.exp(jnp.arange(half_size, dtype=jnp.float32) * (-2.0 * math.log(rope_base) / head_size))
    angles = positions.astype(jnp.float32)[:, None] * frequency[None, :]
    cosine_table = jnp.concatenate([jnp.cos(angles), jnp.cos(angles)], axis=-1)[:, None, :]
    sine_table = jnp.concatenate([jnp.sin(angles), jnp.sin(angles)], axis=-1)[:, None, :]
    return (cosine_table, sine_table)

def rotate_half(values):
    middle = values.shape[-1] // 2
    return jnp.concatenate([-values[..., middle:], values[..., :middle]], axis=-1)

def rotate(values, cosine_table, sine_table):
    return values * cosine_table + rotate_half(values) * sine_table

def attend_sequence(queries, key_rows, value_rows):
    length = queries.shape[0]
    block_size = math.gcd(length, 512)
    key_block = jnp.arange(length, dtype=jnp.int32) // BLOCK
    score_scale = 1.0 / math.sqrt(HD)

    @jax.checkpoint
    def one_block(first_row):
        query_part = lax.dynamic_slice_in_dim(queries, first_row, block_size, 0)
        raw_scores = lowered_cast_backward(jnp.einsum('qhd,khd->hqk', query_part, key_rows, precision=lax.Precision.HIGHEST))
        query_block = (first_row + jnp.arange(block_size, dtype=jnp.int32)) // BLOCK
        allowed = (key_block[None, :] <= query_block[:, None])[None]
        scores = jnp.where(allowed, raw_scores * score_scale, masked_score)
        weights = jnp.exp(scores - lax.optimization_barrier(jnp.max(scores, axis=-1, keepdims=True)))
        probs = lowered_cast(weights / lax.optimization_barrier(jnp.sum(weights, axis=-1, keepdims=True)))
        return jnp.einsum('hqk,khd->qhd', probs, value_rows, precision=lax.Precision.HIGHEST)
    starts = jnp.arange(length // block_size, dtype=jnp.int32) * block_size
    return lax.map(one_block, starts).reshape(length, queries.shape[1], queries.shape[2])

def reference(tokens, timestep, time_table, w_qkv, w_out, w_up, w_down, w_ada, cotangent):
    highest_precision = lax.Precision.HIGHEST

    def forward(inputs, query_key_value_matrix, output_matrix, up_matrix, down_matrix, ada_weight):
        seq_count, length, model_width = inputs.shape
        embedded = lowered_cast(time_table[timestep])
        modulation = jnp.einsum('sbd,de->sbe', embedded, ada_weight, precision=highest_precision)
        per_token = jnp.repeat(modulation, BLOCK, axis=1)
        scale_attn, gate_attn, scale_mlp, gate_mlp = jnp.split(per_token, 4, axis=2)
        residual_first = lowered_cast(layer_norm(inputs) * (1.0 + scale_attn))
        projected_output = lowered_cast_backward(jnp.einsum('qyb,bm->qym', residual_first, query_key_value_matrix, precision=highest_precision))
        projected_output = projected_output.reshape(seq_count, length, 3, model_width // HD, HD)
        cosine_table, sine_table = rope_tables(jnp.arange(length, dtype=jnp.int32), HD)
        queries = lowered_cast(rotate(projected_output[:, :, 0], cosine_table, sine_table))
        key_rows = lowered_cast(rotate(projected_output[:, :, 1], cosine_table, sine_table))
        value_rows = lowered_cast(projected_output[:, :, 2])
        attention_mixed = lax.map(lambda sequence_parts: attend_sequence(*sequence_parts), (queries, key_rows, value_rows))
        attention_mixed = lowered_cast_backward(attention_mixed.reshape(seq_count, length, model_width))
        attention_projected = lowered_cast_backward(jnp.einsum('qyb,bm->qym', lowered_cast(attention_mixed), output_matrix, precision=highest_precision))
        middle = inputs + gate_attn * attention_projected
        residual_second = lowered_cast(layer_norm(middle) * (1.0 + scale_mlp))
        before_activation = lowered_cast_backward(jnp.einsum('ogi,iy->ogy', residual_second, up_matrix, precision=highest_precision))
        gelu_activated = lowered_cast(jax.nn.gelu(before_activation, approximate=True))
        feedforward_output = lowered_cast_backward(jnp.einsum('vqy,yx->vqx', gelu_activated, down_matrix, precision=highest_precision))
        return middle + gate_mlp * feedforward_output
    weights_f = (w_qkv.astype(jnp.float32), w_out.astype(jnp.float32), w_up.astype(jnp.float32), w_down.astype(jnp.float32), w_ada.astype(jnp.float32))
    result, backward = jax.vjp(forward, tokens.astype(jnp.float32), *weights_f)
    gradients = backward(cotangent.astype(jnp.float32))
    return (result, gradients[0], gradients[1], gradients[2], gradients[3], gradients[4], gradients[5])
```

```python
import functools
import math

import jax
import jax.numpy as jnp
from jax import lax
from jax.experimental import pallas as pl
from jax.experimental.pallas import tpu as pltpu
from jax.sharding import PartitionSpec as P

HD = 64
BLOCK = 256
VMEM_LIMIT = 60 * 1024 * 1024
MESH = pl.DeviceIdType.MESH


norm_eps = 1e-06
masked_score = -1e30
rope_base = 10000.0


def layer_norm(values):
    center = values - jnp.mean(values, axis=-1, keepdims=True)
    inverse = lax.rsqrt(jnp.mean(center * center, axis=-1, keepdims=True) + norm_eps)
    return (center * inverse, inverse)


def norm_back(grad_norm, normed, inverse):
    mean_grad = jnp.mean(grad_norm, axis=-1, keepdims=True)
    mean_cross = jnp.mean(grad_norm * normed, axis=-1, keepdims=True)
    return inverse * (grad_norm - mean_grad - normed * mean_cross)


def rope_tables(positions, head_size):
    half_size = head_size // 2
    frequency = jnp.exp(
        jnp.arange(half_size, dtype=jnp.float32) * (-2.0 * math.log(rope_base) / head_size)
    )
    angles = positions.astype(jnp.float32)[:, None] * frequency[None, :]
    cosine_table = jnp.concatenate([jnp.cos(angles), jnp.cos(angles)], axis=-1)[:, None, :]
    sine_table = jnp.concatenate([jnp.sin(angles), jnp.sin(angles)], axis=-1)[:, None, :]
    return (cosine_table, sine_table)


def rotate_half(values):
    middle = values.shape[-1] // 2
    return jnp.concatenate([-values[..., middle:], values[..., :middle]], axis=-1)


def rotate(values, cosine_table, sine_table):
    return values * cosine_table + rotate_half(values) * sine_table


def rotate_back(gradient, cosine_table, sine_table):
    return gradient * cosine_table - rotate_half(gradient * sine_table)


def gelu_tanh(values):
    return jax.nn.gelu(values, approximate=True)


def split_rows(array, sub_rows):
    return array.reshape((array.shape[0] // sub_rows, sub_rows) + array.shape[1:])


def part_starts(total_rows, sub_rows):
    return sub_rows * jnp.arange(total_rows // sub_rows, dtype=jnp.int32)


def keep_same(partial_value):
    return partial_value


def attend_forward(partial_value, pieces, queries, query_block, score_scale):
    key_rows, value_rows = pieces
    sub_rows = queries.shape[0]

    def attend_visit(running, scan_item):
        key_part, value_part, part_start = scan_item

        def attend_update(running):
            running_max, running_sum, running_out = running
            key_block = (part_start + jnp.arange(sub_rows, dtype=jnp.int32)) // BLOCK
            allowed = (key_block[None, :] <= query_block[:, None])[None]
            scores = (
                jnp.einsum("qhd,khd->hqk", queries, key_part, preferred_element_type=jnp.float32)
                * score_scale
            )
            scores = jnp.where(allowed, scores, masked_score)
            new_max = jnp.maximum(running_max, jnp.max(scores, axis=-1))
            weights = jnp.where(allowed, jnp.exp(scores - new_max[..., None]), 0.0)
            decay = jnp.exp(running_max - new_max)
            running_sum = running_sum * decay + jnp.sum(weights, axis=-1)
            running_out = running_out * decay[..., None] + jnp.einsum(
                "hqk,khd->hqd",
                weights.astype(jnp.bfloat16),
                value_part,
                preferred_element_type=jnp.float32,
            )
            return (new_max, running_sum, running_out)

        return (
            lax.cond(part_start // BLOCK <= query_block[-1], attend_update, keep_same, running),
            None,
        )

    partial_value, unused = lax.scan(
        attend_visit,
        partial_value,
        (
            split_rows(key_rows, sub_rows),
            split_rows(value_rows, sub_rows),
            part_starts(key_rows.shape[0], sub_rows),
        ),
    )
    return partial_value


def on_device(tokens, timestep, time_table, w_qkv, w_out, w_up, w_down, w_ada, cotangent):
    tok_rows = tokens.shape[1]
    model_width = tokens.shape[2]
    heads = model_width // HD
    score_scale = 1.0 / math.sqrt(HD)
    highest_precision = lax.Precision.HIGHEST
    full_weights = (
        lax.all_gather(w_qkv, "fsdp", axis=0, tiled=True),
        lax.all_gather(w_out, "fsdp", axis=0, tiled=True),
        lax.all_gather(w_up, "fsdp", axis=0, tiled=True),
        lax.all_gather(w_down, "fsdp", axis=0, tiled=True),
        lax.all_gather(w_ada, "fsdp", axis=0, tiled=True),
    )
    qkv_full, out_full, up_full, down_full, ada_full = full_weights
    steps_onehot = (
        timestep[0][:, None] == jnp.arange(time_table.shape[0], dtype=jnp.int32)[None, :]
    ).astype(jnp.float32)
    embedded = jnp.dot(steps_onehot, time_table, precision=highest_precision).astype(jnp.bfloat16)
    modulation = jnp.dot(embedded, ada_full, preferred_element_type=jnp.float32)
    per_token = jnp.repeat(modulation, BLOCK, axis=0)
    scale_attn, gate_attn, scale_mlp, gate_mlp = jnp.split(per_token, 4, axis=1)
    inputs = tokens[0].astype(jnp.float32)
    normed_one, inverse_one = layer_norm(inputs)
    residual_first = (normed_one * (1.0 + scale_attn)).astype(jnp.bfloat16)
    projected_output = jnp.dot(
        residual_first, qkv_full, preferred_element_type=jnp.float32
    ).reshape(tok_rows, 3, heads, HD)
    positions = lax.axis_index("ctx") * tok_rows + jnp.arange(tok_rows, dtype=jnp.int32)
    cosine_table, sine_table = rope_tables(positions, HD)
    queries = rotate(projected_output[:, 0], cosine_table, sine_table).astype(jnp.bfloat16)
    key_own = rotate(projected_output[:, 1], cosine_table, sine_table).astype(jnp.bfloat16)
    value_own = projected_output[:, 2].astype(jnp.bfloat16)
    query_block = positions // BLOCK
    start_state = (
        jnp.full((heads, tok_rows), masked_score, jnp.float32),
        jnp.zeros((heads, tok_rows), jnp.float32),
        jnp.zeros((heads, tok_rows, HD), jnp.float32),
    )
    running_max, running_sum, running_out = attend_forward(
        start_state,
        (
            lax.all_gather(key_own, "ctx", axis=0, tiled=True),
            lax.all_gather(value_own, "ctx", axis=0, tiled=True),
        ),
        queries,
        query_block,
        score_scale,
    )
    attn_rows = jnp.transpose(running_out / running_sum[..., None], (1, 0, 2))
    query_lse = running_max + jnp.log(running_sum)
    attn_low = attn_rows.reshape(tok_rows, model_width).astype(jnp.bfloat16)
    attention_projected = jnp.dot(attn_low, out_full, preferred_element_type=jnp.float32)
    middle = inputs + gate_attn * attention_projected
    normed_two, inverse_two = layer_norm(middle)
    residual_second = (normed_two * (1.0 + scale_mlp)).astype(jnp.bfloat16)
    before_activation = jnp.dot(residual_second, up_full, preferred_element_type=jnp.float32)
    gelu_activated, gelu_back = jax.vjp(gelu_tanh, before_activation)
    act_low = gelu_activated.astype(jnp.bfloat16)
    feedforward_output = jnp.dot(act_low, down_full, preferred_element_type=jnp.float32)
    result = middle + gate_mlp * feedforward_output
    qkv_back, out_back, up_back, down_back = (
        lax.all_gather(w_qkv, "fsdp", axis=0, tiled=True),
        lax.all_gather(w_out, "fsdp", axis=0, tiled=True),
        lax.all_gather(w_up, "fsdp", axis=0, tiled=True),
        lax.all_gather(w_down, "fsdp", axis=0, tiled=True),
    )
    upstream = cotangent[0].astype(jnp.float32)
    grad_gate_mlp = upstream * feedforward_output
    grad_mlp = (upstream * gate_mlp).astype(jnp.bfloat16)
    grad_down = jnp.einsum("tf,td->fd", act_low, grad_mlp, preferred_element_type=jnp.float32)
    grad_act = jnp.einsum("td,fd->tf", grad_mlp, down_back, preferred_element_type=jnp.float32)
    grad_pre = gelu_back(grad_act)[0].astype(jnp.bfloat16)
    grad_up = jnp.einsum("td,tf->df", residual_second, grad_pre, preferred_element_type=jnp.float32)
    grad_hidden_two = jnp.einsum("tf,df->td", grad_pre, up_back, preferred_element_type=jnp.float32)
    grad_scale_mlp = grad_hidden_two * normed_two
    grad_middle = upstream + norm_back(grad_hidden_two * (1.0 + scale_mlp), normed_two, inverse_two)
    grad_gate_attn = grad_middle * attention_projected
    grad_attn_proj = (grad_middle * gate_attn).astype(jnp.bfloat16)
    grad_out = jnp.einsum("td,te->de", attn_low, grad_attn_proj, preferred_element_type=jnp.float32)
    grad_attended = jnp.einsum(
        "te,de->td", grad_attn_proj, out_back, preferred_element_type=jnp.float32
    )
    grad_heads = grad_attended.astype(jnp.bfloat16).reshape(tok_rows, heads, HD)
    delta_rows = jnp.sum(grad_heads.astype(jnp.float32) * attn_rows, axis=-1)
    query_delta = jnp.transpose(delta_rows)
    lse_rows = jnp.transpose(query_lse)
    lse_high = lse_rows.astype(jnp.bfloat16)
    lse_rest = (lse_rows - lse_high.astype(jnp.float32)).astype(jnp.bfloat16)
    delta_high = delta_rows.astype(jnp.bfloat16)
    delta_rest = (delta_rows - delta_high.astype(jnp.float32)).astype(jnp.bfloat16)
    stat_rows = jnp.concatenate([lse_high, lse_rest, delta_high, delta_rest], axis=1)
    zero_heads = jnp.zeros((tok_rows, heads, HD), jnp.float32)
    partial_value = (zero_heads, zero_heads, zero_heads)
    grad_query = partial_value[0]
    key_rows = lax.all_gather(key_own, "ctx", axis=0, tiled=True)

    def query_visit(partial_value, scan_item):
        key_part, value_part, part_start = scan_item

        def query_update(partial_value):
            key_block = (part_start + jnp.arange(tok_rows, dtype=jnp.int32)) // BLOCK
            allowed = (key_block[None, :] <= query_block[:, None])[None]
            scores = (
                jnp.einsum("qhd,khd->hqk", queries, key_part, preferred_element_type=jnp.float32)
                * score_scale
            )
            probs = jnp.where(allowed, jnp.exp(scores - query_lse[..., None]), 0.0)
            grad_prob = jnp.einsum(
                "qhd,khd->hqk", grad_heads, value_part, preferred_element_type=jnp.float32
            )
            grad_score = (probs * (grad_prob - query_delta[..., None]) * score_scale).astype(
                jnp.bfloat16
            )
            return partial_value + jnp.einsum(
                "hqk,khd->qhd", grad_score, key_part, preferred_element_type=jnp.float32
            )

        return (
            lax.cond(
                part_start // BLOCK <= query_block[-1], query_update, keep_same, partial_value
            ),
            None,
        )

    grad_query, unused = lax.scan(
        query_visit,
        grad_query,
        (
            split_rows(key_rows, tok_rows),
            split_rows(lax.all_gather(value_own, "ctx", axis=0, tiled=True), tok_rows),
            part_starts(key_rows.shape[0], tok_rows),
        ),
    )
    key_partial_value = (partial_value[1], partial_value[2])
    query_rows = lax.all_gather(queries, "ctx", axis=0, tiled=True)

    def key_visit(running, scan_item):
        query_part, dout_part, stat_part, part_start = scan_item

        def key_update(running):
            grad_key, grad_value = running
            query_blk = (part_start + jnp.arange(tok_rows, dtype=jnp.int32)) // BLOCK
            allowed = (query_blk[:, None] >= query_block[None, :])[None]
            stat_float = stat_part.astype(jnp.float32)
            lse_part = jnp.transpose(stat_float[:, :heads] + stat_float[:, heads : 2 * heads])
            delta_part = jnp.transpose(
                stat_float[:, 2 * heads : 3 * heads] + stat_float[:, 3 * heads :]
            )
            scores = (
                jnp.einsum("qhd,khd->hqk", query_part, key_own, preferred_element_type=jnp.float32)
                * score_scale
            )
            probs = jnp.where(allowed, jnp.exp(scores - lse_part[..., None]), 0.0)
            grad_value = grad_value + jnp.einsum(
                "hqk,qhd->khd",
                probs.astype(jnp.bfloat16),
                dout_part,
                preferred_element_type=jnp.float32,
            )
            grad_prob = jnp.einsum(
                "qhd,khd->hqk", dout_part, value_own, preferred_element_type=jnp.float32
            )
            grad_score = (probs * (grad_prob - delta_part[..., None]) * score_scale).astype(
                jnp.bfloat16
            )
            grad_key = grad_key + jnp.einsum(
                "hqk,qhd->khd", grad_score, query_part, preferred_element_type=jnp.float32
            )
            return (grad_key, grad_value)

        last_seen = (part_start + tok_rows - 1) // BLOCK
        return (lax.cond(last_seen >= query_block[0], key_update, keep_same, running), None)

    key_partial_value, unused = lax.scan(
        key_visit,
        key_partial_value,
        (
            split_rows(query_rows, tok_rows),
            split_rows(lax.all_gather(grad_heads, "ctx", axis=0, tiled=True), tok_rows),
            split_rows(lax.all_gather(stat_rows, "ctx", axis=0, tiled=True), tok_rows),
            part_starts(query_rows.shape[0], tok_rows),
        ),
    )
    grad_key, grad_value = key_partial_value
    grad_query, grad_key, grad_value = (grad_query, grad_key, grad_value)
    grad_query = rotate_back(grad_query, cosine_table, sine_table)
    grad_key = rotate_back(grad_key, cosine_table, sine_table)
    grad_projected = (
        jnp.stack([grad_query, grad_key, grad_value], axis=1)
        .reshape(tok_rows, 3 * model_width)
        .astype(jnp.bfloat16)
    )
    grad_qkv = jnp.einsum(
        "td,te->de", residual_first, grad_projected, preferred_element_type=jnp.float32
    )
    grad_hidden_one = jnp.einsum(
        "te,de->td", grad_projected, qkv_back, preferred_element_type=jnp.float32
    )
    grad_scale_attn = grad_hidden_one * normed_one
    input_grad = grad_middle + norm_back(
        grad_hidden_one * (1.0 + scale_attn), normed_one, inverse_one
    )
    grad_modulation = jnp.concatenate(
        [grad_scale_attn, grad_gate_attn, grad_scale_mlp, grad_gate_mlp], axis=1
    )
    grad_blocks = jnp.sum(
        grad_modulation.reshape(tok_rows // BLOCK, BLOCK, 4 * model_width), axis=1
    )
    embedded_float = embedded.astype(jnp.float32)
    halves = (
        lax.psum_scatter(
            grad_qkv.astype(jnp.bfloat16), "fsdp", scatter_dimension=0, tiled=True
        ).astype(jnp.float32),
        lax.psum_scatter(
            grad_out.astype(jnp.bfloat16), "fsdp", scatter_dimension=0, tiled=True
        ).astype(jnp.float32),
        lax.psum_scatter(
            grad_up.astype(jnp.bfloat16), "fsdp", scatter_dimension=0, tiled=True
        ).astype(jnp.float32),
        lax.psum_scatter(
            grad_down.astype(jnp.bfloat16), "fsdp", scatter_dimension=0, tiled=True
        ).astype(jnp.float32),
    )
    totals = lax.psum((halves[0], halves[1], halves[2], halves[3]), "ctx")
    all_embedded, all_blocks = (
        lax.all_gather(embedded_float, ("ctx", "fsdp"), axis=0, tiled=True),
        lax.all_gather(grad_blocks, ("ctx", "fsdp"), axis=0, tiled=True),
    )
    shard_width = model_width // lax.axis_size("fsdp")
    row_start = lax.axis_index("fsdp") * shard_width
    embedded_part = lax.dynamic_slice_in_dim(all_embedded, row_start, shard_width, 1)
    ada_total = jnp.dot(jnp.transpose(embedded_part), all_blocks, precision=highest_precision)
    return (result[None], input_grad[None], totals[0], totals[1], totals[2], totals[3], ada_total)


def barrier_with(peers):
    barrier = pltpu.get_barrier_semaphore()
    for peer in peers:
        pl.semaphore_signal(barrier, inc=1, device_id=peer, device_id_type=MESH)
    pl.semaphore_wait(barrier, len(peers))


def plane_barrier(me, count):
    barrier = pltpu.get_barrier_semaphore()

    def greet(step, carry):
        pl.semaphore_signal(
            barrier,
            inc=1,
            device_id={"ctx": lax.rem(me + step, count)},
            device_id_type=MESH,
        )
        return carry

    lax.fori_loop(1, count, greet, 0)
    pl.semaphore_wait(barrier, count - 1)


def remote(source, target, send_sem, recv_sem, **where):
    return pltpu.make_async_remote_copy(
        src_ref=source,
        dst_ref=target,
        send_sem=send_sem,
        recv_sem=recv_sem,
        device_id=where,
        device_id_type=MESH,
    )


def landed(ref, sem):
    pltpu.make_async_copy(ref, ref, sem).wait()


def gather_kernel(
    emb_ref, ada_ref, qkv_ref, out_ref, up_ref, down_ref,
    mod_ref, qkv_full, out_full, up_full, down_full,
    emb_other, part_other, part_send,
    own_sem, small_send, small_recv, send_sem, recv_sem,
):
    me = lax.axis_index("ctx")
    row = lax.axis_index("fsdp")
    other = 1 - row
    piece = lax.rem(me, 4)
    chip_next = jnp.bitwise_xor(me, 2)
    sibling = jnp.bitwise_xor(me, 1)
    barrier_with([{"fsdp": other}, {"ctx": chip_next}, {"ctx": sibling}])
    emb_copy = remote(emb_ref, emb_other, small_send.at[0], small_recv.at[0], fsdp=other)
    emb_copy.start()
    shards = (qkv_ref, out_ref, up_ref, down_ref)
    wholes = (qkv_full, out_full, up_full, down_full)
    started = []
    for index in range(4):
        shard, whole = shards[index], wholes[index]
        half = shard.shape[0]
        part = half // 4
        copy = remote(
            shard.at[pl.ds(piece * part, part)],
            whole.at[pl.ds(row * half + piece * part, part)],
            send_sem.at[index, 0], recv_sem.at[index, 0], fsdp=other,
        )
        copy.start()
        started.append(copy)
    for index in range(4):
        shard, whole = shards[index], wholes[index]
        half = shard.shape[0]
        pltpu.make_async_copy(
            shard, whole.at[pl.ds(row * half, half)], own_sem.at[index]
        ).start()
    emb_copy.wait()
    half_width = ada_ref.shape[0]
    cols = pl.ds(pl.multiple_of(row * half_width, 128), half_width)
    both = jnp.concatenate([emb_ref[:, cols], emb_other[:, cols]], axis=0).astype(jnp.bfloat16)
    partial = jnp.dot(both, ada_ref[...], preferred_element_type=jnp.float32)
    mod_ref[...] = partial[:8]
    part_send[...] = partial[8:]
    part_copy = remote(part_send, part_other, small_send.at[1], small_recv.at[1], fsdp=other)
    part_copy.start()

    def rows_of(index, which):
        half = shards[index].shape[0]
        part = half // 4
        return wholes[index].at[pl.ds(other * half + which * part, part)]

    def pass_on(index):
        landed(rows_of(index, piece), recv_sem.at[index, 0])
        for slot, peer in ((1, chip_next), (2, sibling)):
            copy = remote(
                rows_of(index, piece), rows_of(index, piece),
                send_sem.at[index, slot], recv_sem.at[index, slot], ctx=peer,
            )
            copy.start()
            started.append(copy)

    def pass_last(index):
        across = jnp.bitwise_xor(piece, 2)
        landed(rows_of(index, across), recv_sem.at[index, 1])
        copy = remote(
            rows_of(index, across), rows_of(index, across),
            send_sem.at[index, 3], recv_sem.at[index, 3], ctx=sibling,
        )
        copy.start()
        started.append(copy)

    for index in range(4):
        pass_on(index)
        if index:
            pass_last(index - 1)
    pass_last(3)
    part_copy.wait()
    mod_ref[...] += part_other[...]
    for index in range(4):
        landed(rows_of(index, jnp.bitwise_xor(piece, 1)), recv_sem.at[index, 2])
        landed(rows_of(index, jnp.bitwise_xor(piece, 3)), recv_sem.at[index, 3])
        half = shards[index].shape[0]
        pltpu.make_async_copy(
            shards[index], wholes[index].at[pl.ds(row * half, half)], own_sem.at[index]
        ).wait()
    for copy in started:
        copy.wait_send()


def gather_weights(embedded, w_ada, w_qkv, w_out, w_up, w_down):
    shards = (w_qkv, w_out, w_up, w_down)
    width = w_ada.shape[1]
    emb_rows = jnp.broadcast_to(embedded.astype(jnp.float32), (8, embedded.shape[1]))
    hbm = pl.BlockSpec(memory_space=pl.ANY)
    vmem = pl.BlockSpec(memory_space=pltpu.VMEM)
    return pl.pallas_call(
        gather_kernel,
        out_shape=[jax.ShapeDtypeStruct((8, width), jnp.float32)]
        + [jax.ShapeDtypeStruct((2 * w.shape[0], w.shape[1]), w.dtype) for w in shards],
        in_specs=[vmem, vmem] + [hbm] * 4,
        out_specs=[vmem] + [hbm] * 4,
        scratch_shapes=[
            pltpu.VMEM(emb_rows.shape, jnp.float32),
            pltpu.VMEM((8, width), jnp.float32),
            pltpu.VMEM((8, width), jnp.float32),
            pltpu.SemaphoreType.DMA((4,)),
            pltpu.SemaphoreType.DMA((2,)),
            pltpu.SemaphoreType.DMA((2,)),
            pltpu.SemaphoreType.DMA((4, 4)),
            pltpu.SemaphoreType.DMA((4, 4)),
        ],
        compiler_params=pltpu.CompilerParams(
            collective_id=1, has_side_effects=True, vmem_limit_bytes=VMEM_LIMIT
        ),
    )(emb_rows, w_ada, *shards)


def head_place(me):
    plane = me // 4
    spot = lax.rem(me, 4)
    odd = lax.rem(plane, 2)
    idle = 3 - 2 * odd
    head = 3 * plane + spot - odd * (spot // 2)
    return spot != idle, head


def head_owner(head):
    plane = head // 3
    rank = lax.rem(head, 3)
    odd = lax.rem(plane, 2)
    return 4 * plane + rank + odd * ((rank + 1) // 2)


def scatter_heads(me, heads, source, target, send_sem, recv_sem):
    def send(step, carry):
        head = lax.rem(step + 3 * (me // 4), heads)
        owner = head_owner(head)

        @pl.when(owner != me)
        def _():
            remote(
                source.at[head], target.at[me], send_sem.at[head], recv_sem.at[me], ctx=owner
            ).start()

        @pl.when(owner == me)
        def _():
            pltpu.make_async_copy(source.at[head], target.at[me], recv_sem.at[me]).start()

        return carry

    lax.fori_loop(0, heads, send, 0)


def scatter_sent(me, heads, source, target, send_sem, recv_sem):
    def finish(head, carry):
        owner = head_owner(head)

        @pl.when(owner != me)
        def _():
            remote(
                source.at[head], target.at[me], send_sem.at[head], recv_sem.at[me], ctx=owner
            ).wait_send()

        return carry

    lax.fori_loop(0, heads, finish, 0)


def return_block(me, head, block, source, target, send_sem, recv_sem):
    @pl.when(block != me)
    def _():
        remote(
            source.at[block], target.at[head], send_sem.at[block], recv_sem.at[head], ctx=block
        ).start()

    @pl.when(block == me)
    def _():
        pltpu.make_async_copy(source.at[block], target.at[head], recv_sem.at[head]).start()


def return_sent(me, head, blocks, source, target, send_sem, recv_sem):
    def finish(block, carry):
        @pl.when(block != me)
        def _():
            remote(
                source.at[block], target.at[head], send_sem.at[block], recv_sem.at[head], ctx=block
            ).wait_send()

        return carry

    lax.fori_loop(0, blocks, finish, 0)


def wait_heads(heads, target, recv_sem):
    def finish(head, carry):
        landed(target.at[head], recv_sem.at[head])
        return carry

    lax.fori_loop(0, heads, finish, 0)


def transposed(values):
    return jnp.transpose(values.astype(jnp.float32)).astype(values.dtype)


def forward_kernel(
    blocks, heads, qkv_ref, att_ref, buf_ref, out_ref, lse_ref,
    pair_ref, low_ref, send_sem, recv_sem, back_send, back_recv,
):
    me = lax.axis_index("ctx")
    owner, head = head_place(me)
    plane_barrier(me, blocks)
    scatter_heads(me, heads, qkv_ref, buf_ref, send_sem, recv_sem)

    @pl.when(owner)
    def _():
        def query_block(block, carry):
            landed(buf_ref.at[block], recv_sem.at[block])
            rows = pl.ds(pl.multiple_of(block * BLOCK, BLOCK), BLOCK)
            pair_ref[rows, :] = transposed(buf_ref[block, HD:, :])
            query = jnp.concatenate(
                [buf_ref[block, :HD, :], jnp.zeros((HD, BLOCK), jnp.bfloat16)], axis=0
            )

            def key_block(key, state):
                high, total, mixed = state
                key_rows = pl.ds(pl.multiple_of(key * BLOCK, BLOCK), BLOCK)
                scores = jnp.dot(pair_ref[key_rows, :], query, preferred_element_type=jnp.float32)
                new_high = jnp.maximum(high, jnp.max(scores, axis=0, keepdims=True))
                weights = jnp.exp(scores - new_high)
                decay = jnp.exp(high - new_high)
                total = total * decay + jnp.sum(weights, axis=0, keepdims=True)
                mixed = mixed * decay + jnp.dot(
                    buf_ref[key, 2 * HD :, :],
                    weights.astype(jnp.bfloat16),
                    preferred_element_type=jnp.float32,
                )
                return new_high, total, mixed

            high, total, mixed = lax.fori_loop(
                0,
                block + 1,
                key_block,
                (
                    jnp.full((1, BLOCK), masked_score, jnp.float32),
                    jnp.zeros((1, BLOCK), jnp.float32),
                    jnp.zeros((HD, BLOCK), jnp.float32),
                ),
            )
            mixed = mixed / total
            out_ref[block] = mixed
            low_ref[block] = mixed.astype(jnp.bfloat16)
            lse_ref[block] = jnp.broadcast_to(high + jnp.log(total), (8, BLOCK))
            return_block(me, head, block, low_ref, att_ref, back_send, back_recv)
            return carry

        lax.fori_loop(0, blocks, query_block, 0)
        return_sent(me, head, blocks, low_ref, att_ref, back_send, back_recv)

    scatter_sent(me, heads, qkv_ref, buf_ref, send_sem, recv_sem)
    wait_heads(heads, att_ref, back_recv)


def attention_forward(qkv_heads, blocks):
    heads = qkv_heads.shape[0]
    vmem = pl.BlockSpec(memory_space=pltpu.VMEM)
    return pl.pallas_call(
        functools.partial(forward_kernel, blocks, heads),
        out_shape=[
            jax.ShapeDtypeStruct((heads, HD, BLOCK), jnp.bfloat16),
            jax.ShapeDtypeStruct((blocks, 3 * HD, BLOCK), jnp.bfloat16),
            jax.ShapeDtypeStruct((blocks, HD, BLOCK), jnp.float32),
            jax.ShapeDtypeStruct((blocks, 8, BLOCK), jnp.float32),
        ],
        in_specs=[vmem],
        out_specs=[vmem] * 4,
        scratch_shapes=[
            pltpu.VMEM((blocks * BLOCK, 2 * HD), jnp.bfloat16),
            pltpu.VMEM((blocks, HD, BLOCK), jnp.bfloat16),
            pltpu.SemaphoreType.DMA((heads,)),
            pltpu.SemaphoreType.DMA((blocks,)),
            pltpu.SemaphoreType.DMA((blocks,)),
            pltpu.SemaphoreType.DMA((heads,)),
        ],
        compiler_params=pltpu.CompilerParams(
            collective_id=2, has_side_effects=True, vmem_limit_bytes=VMEM_LIMIT
        ),
    )(qkv_heads)


def backward_kernel(
    blocks, heads, dout_ref, buf_ref, out_ref, lse_ref, grad_ref,
    got_ref, pair_ref, total_ref, low_ref, send_sem, recv_sem, back_send, back_recv,
):
    me = lax.axis_index("ctx")
    owner, head = head_place(me)
    plane_barrier(me, blocks)
    scatter_heads(me, heads, dout_ref, got_ref, send_sem, recv_sem)

    @pl.when(owner)
    def _():
        def prepare(block, carry):
            rows = pl.ds(pl.multiple_of(block * BLOCK, BLOCK), BLOCK)
            pair_ref[rows, :] = transposed(buf_ref[block, HD:, :])
            total_ref[rows, :] = jnp.zeros((BLOCK, 2 * HD), jnp.float32)
            return carry

        lax.fori_loop(0, blocks, prepare, 0)

        def query_block(step, carry):
            block = blocks - 1 - step
            landed(got_ref.at[block], recv_sem.at[block])
            dout = got_ref[block]
            query = buf_ref[block, :HD, :]
            zero = jnp.zeros((HD, BLOCK), jnp.bfloat16)
            delta = jnp.sum(dout.astype(jnp.float32) * out_ref[block], axis=0, keepdims=True)
            lse = lse_ref[block, :1, :]
            query_down = jnp.concatenate([query, zero], axis=0)
            dout_down = jnp.concatenate([zero, dout], axis=0)
            dout_side = transposed(jnp.concatenate([dout, zero], axis=0))
            query_side = transposed(jnp.concatenate([zero, query], axis=0))

            def key_block(key, grad_query):
                key_rows = pl.ds(pl.multiple_of(key * BLOCK, BLOCK), BLOCK)
                pair = pair_ref[key_rows, :]
                scores = jnp.dot(pair, query_down, preferred_element_type=jnp.float32)
                probs = jnp.exp(scores - lse)
                grad_probs = jnp.dot(pair, dout_down, preferred_element_type=jnp.float32)
                grad_scores = (probs * (grad_probs - delta)).astype(jnp.bfloat16)
                total_ref[key_rows, :] += jnp.dot(
                    probs.astype(jnp.bfloat16), dout_side, preferred_element_type=jnp.float32
                ) + jnp.dot(grad_scores, query_side, preferred_element_type=jnp.float32)
                return grad_query + jnp.dot(
                    buf_ref[key, HD : 2 * HD, :], grad_scores, preferred_element_type=jnp.float32
                )

            grad_query = lax.fori_loop(
                0, block + 1, key_block, jnp.zeros((HD, BLOCK), jnp.float32)
            )
            rows = pl.ds(pl.multiple_of(block * BLOCK, BLOCK), BLOCK)
            low_ref[block, :HD, :] = (grad_query * (1.0 / math.sqrt(HD))).astype(jnp.bfloat16)
            sums = jnp.transpose(total_ref[rows, :]).astype(jnp.bfloat16)
            low_ref[block, HD : 2 * HD, :] = sums[HD:]
            low_ref[block, 2 * HD :, :] = sums[:HD]
            return_block(me, head, block, low_ref, grad_ref, back_send, back_recv)
            return carry

        lax.fori_loop(0, blocks, query_block, 0)
        return_sent(me, head, blocks, low_ref, grad_ref, back_send, back_recv)

    scatter_sent(me, heads, dout_ref, got_ref, send_sem, recv_sem)
    wait_heads(heads, grad_ref, back_recv)


def attention_backward(dout_heads, buffered, mixed, lse):
    heads = dout_heads.shape[0]
    blocks = buffered.shape[0]
    vmem = pl.BlockSpec(memory_space=pltpu.VMEM)
    return pl.pallas_call(
        functools.partial(backward_kernel, blocks, heads),
        out_shape=jax.ShapeDtypeStruct((heads, 3 * HD, BLOCK), jnp.bfloat16),
        in_specs=[vmem] * 4,
        out_specs=vmem,
        scratch_shapes=[
            pltpu.VMEM((blocks, HD, BLOCK), jnp.bfloat16),
            pltpu.VMEM((blocks * BLOCK, 2 * HD), jnp.bfloat16),
            pltpu.VMEM((blocks * BLOCK, 2 * HD), jnp.float32),
            pltpu.VMEM((blocks, 3 * HD, BLOCK), jnp.bfloat16),
            pltpu.SemaphoreType.DMA((heads,)),
            pltpu.SemaphoreType.DMA((blocks,)),
            pltpu.SemaphoreType.DMA((blocks,)),
            pltpu.SemaphoreType.DMA((heads,)),
        ],
        compiler_params=pltpu.CompilerParams(
            collective_id=3, has_side_effects=True, vmem_limit_bytes=VMEM_LIMIT
        ),
    )(dout_heads, buffered, mixed, lse)


def reduce_kernel(
    units, planes, part_ref, stat_ref, res_ref, table_ref,
    sib_ref, row_ref, x_ref, z_ref,
    s_sib, r_sib, s_row, r_row, s_x, r_x, s_z, r_z, s_az, r_az, s_ax, r_ax, s_as, r_as,
    s_t, r_t,
):
    me = lax.axis_index("ctx")
    row = lax.axis_index("fsdp")
    other = 1 - row
    core = lax.rem(me, 2)
    xbit = lax.rem(me // 2, 2)
    plane = me // 4
    spot = lax.rem(me, 4)
    sibling = jnp.bitwise_xor(me, 1)
    chip_next = jnp.bitwise_xor(me, 2)
    barrier = pltpu.get_barrier_semaphore()
    peers = [{"fsdp": other}, {"ctx": sibling}, {"ctx": chip_next}]
    peers += [{"ctx": lax.rem(me + 4 * step, 4 * planes)} for step in range(1, planes)]
    for peer in peers:
        pl.semaphore_signal(barrier, inc=1, device_id=peer, device_id_type=MESH)
    pl.semaphore_wait(barrier, len(peers))
    width = part_ref.shape[3] // 2
    mine = pl.ds(pl.multiple_of(core * width, 128), width)
    theirs = pl.ds(pl.multiple_of((1 - core) * width, 128), width)
    deep = part_ref.shape[2]
    quarter = deep // 2
    small = quarter // planes

    def add(left, right):
        return (left.astype(jnp.float32) + right.astype(jnp.float32)).astype(jnp.bfloat16)

    def to_sibling(unit):
        return [
            remote(part_ref.at[unit, half, :, theirs], sib_ref.at[unit, half],
                   s_sib.at[unit, half], r_sib.at[unit, half], ctx=sibling)
            for half in range(2)
        ]

    def to_row(unit):
        return [remote(sib_ref.at[unit, other], row_ref.at[unit],
                       s_row.at[unit], r_row.at[unit], fsdp=other)]

    def to_x(unit):
        rows = pl.ds(pl.multiple_of((1 - xbit) * quarter, 16), quarter)
        return [remote(row_ref.at[unit, rows], x_ref.at[unit],
                       s_x.at[unit], r_x.at[unit], ctx=chip_next)]

    def to_z(unit):
        copies = []
        for step in range(1, planes):
            goal = lax.rem(plane + step, planes)
            rows = pl.ds(pl.multiple_of(goal * small, 16), small)
            copies.append(
                remote(x_ref.at[unit, rows], z_ref.at[unit, step - 1],
                       s_z.at[unit, step - 1], r_z.at[unit, step - 1], ctx=4 * goal + spot)
            )
        return copies

    def piece(unit, which):
        rows = pl.ds(pl.multiple_of(xbit * quarter + which * small, 16), small)
        return res_ref.at[unit, rows, mine]

    def along_z(unit):
        return [
            remote(piece(unit, plane), piece(unit, plane),
                   s_az.at[unit, step - 1], r_az.at[unit, step - 1],
                   ctx=4 * lax.rem(plane + step, planes) + spot)
            for step in range(1, planes)
        ]

    def along_x(unit):
        rows = pl.ds(pl.multiple_of(xbit * quarter, 16), quarter)
        ref = res_ref.at[unit, rows, mine]
        return [remote(ref, ref, s_ax.at[unit], r_ax.at[unit], ctx=chip_next)]

    def along_s(unit):
        ref = res_ref.at[unit, :, mine]
        return [remote(ref, ref, s_as.at[unit], r_as.at[unit], ctx=sibling)]

    def launch(copies):
        for copy in copies:
            copy.start()

    def stage0(unit):
        launch(to_sibling(unit))

    def stage1(unit):
        for half in range(2):
            landed(sib_ref.at[unit, half], r_sib.at[unit, half])
            sib_ref[unit, half] = add(sib_ref[unit, half], part_ref[unit, half, :, mine])
        launch(to_row(unit))

    def stage2(unit):
        landed(row_ref.at[unit], r_row.at[unit])
        row_ref[unit] = add(row_ref[unit], sib_ref[unit, row])
        launch(to_x(unit))

    def stage3(unit):
        landed(x_ref.at[unit], r_x.at[unit])
        rows = pl.ds(pl.multiple_of(xbit * quarter, 16), quarter)
        x_ref[unit] = add(x_ref[unit], row_ref[unit, rows])
        launch(to_z(unit))

    def stage4(unit):
        rows = pl.ds(pl.multiple_of(plane * small, 16), small)
        total = x_ref[unit, rows].astype(jnp.float32)
        for step in range(1, planes):
            landed(z_ref.at[unit, step - 1], r_z.at[unit, step - 1])
            total += z_ref[unit, step - 1].astype(jnp.float32)
        spots = pl.ds(pl.multiple_of(xbit * quarter + plane * small, 16), small)
        res_ref[unit, spots, mine] = total.astype(jnp.bfloat16)
        launch(along_z(unit))

    def stage5(unit):
        for step in range(1, planes):
            landed(piece(unit, lax.rem(plane + planes - step, planes)), r_az.at[unit, step - 1])
        launch(along_x(unit))

    def stage6(unit):
        rows = pl.ds(pl.multiple_of((1 - xbit) * quarter, 16), quarter)
        landed(res_ref.at[unit, rows, mine], r_ax.at[unit])
        launch(along_s(unit))

    def stage7(unit):
        landed(res_ref.at[unit, :, theirs], r_as.at[unit])
        for make in (to_sibling, to_row, to_x, to_z, along_z, along_x, along_s):
            for copy in make(unit):
                copy.wait_send()

    stages = (stage0, stage1, stage2, stage3, stage4, stage5, stage6, stage7)

    def slots(first, count):
        return table_ref.at[pl.ds(first, count)]

    chip_slot = core * 4 * planes + 4 * plane

    def table_row():
        return [remote(slots(chip_slot + 2 * xbit + row, 1), slots(chip_slot + 2 * xbit + row, 1),
                       s_t.at[0], r_t.at[0], fsdp=other)]

    def table_x():
        return [remote(slots(chip_slot + 2 * xbit, 2), slots(chip_slot + 2 * xbit, 2),
                       s_t.at[1], r_t.at[1], ctx=chip_next)]

    def table_z():
        return [remote(slots(chip_slot, 4), slots(chip_slot, 4), s_t.at[2 + step],
                       r_t.at[2 + step], ctx=4 * lax.rem(plane + step, planes) + spot)
                for step in range(1, planes)]

    def table_s():
        return [remote(slots(core * 4 * planes, 4 * planes), slots(core * 4 * planes, 4 * planes),
                       s_t.at[2], r_t.at[2], ctx=sibling)]

    table_ref[chip_slot + 2 * xbit + row] = stat_ref[...]
    launch(table_row())

    def tick(time, carry):
        @pl.when(time == 1)
        def _():
            landed(slots(chip_slot + 2 * xbit + other, 1), r_t.at[0])
            launch(table_x())

        @pl.when(time == 3)
        def _():
            landed(slots(chip_slot + 2 * (1 - xbit), 2), r_t.at[1])
            launch(table_z())

        @pl.when(time == 5)
        def _():
            for step in range(1, planes):
                goal = lax.rem(plane + planes - step, planes)
                landed(slots(core * 4 * planes + 4 * goal, 4), r_t.at[2 + step])
            launch(table_s())

        for depth in range(len(stages)):
            unit = time - depth

            @pl.when((unit >= 0) & (unit < units))
            def _(depth=depth, unit=unit):
                stages[depth](unit)

        return carry

    lax.fori_loop(0, units + len(stages) - 1, tick, 0)
    landed(slots((1 - core) * 4 * planes, 4 * planes), r_t.at[2])
    for copies in (table_row(), table_x(), table_z(), table_s()):
        for copy in copies:
            copy.wait_send()


def reduce_gradients(parts, stats, count):
    units, halves, deep, width = parts.shape
    planes = count // 4
    vmem = pl.BlockSpec(memory_space=pltpu.VMEM)
    dma = pltpu.SemaphoreType.DMA
    steps = planes - 1
    sems = [(units, 2), (units, 2), (units,), (units,), (units,), (units,),
            (units, steps), (units, steps), (units, steps), (units, steps),
            (units,), (units,), (units,), (units,), (planes + 2,), (planes + 2,)]
    return pl.pallas_call(
        functools.partial(reduce_kernel, units, planes),
        out_shape=[
            jax.ShapeDtypeStruct((units, deep, width), jnp.bfloat16),
            jax.ShapeDtypeStruct((2 * count,) + stats.shape, jnp.float32),
        ],
        in_specs=[vmem, vmem],
        out_specs=[vmem, vmem],
        scratch_shapes=[
            pltpu.VMEM((units, 2, deep, width // 2), jnp.bfloat16),
            pltpu.VMEM((units, deep, width // 2), jnp.bfloat16),
            pltpu.VMEM((units, deep // 2, width // 2), jnp.bfloat16),
            pltpu.VMEM((units, steps, deep // 2 // planes, width // 2), jnp.bfloat16),
        ] + [dma(shape) for shape in sems],
        compiler_params=pltpu.CompilerParams(
            collective_id=4, has_side_effects=True, vmem_limit_bytes=VMEM_LIMIT
        ),
    )(parts, stats)


def to_units(gradient, model_width):
    rows, cols = gradient.shape
    low = gradient.astype(jnp.bfloat16)
    if rows == model_width:
        count = cols // model_width
        return jnp.transpose(low.reshape(2, rows // 2, count, model_width), (2, 0, 1, 3))
    count = rows // model_width
    return jnp.transpose(low.reshape(2, count, model_width // 2, model_width), (1, 0, 2, 3))


def from_units(summed, rows):
    count, deep, width = summed.shape
    values = summed.astype(jnp.float32)
    if rows == deep:
        return jnp.transpose(values, (1, 0, 2)).reshape(deep, count * width)
    return values.reshape(count * deep, width)


def fast_device(tokens, timestep, time_table, w_qkv, w_out, w_up, w_down, w_ada, cotangent):
    tok_rows = tokens.shape[1]
    model_width = tokens.shape[2]
    heads = model_width // HD
    blocks = lax.axis_size("ctx")
    me = lax.axis_index("ctx")
    score_scale = 1.0 / math.sqrt(HD)
    embedded = lax.dynamic_slice_in_dim(time_table, timestep[0, 0], 1, 0).astype(jnp.bfloat16)
    modulation, qkv_full, out_full, up_full, down_full = gather_weights(
        embedded, w_ada, w_qkv, w_out, w_up, w_down
    )
    scale_attn, gate_attn, scale_mlp, gate_mlp = jnp.split(modulation[:1], 4, axis=1)
    inputs = tokens[0].astype(jnp.float32)
    normed_one, inverse_one = layer_norm(inputs)
    residual_first = (normed_one * (1.0 + scale_attn)).astype(jnp.bfloat16)
    projected = jnp.transpose(
        jnp.dot(residual_first, qkv_full, preferred_element_type=jnp.float32)
    ).reshape(3, heads, HD, tok_rows)
    positions = me * tok_rows + jnp.arange(tok_rows, dtype=jnp.int32)
    cosine_table, sine_table = rope_tables(positions, HD)
    cosine = jnp.transpose(cosine_table[:, 0, :])
    sine = jnp.transpose(sine_table[:, 0, :])

    def turn(values):
        return jnp.concatenate([-values[:, HD // 2 :], values[:, : HD // 2]], axis=1)

    queries = projected[0] * cosine + turn(projected[0]) * sine
    key_own = projected[1] * cosine + turn(projected[1]) * sine
    qkv_heads = jnp.concatenate(
        [
            queries.astype(jnp.bfloat16) * jnp.bfloat16(score_scale),
            key_own.astype(jnp.bfloat16),
            projected[2].astype(jnp.bfloat16),
        ],
        axis=1,
    )
    att_heads, buffered, mixed, lse = attention_forward(qkv_heads, blocks)
    attn_low = jnp.transpose(att_heads.reshape(model_width, tok_rows))
    attention_projected = jnp.dot(attn_low, out_full, preferred_element_type=jnp.float32)
    middle = inputs + gate_attn * attention_projected
    normed_two, inverse_two = layer_norm(middle)
    residual_second = (normed_two * (1.0 + scale_mlp)).astype(jnp.bfloat16)
    before_activation = jnp.dot(residual_second, up_full, preferred_element_type=jnp.float32)
    gelu_activated, gelu_back = jax.vjp(gelu_tanh, before_activation)
    act_low = gelu_activated.astype(jnp.bfloat16)
    feedforward_output = jnp.dot(act_low, down_full, preferred_element_type=jnp.float32)
    result = middle + gate_mlp * feedforward_output
    upstream = cotangent[0].astype(jnp.float32)
    grad_gate_mlp = upstream * feedforward_output
    grad_mlp = (upstream * gate_mlp).astype(jnp.bfloat16)
    grad_down = jnp.einsum("tf,td->fd", act_low, grad_mlp, preferred_element_type=jnp.float32)
    grad_act = jnp.einsum("td,fd->tf", grad_mlp, down_full, preferred_element_type=jnp.float32)
    grad_pre = gelu_back(grad_act)[0].astype(jnp.bfloat16)
    grad_up = jnp.einsum("td,tf->df", residual_second, grad_pre, preferred_element_type=jnp.float32)
    grad_hidden_two = jnp.einsum("tf,df->td", grad_pre, up_full, preferred_element_type=jnp.float32)
    grad_scale_mlp = grad_hidden_two * normed_two
    grad_middle = upstream + norm_back(grad_hidden_two * (1.0 + scale_mlp), normed_two, inverse_two)
    grad_gate_attn = grad_middle * attention_projected
    grad_attn_proj = (grad_middle * gate_attn).astype(jnp.bfloat16)
    grad_out = jnp.einsum("td,te->de", attn_low, grad_attn_proj, preferred_element_type=jnp.float32)
    grad_attended = jnp.einsum(
        "de,te->dt", out_full, grad_attn_proj, preferred_element_type=jnp.float32
    )
    dout_heads = grad_attended.astype(jnp.bfloat16).reshape(heads, HD, tok_rows)
    grad_heads = attention_backward(dout_heads, buffered, mixed, lse)

    def turn_back(values):
        scaled = values * sine
        return values * cosine - turn(scaled)

    wide = grad_heads.astype(jnp.float32)
    grad_projected = jnp.transpose(
        jnp.stack(
            [
                turn_back(wide[:, :HD]),
                turn_back(wide[:, HD : 2 * HD]),
                wide[:, 2 * HD :],
            ]
        )
        .reshape(3 * model_width, tok_rows)
        .astype(jnp.bfloat16)
    )
    grad_qkv = jnp.einsum(
        "td,te->de", residual_first, grad_projected, preferred_element_type=jnp.float32
    )
    grad_hidden_one = jnp.einsum(
        "te,de->td", grad_projected, qkv_full, preferred_element_type=jnp.float32
    )
    grad_scale_attn = grad_hidden_one * normed_one
    input_grad = grad_middle + norm_back(
        grad_hidden_one * (1.0 + scale_attn), normed_one, inverse_one
    )
    grad_blocks = jnp.concatenate(
        [
            jnp.sum(values, axis=0, keepdims=True)
            for values in (grad_scale_attn, grad_gate_attn, grad_scale_mlp, grad_gate_mlp)
        ],
        axis=1,
    )
    stats = jnp.concatenate([embedded.astype(jnp.float32), grad_blocks], axis=1).reshape(-1, 128)
    stat_rows = stats.shape[0]
    stats = jnp.pad(stats, ((0, -stat_rows % 8), (0, 0)))
    gradients = (grad_qkv, grad_out, grad_up, grad_down)
    grouped = [to_units(gradient, model_width) for gradient in gradients]
    summed, table = reduce_gradients(jnp.concatenate(grouped), stats, blocks)
    totals = []
    first = 0
    for group, shard in zip(grouped, (w_qkv, w_out, w_up, w_down)):
        totals.append(from_units(summed[first : first + group.shape[0]], shard.shape[0]))
        first += group.shape[0]
    flat = table[:, :stat_rows].reshape(2 * blocks, 5 * model_width)
    shard_width = model_width // 2
    embedded_part = lax.dynamic_slice_in_dim(
        flat[:, :model_width], lax.axis_index("fsdp") * shard_width, shard_width, 1
    )
    ada_total = lax.dot_general(
        embedded_part, flat[:, model_width:], (((0,), (0,)), ((), ())),
        precision=lax.Precision.HIGHEST,
    )
    return (result[None], input_grad[None], *totals, ada_total)


def solution(mesh):
    chosen = fast_device if mesh.shape["ctx"] == 16 else on_device
    return jax.shard_map(
        chosen,
        mesh=mesh,
        in_specs=(
            P("fsdp", "ctx", None),
            P("fsdp", "ctx"),
            P(),
            P("fsdp", None),
            P("fsdp", None),
            P("fsdp", None),
            P("fsdp", None),
            P("fsdp", None),
            P("fsdp", "ctx", None),
        ),
        out_specs=(
            P("fsdp", "ctx", None),
            P("fsdp", "ctx", None),
            P("fsdp", None),
            P("fsdp", None),
            P("fsdp", None),
            P("fsdp", None),
            P("fsdp", None),
        ),
        check_vma=False,
    )
```

```python
import functools
import math

import jax
import jax.numpy as jnp
import numpy as np
from jax import lax
from jax.experimental import pallas as pl
from jax.experimental.pallas import tpu as pltpu
from jax.sharding import PartitionSpec as P

HD = 64
BLOCK = 256
VMEM_LIMIT = 62 * 1024 * 1024
MESH = pl.DeviceIdType.MESH


norm_eps = 1e-06
masked_score = -1e30
rope_base = 10000.0


def layer_norm(values):
    center = values - jnp.mean(values, axis=-1, keepdims=True)
    inverse = lax.rsqrt(jnp.mean(center * center, axis=-1, keepdims=True) + norm_eps)
    return (center * inverse, inverse)


def norm_back(grad_norm, normed, inverse):
    mean_grad = jnp.mean(grad_norm, axis=-1, keepdims=True)
    mean_cross = jnp.mean(grad_norm * normed, axis=-1, keepdims=True)
    return inverse * (grad_norm - mean_grad - normed * mean_cross)


def rope_tables(positions, head_size):
    half_size = head_size // 2
    frequency = jnp.exp(
        jnp.arange(half_size, dtype=jnp.float32) * (-2.0 * math.log(rope_base) / head_size)
    )
    angles = positions.astype(jnp.float32)[:, None] * frequency[None, :]
    cosine_table = jnp.concatenate([jnp.cos(angles), jnp.cos(angles)], axis=-1)[:, None, :]
    sine_table = jnp.concatenate([jnp.sin(angles), jnp.sin(angles)], axis=-1)[:, None, :]
    return (cosine_table, sine_table)


def rotate_half(values):
    middle = values.shape[-1] // 2
    return jnp.concatenate([-values[..., middle:], values[..., :middle]], axis=-1)


def rotate(values, cosine_table, sine_table):
    return values * cosine_table + rotate_half(values) * sine_table


def rotate_back(gradient, cosine_table, sine_table):
    return gradient * cosine_table - rotate_half(gradient * sine_table)


def gelu_tanh(values):
    return jax.nn.gelu(values, approximate=True)


def split_rows(array, sub_rows):
    return array.reshape((array.shape[0] // sub_rows, sub_rows) + array.shape[1:])


def part_starts(total_rows, sub_rows):
    return sub_rows * jnp.arange(total_rows // sub_rows, dtype=jnp.int32)


def keep_same(partial_value):
    return partial_value


def attend_forward(partial_value, pieces, queries, query_block, score_scale):
    key_rows, value_rows = pieces
    sub_rows = queries.shape[0]

    def attend_visit(running, scan_item):
        key_part, value_part, part_start = scan_item

        def attend_update(running):
            running_max, running_sum, running_out = running
            key_block = (part_start + jnp.arange(sub_rows, dtype=jnp.int32)) // BLOCK
            allowed = (key_block[None, :] <= query_block[:, None])[None]
            scores = (
                jnp.einsum("qhd,khd->hqk", queries, key_part, preferred_element_type=jnp.float32)
                * score_scale
            )
            scores = jnp.where(allowed, scores, masked_score)
            new_max = jnp.maximum(running_max, jnp.max(scores, axis=-1))
            weights = jnp.where(allowed, jnp.exp(scores - new_max[..., None]), 0.0)
            decay = jnp.exp(running_max - new_max)
            running_sum = running_sum * decay + jnp.sum(weights, axis=-1)
            running_out = running_out * decay[..., None] + jnp.einsum(
                "hqk,khd->hqd",
                weights.astype(jnp.bfloat16),
                value_part,
                preferred_element_type=jnp.float32,
            )
            return (new_max, running_sum, running_out)

        return (
            lax.cond(part_start // BLOCK <= query_block[-1], attend_update, keep_same, running),
            None,
        )

    partial_value, unused = lax.scan(
        attend_visit,
        partial_value,
        (
            split_rows(key_rows, sub_rows),
            split_rows(value_rows, sub_rows),
            part_starts(key_rows.shape[0], sub_rows),
        ),
    )
    return partial_value


def on_device(tokens, timestep, time_table, w_qkv, w_out, w_up, w_down, w_ada, cotangent):
    tok_rows = tokens.shape[1]
    model_width = tokens.shape[2]
    heads = model_width // HD
    score_scale = 1.0 / math.sqrt(HD)
    highest_precision = lax.Precision.HIGHEST
    full_weights = (
        lax.all_gather(w_qkv, "fsdp", axis=0, tiled=True),
        lax.all_gather(w_out, "fsdp", axis=0, tiled=True),
        lax.all_gather(w_up, "fsdp", axis=0, tiled=True),
        lax.all_gather(w_down, "fsdp", axis=0, tiled=True),
        lax.all_gather(w_ada, "fsdp", axis=0, tiled=True),
    )
    qkv_full, out_full, up_full, down_full, ada_full = full_weights
    steps_onehot = (
        timestep[0][:, None] == jnp.arange(time_table.shape[0], dtype=jnp.int32)[None, :]
    ).astype(jnp.float32)
    embedded = jnp.dot(steps_onehot, time_table, precision=highest_precision).astype(jnp.bfloat16)
    modulation = jnp.dot(embedded, ada_full, preferred_element_type=jnp.float32)
    per_token = jnp.repeat(modulation, BLOCK, axis=0)
    scale_attn, gate_attn, scale_mlp, gate_mlp = jnp.split(per_token, 4, axis=1)
    inputs = tokens[0].astype(jnp.float32)
    normed_one, inverse_one = layer_norm(inputs)
    residual_first = (normed_one * (1.0 + scale_attn)).astype(jnp.bfloat16)
    projected_output = jnp.dot(
        residual_first, qkv_full, preferred_element_type=jnp.float32
    ).reshape(tok_rows, 3, heads, HD)
    positions = lax.axis_index("ctx") * tok_rows + jnp.arange(tok_rows, dtype=jnp.int32)
    cosine_table, sine_table = rope_tables(positions, HD)
    queries = rotate(projected_output[:, 0], cosine_table, sine_table).astype(jnp.bfloat16)
    key_own = rotate(projected_output[:, 1], cosine_table, sine_table).astype(jnp.bfloat16)
    value_own = projected_output[:, 2].astype(jnp.bfloat16)
    query_block = positions // BLOCK
    start_state = (
        jnp.full((heads, tok_rows), masked_score, jnp.float32),
        jnp.zeros((heads, tok_rows), jnp.float32),
        jnp.zeros((heads, tok_rows, HD), jnp.float32),
    )
    running_max, running_sum, running_out = attend_forward(
        start_state,
        (
            lax.all_gather(key_own, "ctx", axis=0, tiled=True),
            lax.all_gather(value_own, "ctx", axis=0, tiled=True),
        ),
        queries,
        query_block,
        score_scale,
    )
    attn_rows = jnp.transpose(running_out / running_sum[..., None], (1, 0, 2))
    query_lse = running_max + jnp.log(running_sum)
    attn_low = attn_rows.reshape(tok_rows, model_width).astype(jnp.bfloat16)
    attention_projected = jnp.dot(attn_low, out_full, preferred_element_type=jnp.float32)
    middle = inputs + gate_attn * attention_projected
    normed_two, inverse_two = layer_norm(middle)
    residual_second = (normed_two * (1.0 + scale_mlp)).astype(jnp.bfloat16)
    before_activation = jnp.dot(residual_second, up_full, preferred_element_type=jnp.float32)
    gelu_activated, gelu_back = jax.vjp(gelu_tanh, before_activation)
    act_low = gelu_activated.astype(jnp.bfloat16)
    feedforward_output = jnp.dot(act_low, down_full, preferred_element_type=jnp.float32)
    result = middle + gate_mlp * feedforward_output
    qkv_back, out_back, up_back, down_back = (
        lax.all_gather(w_qkv, "fsdp", axis=0, tiled=True),
        lax.all_gather(w_out, "fsdp", axis=0, tiled=True),
        lax.all_gather(w_up, "fsdp", axis=0, tiled=True),
        lax.all_gather(w_down, "fsdp", axis=0, tiled=True),
    )
    upstream = cotangent[0].astype(jnp.float32)
    grad_gate_mlp = upstream * feedforward_output
    grad_mlp = (upstream * gate_mlp).astype(jnp.bfloat16)
    grad_down = jnp.einsum("tf,td->fd", act_low, grad_mlp, preferred_element_type=jnp.float32)
    grad_act = jnp.einsum("td,fd->tf", grad_mlp, down_back, preferred_element_type=jnp.float32)
    grad_pre = gelu_back(grad_act)[0].astype(jnp.bfloat16)
    grad_up = jnp.einsum("td,tf->df", residual_second, grad_pre, preferred_element_type=jnp.float32)
    grad_hidden_two = jnp.einsum("tf,df->td", grad_pre, up_back, preferred_element_type=jnp.float32)
    grad_scale_mlp = grad_hidden_two * normed_two
    grad_middle = upstream + norm_back(grad_hidden_two * (1.0 + scale_mlp), normed_two, inverse_two)
    grad_gate_attn = grad_middle * attention_projected
    grad_attn_proj = (grad_middle * gate_attn).astype(jnp.bfloat16)
    grad_out = jnp.einsum("td,te->de", attn_low, grad_attn_proj, preferred_element_type=jnp.float32)
    grad_attended = jnp.einsum(
        "te,de->td", grad_attn_proj, out_back, preferred_element_type=jnp.float32
    )
    grad_heads = grad_attended.astype(jnp.bfloat16).reshape(tok_rows, heads, HD)
    delta_rows = jnp.sum(grad_heads.astype(jnp.float32) * attn_rows, axis=-1)
    query_delta = jnp.transpose(delta_rows)
    lse_rows = jnp.transpose(query_lse)
    lse_high = lse_rows.astype(jnp.bfloat16)
    lse_rest = (lse_rows - lse_high.astype(jnp.float32)).astype(jnp.bfloat16)
    delta_high = delta_rows.astype(jnp.bfloat16)
    delta_rest = (delta_rows - delta_high.astype(jnp.float32)).astype(jnp.bfloat16)
    stat_rows = jnp.concatenate([lse_high, lse_rest, delta_high, delta_rest], axis=1)
    zero_heads = jnp.zeros((tok_rows, heads, HD), jnp.float32)
    partial_value = (zero_heads, zero_heads, zero_heads)
    grad_query = partial_value[0]
    key_rows = lax.all_gather(key_own, "ctx", axis=0, tiled=True)

    def query_visit(partial_value, scan_item):
        key_part, value_part, part_start = scan_item

        def query_update(partial_value):
            key_block = (part_start + jnp.arange(tok_rows, dtype=jnp.int32)) // BLOCK
            allowed = (key_block[None, :] <= query_block[:, None])[None]
            scores = (
                jnp.einsum("qhd,khd->hqk", queries, key_part, preferred_element_type=jnp.float32)
                * score_scale
            )
            probs = jnp.where(allowed, jnp.exp(scores - query_lse[..., None]), 0.0)
            grad_prob = jnp.einsum(
                "qhd,khd->hqk", grad_heads, value_part, preferred_element_type=jnp.float32
            )
            grad_score = (probs * (grad_prob - query_delta[..., None]) * score_scale).astype(
                jnp.bfloat16
            )
            return partial_value + jnp.einsum(
                "hqk,khd->qhd", grad_score, key_part, preferred_element_type=jnp.float32
            )

        return (
            lax.cond(
                part_start // BLOCK <= query_block[-1], query_update, keep_same, partial_value
            ),
            None,
        )

    grad_query, unused = lax.scan(
        query_visit,
        grad_query,
        (
            split_rows(key_rows, tok_rows),
            split_rows(lax.all_gather(value_own, "ctx", axis=0, tiled=True), tok_rows),
            part_starts(key_rows.shape[0], tok_rows),
        ),
    )
    key_partial_value = (partial_value[1], partial_value[2])
    query_rows = lax.all_gather(queries, "ctx", axis=0, tiled=True)

    def key_visit(running, scan_item):
        query_part, dout_part, stat_part, part_start = scan_item

        def key_update(running):
            grad_key, grad_value = running
            query_blk = (part_start + jnp.arange(tok_rows, dtype=jnp.int32)) // BLOCK
            allowed = (query_blk[:, None] >= query_block[None, :])[None]
            stat_float = stat_part.astype(jnp.float32)
            lse_part = jnp.transpose(stat_float[:, :heads] + stat_float[:, heads : 2 * heads])
            delta_part = jnp.transpose(
                stat_float[:, 2 * heads : 3 * heads] + stat_float[:, 3 * heads :]
            )
            scores = (
                jnp.einsum("qhd,khd->hqk", query_part, key_own, preferred_element_type=jnp.float32)
                * score_scale
            )
            probs = jnp.where(allowed, jnp.exp(scores - lse_part[..., None]), 0.0)
            grad_value = grad_value + jnp.einsum(
                "hqk,qhd->khd",
                probs.astype(jnp.bfloat16),
                dout_part,
                preferred_element_type=jnp.float32,
            )
            grad_prob = jnp.einsum(
                "qhd,khd->hqk", dout_part, value_own, preferred_element_type=jnp.float32
            )
            grad_score = (probs * (grad_prob - delta_part[..., None]) * score_scale).astype(
                jnp.bfloat16
            )
            grad_key = grad_key + jnp.einsum(
                "hqk,qhd->khd", grad_score, query_part, preferred_element_type=jnp.float32
            )
            return (grad_key, grad_value)

        last_seen = (part_start + tok_rows - 1) // BLOCK
        return (lax.cond(last_seen >= query_block[0], key_update, keep_same, running), None)

    key_partial_value, unused = lax.scan(
        key_visit,
        key_partial_value,
        (
            split_rows(query_rows, tok_rows),
            split_rows(lax.all_gather(grad_heads, "ctx", axis=0, tiled=True), tok_rows),
            split_rows(lax.all_gather(stat_rows, "ctx", axis=0, tiled=True), tok_rows),
            part_starts(query_rows.shape[0], tok_rows),
        ),
    )
    grad_key, grad_value = key_partial_value
    grad_query, grad_key, grad_value = (grad_query, grad_key, grad_value)
    grad_query = rotate_back(grad_query, cosine_table, sine_table)
    grad_key = rotate_back(grad_key, cosine_table, sine_table)
    grad_projected = (
        jnp.stack([grad_query, grad_key, grad_value], axis=1)
        .reshape(tok_rows, 3 * model_width)
        .astype(jnp.bfloat16)
    )
    grad_qkv = jnp.einsum(
        "td,te->de", residual_first, grad_projected, preferred_element_type=jnp.float32
    )
    grad_hidden_one = jnp.einsum(
        "te,de->td", grad_projected, qkv_back, preferred_element_type=jnp.float32
    )
    grad_scale_attn = grad_hidden_one * normed_one
    input_grad = grad_middle + norm_back(
        grad_hidden_one * (1.0 + scale_attn), normed_one, inverse_one
    )
    grad_modulation = jnp.concatenate(
        [grad_scale_attn, grad_gate_attn, grad_scale_mlp, grad_gate_mlp], axis=1
    )
    grad_blocks = jnp.sum(
        grad_modulation.reshape(tok_rows // BLOCK, BLOCK, 4 * model_width), axis=1
    )
    embedded_float = embedded.astype(jnp.float32)
    halves = (
        lax.psum_scatter(
            grad_qkv.astype(jnp.bfloat16), "fsdp", scatter_dimension=0, tiled=True
        ).astype(jnp.float32),
        lax.psum_scatter(
            grad_out.astype(jnp.bfloat16), "fsdp", scatter_dimension=0, tiled=True
        ).astype(jnp.float32),
        lax.psum_scatter(
            grad_up.astype(jnp.bfloat16), "fsdp", scatter_dimension=0, tiled=True
        ).astype(jnp.float32),
        lax.psum_scatter(
            grad_down.astype(jnp.bfloat16), "fsdp", scatter_dimension=0, tiled=True
        ).astype(jnp.float32),
    )
    totals = lax.psum((halves[0], halves[1], halves[2], halves[3]), "ctx")
    all_embedded, all_blocks = (
        lax.all_gather(embedded_float, ("ctx", "fsdp"), axis=0, tiled=True),
        lax.all_gather(grad_blocks, ("ctx", "fsdp"), axis=0, tiled=True),
    )
    shard_width = model_width // lax.axis_size("fsdp")
    row_start = lax.axis_index("fsdp") * shard_width
    embedded_part = lax.dynamic_slice_in_dim(all_embedded, row_start, shard_width, 1)
    ada_total = jnp.dot(jnp.transpose(embedded_part), all_blocks, precision=highest_precision)
    return (result[None], input_grad[None], totals[0], totals[1], totals[2], totals[3], ada_total)


def remote(source, target, send_sem, recv_sem, **where):
    return pltpu.make_async_remote_copy(
        src_ref=source,
        dst_ref=target,
        send_sem=send_sem,
        recv_sem=recv_sem,
        device_id=where,
        device_id_type=MESH,
    )


def landed(ref, sem):
    pltpu.make_async_copy(ref, ref, sem).wait()


def head_place(me):
    plane = me // 4
    spot = lax.rem(me, 4)
    odd = lax.rem(plane, 2)
    idle = 3 - 2 * odd
    head = 3 * plane + spot - odd * (spot // 2)
    return spot != idle, head


def head_owner(head):
    plane = head // 3
    rank = lax.rem(head, 3)
    odd = lax.rem(plane, 2)
    return 4 * plane + rank + odd * ((rank + 1) // 2)


def scatter_sent(me, heads, source, target, send_sem, recv_sem):
    def finish(head, carry):
        owner = head_owner(head)

        @pl.when(owner != me)
        def _():
            remote(
                source.at[head], target.at[me], send_sem.at[head], recv_sem.at[me], ctx=owner
            ).wait_send()

        return carry

    lax.fori_loop(0, heads, finish, 0)


def return_block(me, head, block, source, target, send_sem, recv_sem):
    @pl.when(block != me)
    def _():
        remote(
            source.at[block], target.at[head], send_sem.at[block], recv_sem.at[head], ctx=block
        ).start()

    @pl.when(block == me)
    def _():
        pltpu.make_async_copy(source.at[block], target.at[head], recv_sem.at[head]).start()


def return_sent(me, head, blocks, source, target, send_sem, recv_sem):
    def finish(block, carry):
        @pl.when(block != me)
        def _():
            remote(
                source.at[block], target.at[head], send_sem.at[block], recv_sem.at[head], ctx=block
            ).wait_send()

        return carry

    lax.fori_loop(0, blocks, finish, 0)


def wait_heads(heads, target, recv_sem):
    def finish(head, carry):
        landed(target.at[head], recv_sem.at[head])
        return carry

    lax.fori_loop(0, heads, finish, 0)


def transposed(values):
    return jnp.transpose(values.astype(jnp.float32)).astype(values.dtype)


def add_into(target, left, right, rows):
    step = 48

    def body(index, carry):
        spot = pl.ds(pl.multiple_of(index * step, step), step)
        total = left(spot).astype(jnp.float32) + right(spot).astype(jnp.float32)
        target(spot, total.astype(jnp.bfloat16))
        return carry

    lax.fori_loop(0, rows // step, body, 0)


def product(left, right):
    return jnp.dot(left, right, preferred_element_type=jnp.float32)


def product_back(left, right):
    return lax.dot_general(
        left, right, (((1,), (1,)), ((), ())), preferred_element_type=jnp.float32
    )


def layer_kernel(
    blocks, heads,
    tok_ref, cot_ref, emb_ref, rope_ref, ada_hbm, qkv_hbm, out_hbm, up_hbm, down_hbm,
    result_ref, ingrad_ref, table_ref, og_qkv, og_out, og_up, og_down,
    wq, wo, wu, wd, mod_ref, emb_other, part_other, part_send,
    hid1_t, mid_ref, ap_ref, sums_ref, cos_ref, sin_ref,
    qs_ref, buf_ref, mix_ref, lse_ref, att_ref, douts_ref, got_ref,
    parts, sib_ref, row_ref, x_ref, z_ref, res_ref, stage_ref,
    own_sem, small_send, small_recv, w_send, w_recv,
    fs, fr, fbs, fbr, bs, br, bbs, bbr,
    s_sib, r_sib, s_row, r_row, s_x, r_x, s_z, r_z, s_az, r_az, s_ax, r_ax, s_as, r_as,
    s_t, r_t, out_sem, free_sem,
):
    me = lax.axis_index("ctx")
    row = lax.axis_index("fsdp")
    other = 1 - row
    piece = lax.rem(me, 4)
    core = lax.rem(me, 2)
    xbit = lax.rem(me // 2, 2)
    plane = me // 4
    planes = blocks // 4
    chip_next = jnp.bitwise_xor(me, 2)
    sibling = jnp.bitwise_xor(me, 1)
    gland_ref = qs_ref
    owner, head = head_place(me)
    width = tok_ref.shape[1]
    score_scale = 1.0 / math.sqrt(HD)

    barrier = pltpu.get_barrier_semaphore()
    pl.semaphore_signal(barrier, inc=1, device_id={"fsdp": other}, device_id_type=MESH)

    def greet(step, carry):
        pl.semaphore_signal(
            barrier, inc=1, device_id={"ctx": lax.rem(me + step, blocks)}, device_id_type=MESH
        )
        return carry

    lax.fori_loop(1, blocks, greet, 0)
    pl.semaphore_wait(barrier, blocks)

    shards = (qkv_hbm, out_hbm, up_hbm, down_hbm)
    wholes = (wq, wo, wu, wd)
    quarter_rows = [shard.shape[0] // 4 for shard in shards]
    chunks = [
        (0, 0, quarter_rows[0] // 2),
        (0, quarter_rows[0] // 2, quarter_rows[0] // 2),
        (1, 0, quarter_rows[1]),
        (2, 0, quarter_rows[2]),
        (3, 0, quarter_rows[3]),
    ]

    def chunk_ref(index, which):
        weight, first, count = chunks[index]
        start = other * 4 * quarter_rows[weight] + which * quarter_rows[weight] + first
        return wholes[weight].at[pl.ds(pl.multiple_of(start, 16), count)]

    def y_copy(index):
        weight, first, count = chunks[index]
        near = piece * quarter_rows[weight] + first
        far = row * 4 * quarter_rows[weight] + near
        return remote(
            shards[weight].at[pl.ds(pl.multiple_of(near, 16), count)],
            wholes[weight].at[pl.ds(pl.multiple_of(far, 16), count)],
            w_send.at[index, 0], w_recv.at[index, 0], fsdp=other,
        )

    def onward(index, which, slot, peer):
        ref = chunk_ref(index, which)
        return remote(ref, ref, w_send.at[index, slot], w_recv.at[index, slot], ctx=peer)

    def pass_on(index):
        landed(chunk_ref(index, piece), w_recv.at[index, 0])
        onward(index, piece, 1, chip_next).start()
        onward(index, piece, 2, sibling).start()

    def pass_last(index):
        across = jnp.bitwise_xor(piece, 2)
        landed(chunk_ref(index, across), w_recv.at[index, 1])
        onward(index, across, 3, sibling).start()

    def chunk_done(index):
        landed(chunk_ref(index, jnp.bitwise_xor(piece, 1)), w_recv.at[index, 2])
        landed(chunk_ref(index, jnp.bitwise_xor(piece, 3)), w_recv.at[index, 3])

    def own_copy(weight):
        half = shards[weight].shape[0]
        start = pl.multiple_of(row * half, 16)
        return pltpu.make_async_copy(
            shards[weight], wholes[weight].at[pl.ds(start, half)], own_sem.at[weight]
        )

    emb_copy = remote(emb_ref, emb_other, small_send.at[0], small_recv.at[0], fsdp=other)
    emb_copy.start()
    y_copy(0).start()
    y_copy(1).start()

    def opening(ada_ref, hid1):
        ada_copy = pltpu.make_async_copy(ada_hbm, ada_ref, own_sem.at[4])
        ada_copy.start()
        for weight in range(4):
            own_copy(weight).start()
        half_width = width // 2
        cols = pl.ds(pl.multiple_of(row * half_width, 128), half_width)
        ada_copy.wait()
        emb_copy.wait()
        both = jnp.concatenate([emb_ref[:, cols], emb_other[:, cols]], axis=0)
        partial = product(both.astype(jnp.bfloat16), ada_ref[...])
        mod_ref[...] = partial[:8]
        part_send[...] = partial[8:]
        part_copy = remote(part_send, part_other, small_send.at[1], small_recv.at[1], fsdp=other)
        part_copy.start()
        lanes = lax.broadcasted_iota(jnp.int32, (HD // 2, 128), 1)
        pick = lanes == me
        cos_block = jnp.sum(jnp.where(pick, rope_ref[:, 2 * BLOCK : 2 * BLOCK + 128], 0.0), axis=1, keepdims=True)
        sin_block = jnp.sum(jnp.where(pick, rope_ref[:, 2 * BLOCK + 128 :], 0.0), axis=1, keepdims=True)
        cos_row = rope_ref[:, :BLOCK]
        sin_row = rope_ref[:, BLOCK : 2 * BLOCK]
        cos_ref[...] = cos_row * cos_block - sin_row * sin_block
        sin_ref[...] = sin_row * cos_block + cos_row * sin_block
        pass_on(0)
        normed, unused = layer_norm(tok_ref[...].astype(jnp.float32))
        part_copy.wait()
        mod_ref[...] += part_other[...]
        low = (normed * (1.0 + mod_ref[:1, :width])).astype(jnp.bfloat16)
        hid1[...] = low
        hid1_t[...] = transposed(low)
        pass_on(1)
        pass_last(0)
        pass_last(1)
        for index in (0, 1):
            y_copy(index).wait_send()
        for index in (2, 3, 4):
            y_copy(index).start()
        own_copy(0).wait()
        chunk_done(0)
        chunk_done(1)

        def project(group, carry):
            spans = []
            for kind in range(3):
                cols = pl.ds(pl.multiple_of(kind * width + group * 4 * HD, 4 * HD), 4 * HD)
                spans.append(jnp.transpose(product(hid1[...], wq[:, cols])))
            cos, sin = cos_ref[...], sin_ref[...]
            for inner in range(4):
                which = group * 4 + inner
                for kind in range(2):
                    top = spans[kind][inner * HD : inner * HD + HD // 2]
                    low_half = spans[kind][inner * HD + HD // 2 : (inner + 1) * HD]
                    turned = jnp.concatenate(
                        [top * cos - low_half * sin, low_half * cos + top * sin], axis=0
                    ).astype(jnp.bfloat16)
                    if kind == 0:
                        turned = turned * jnp.bfloat16(score_scale)
                    qs_ref[which, kind * HD : (kind + 1) * HD, :] = turned
                qs_ref[which, 2 * HD :, :] = spans[2][inner * HD : (inner + 1) * HD].astype(
                    jnp.bfloat16
                )
                send_head(which, qs_ref, buf_ref, fs, fr)
            return carry

        lax.fori_loop(0, heads // 4, project, 0)

    def send_head(which, source, target, send_sem, recv_sem):
        goal = head_owner(which)

        @pl.when(goal != me)
        def _():
            remote(
                source.at[which], target.at[me], send_sem.at[which], recv_sem.at[me], ctx=goal
            ).start()

        @pl.when(goal == me)
        def _():
            pltpu.make_async_copy(source.at[which], target.at[me], recv_sem.at[me]).start()

    pl.run_scoped(
        opening,
        pltpu.VMEM((width // 2, 4 * width), jnp.bfloat16),
        pltpu.VMEM((BLOCK, width), jnp.bfloat16),
    )

    def forward(pair_ref, low_ref):
        def attend(block):
            landed(buf_ref.at[block], fr.at[block])
            rows = pl.ds(pl.multiple_of(block * BLOCK, BLOCK), BLOCK)
            pair_ref[rows, :] = transposed(buf_ref[block, HD:, :])
            query = jnp.concatenate(
                [buf_ref[block, :HD, :], jnp.zeros((HD, BLOCK), jnp.bfloat16)], axis=0
            )

            def key_block(key, state):
                high, total, mixed = state
                key_rows = pl.ds(pl.multiple_of(key * BLOCK, BLOCK), BLOCK)
                scores = product(pair_ref[key_rows, :], query)
                new_high = jnp.maximum(high, jnp.max(scores, axis=0, keepdims=True))
                weights = jnp.exp(scores - new_high)
                decay = jnp.exp(high - new_high)
                total = total * decay + jnp.sum(weights, axis=0, keepdims=True)
                mixed = mixed * decay + product(
                    buf_ref[key, 2 * HD :, :], weights.astype(jnp.bfloat16)
                )
                return new_high, total, mixed

            high, total, mixed = lax.fori_loop(
                0,
                block + 1,
                key_block,
                (
                    jnp.full((1, BLOCK), masked_score, jnp.float32),
                    jnp.zeros((1, BLOCK), jnp.float32),
                    jnp.zeros((HD, BLOCK), jnp.float32),
                ),
            )
            mixed = mixed / total
            mix_ref[block] = mixed
            low_ref[block] = mixed.astype(jnp.bfloat16)
            lse_ref[block] = jnp.broadcast_to(high + jnp.log(total), (8, BLOCK))
            return_block(me, head, block, low_ref, att_ref, fbs, fbr)

        def visit(block, carry):
            @pl.when(owner)
            def _():
                attend(block)

            for when, event in FORWARD_EVENTS:
                @pl.when(block == when)
                def _(event=event):
                    (pass_on, pass_last)[event[0]](event[1])

            return carry

        lax.fori_loop(0, blocks, visit, 0)

        @pl.when(owner)
        def _():
            return_sent(me, head, blocks, low_ref, att_ref, fbs, fbr)

        scatter_sent(me, heads, qs_ref, buf_ref, fs, fr)
        wait_heads(heads, att_ref, fbr)

    pl.run_scoped(
        forward,
        pltpu.VMEM((blocks * BLOCK, 2 * HD), jnp.bfloat16),
        pltpu.VMEM((blocks, HD, BLOCK), jnp.bfloat16),
    )

    span = width // 2
    mine = pl.ds(pl.multiple_of(core * span, 128), span)
    theirs = pl.ds(pl.multiple_of((1 - core) * span, 128), span)
    deep = width // 2
    half_deep = deep // 2
    small = half_deep // planes

    def part_of(unit, half, cols):
        return parts.at[unit, half, :, cols]

    def qkv_part(unit, half, cols):
        return wd.at[pl.ds(pl.multiple_of(((unit - 9) * 2 + half) * deep, 16), deep), cols]

    def sib_of(unit, half):
        return sib_ref.at[unit, half]

    def qkv_sib(unit, half):
        cols = pl.ds(pl.multiple_of(((unit - 9) * 2 + half) * span, 128), span)
        return wu.at[pl.ds(0, deep), cols]

    def pipeline(part, sib):
        def to_sibling(unit):
            return [
                remote(part(unit, half, theirs), sib(unit, half),
                       s_sib.at[unit, half], r_sib.at[unit, half], ctx=sibling)
                for half in range(2)
            ]

        def to_row(unit):
            return [remote(sib(unit, other), row_ref.at[unit],
                           s_row.at[unit], r_row.at[unit], fsdp=other)]

        def to_x(unit):
            rows = pl.ds(pl.multiple_of((1 - xbit) * half_deep, 16), half_deep)
            return [remote(row_ref.at[unit, rows], x_ref.at[unit],
                           s_x.at[unit], r_x.at[unit], ctx=chip_next)]

        def to_z(unit):
            copies = []
            for step in range(1, planes):
                goal = lax.rem(plane + step, planes)
                rows = pl.ds(pl.multiple_of(goal * small, 16), small)
                copies.append(
                    remote(x_ref.at[unit, rows], z_ref.at[unit, step - 1],
                           s_z.at[unit, step - 1], r_z.at[unit, step - 1], ctx=4 * goal + piece)
                )
            return copies

        def slab(unit, which):
            rows = pl.ds(pl.multiple_of(xbit * half_deep + which * small, 16), small)
            return res_ref.at[unit, rows, mine]

        def along_z(unit):
            return [
                remote(slab(unit, plane), slab(unit, plane),
                       s_az.at[unit, step - 1], r_az.at[unit, step - 1],
                       ctx=4 * lax.rem(plane + step, planes) + piece)
                for step in range(1, planes)
            ]

        def along_x(unit):
            rows = pl.ds(pl.multiple_of(xbit * half_deep, 16), half_deep)
            ref = res_ref.at[unit, rows, mine]
            return [remote(ref, ref, s_ax.at[unit], r_ax.at[unit], ctx=chip_next)]

        def along_s(unit):
            ref = res_ref.at[unit, :, mine]
            return [remote(ref, ref, s_as.at[unit], r_as.at[unit], ctx=sibling)]

        def launch(copies):
            for copy in copies:
                copy.start()

        def write_out(unit, which, cols):
            def saved():
                return pltpu.make_async_copy(
                    stage_ref.at[which], og_out.at[:, pl.ds(0, span)], out_sem.at[which]
                )

            @pl.when(unit > 0)
            def _():
                saved().wait()

            def convert(index, carry):
                spot = pl.ds(pl.multiple_of(index * 48, 48), 48)
                stage_ref[which, spot, :] = res_ref[unit, spot, cols].astype(jnp.float32)
                return carry

            lax.fori_loop(0, deep // 48, convert, 0)
            side = core if which == 0 else 1 - core
            kind = lax.rem(unit, 4)
            order = 2 * (unit // 4) + lax.rem(kind, 2)

            def save(target):
                pltpu.make_async_copy(stage_ref.at[which], target, out_sem.at[which]).start()

            @pl.when((unit < 8) & (kind < 2))
            def _():
                save(og_down.at[pl.ds(pl.multiple_of(order * deep, 8), deep),
                                pl.ds(pl.multiple_of(side * span, 128), span)])

            @pl.when((unit < 8) & (kind >= 2))
            def _():
                start = side * 4 * span + order * span
                save(og_up.at[:, pl.ds(pl.multiple_of(start, 128), span)])

            @pl.when(unit == 8)
            def _():
                save(og_out.at[:, pl.ds(pl.multiple_of(side * span, 128), span)])

            @pl.when(unit > 8)
            def _():
                start = (unit - 9) * width + side * span
                save(og_qkv.at[:, pl.ds(pl.multiple_of(start, 128), span)])

        def stage0(unit):
            launch(to_sibling(unit))

        def stage1(unit):
            for half in range(2):
                landed(sib(unit, half), r_sib.at[unit, half])
                ref, part_ref = sib(unit, half), part(unit, half, mine)

                def put(spot, value, ref=ref):
                    ref[spot, :] = value

                add_into(put, lambda spot, ref=ref: ref[spot, :],
                         lambda spot, part_ref=part_ref: part_ref[spot, :], deep)
            launch(to_row(unit))

        def stage2(unit):
            landed(row_ref.at[unit], r_row.at[unit])
            ref = sib(unit, row)

            def put(spot, value):
                row_ref[unit, spot, :] = value

            add_into(put, lambda spot: row_ref[unit, spot, :], lambda spot: ref[spot, :], deep)
            launch(to_x(unit))

        def stage3(unit):
            landed(x_ref.at[unit], r_x.at[unit])
            ref = row_ref.at[unit, pl.ds(pl.multiple_of(xbit * half_deep, 16), half_deep)]

            def put(spot, value):
                x_ref[unit, spot, :] = value

            add_into(put, lambda spot: x_ref[unit, spot, :], lambda spot: ref[spot, :], half_deep)
            launch(to_z(unit))

        def stage4(unit):
            rows = pl.ds(pl.multiple_of(plane * small, 16), small)
            total = x_ref[unit, rows, :].astype(jnp.float32)
            for step in range(1, planes):
                landed(z_ref.at[unit, step - 1], r_z.at[unit, step - 1])
                total += z_ref[unit, step - 1].astype(jnp.float32)
            spots = pl.ds(pl.multiple_of(xbit * half_deep + plane * small, 16), small)
            res_ref[unit, spots, mine] = total.astype(jnp.bfloat16)
            launch(along_z(unit))

        def stage5(unit):
            for step in range(1, planes):
                landed(slab(unit, lax.rem(plane + planes - step, planes)), r_az.at[unit, step - 1])
            launch(along_x(unit))

        def stage6(unit):
            rows = pl.ds(pl.multiple_of((1 - xbit) * half_deep, 16), half_deep)
            landed(res_ref.at[unit, rows, mine], r_ax.at[unit])
            launch(along_s(unit))
            write_out(unit, 0, mine)

        def stage7(unit):
            landed(res_ref.at[unit, :, theirs], r_as.at[unit])
            write_out(unit, 1, theirs)
            for make in (to_sibling, to_row, to_x, to_z, along_z, along_x, along_s):
                for copy in make(unit):
                    copy.wait_send()

        return stage0, stage1, stage2, stage3, stage4, stage5, stage6, stage7

    early = pipeline(part_of, sib_of)
    late = pipeline(qkv_part, qkv_sib)

    def tick(stages, first, count, time):
        for depth in range(1, 8):
            unit = time - (depth - 1)

            @pl.when((unit >= 0) & (unit < count))
            def _(depth=depth, unit=unit):
                stages[depth](first + unit)

    def middle_part(act_ref, slope_ref, hid2, hid2_t, low_ref):
        acc_ref = ingrad_ref
        own_copy(1).wait()
        chunk_done(2)
        att_t = att_ref[...].reshape(width, BLOCK)
        ap_ref[...] = product(transposed(att_t), wo[...])
        gate_attn = mod_ref[:1, width : 2 * width]
        scale_mlp = mod_ref[:1, 2 * width : 3 * width]
        gate_mlp = mod_ref[:1, 3 * width :]
        mid_ref[...] = tok_ref[...].astype(jnp.float32) + gate_attn * ap_ref[...]
        normed, unused = layer_norm(mid_ref[...])
        low = (normed * (1.0 + scale_mlp)).astype(jnp.bfloat16)
        hid2[...] = low
        hid2_t[...] = transposed(low)
        acc_ref[...] = jnp.zeros_like(acc_ref)
        own_copy(2).wait()
        chunk_done(3)
        for late_event in AFTER_EVENTS:
            (pass_on, pass_last)[late_event[0]](late_event[1])
        own_copy(3).wait()
        chunk_done(4)
        curve = math.sqrt(2.0 / math.pi)

        def up(index, carry):
            cols = pl.ds(pl.multiple_of(index * width, width), width)
            before = product(hid2[...], wu[:, cols])
            square = before * before
            bent = jnp.tanh(curve * (before + 0.044715 * (square * before)))
            after = (0.5 * before * (1.0 + bent)).astype(jnp.bfloat16)
            act_ref[:, cols] = after
            slope_ref[:, cols] = 0.5 * (1.0 + bent) + 0.5 * before * (1.0 - bent * bent) * (
                curve * (1.0 + 3.0 * 0.044715 * square)
            )
            acc_ref[...] += product(after, wd[cols, :])
            return carry

        lax.fori_loop(0, 4, up, 0)
        grad = cot_ref[...].astype(jnp.float32)
        mlp_out = acc_ref[...]
        result_ref[...] = mid_ref[...] + gate_mlp * mlp_out
        sums_ref[3:4, :] = jnp.sum(grad * mlp_out, axis=0, keepdims=True)
        low_ref[...] = (grad * gate_mlp).astype(jnp.bfloat16)
        acc_ref[...] = jnp.zeros_like(acc_ref)

        def down(index, carry):
            for side in range(2):
                cols = pl.ds(pl.multiple_of(side * 2 * width + index * width, width), width)
                grad_act = product_back(low_ref[...], wd[cols, :])
                grad_pre = (grad_act * slope_ref[:, cols]).astype(jnp.bfloat16)
                grad_down = product(transposed(act_ref[:, cols]), low_ref[...])
                for pick in range(2):
                    parts[4 * index + pick, side] = grad_down[
                        pick * deep : (pick + 1) * deep
                    ].astype(jnp.bfloat16)
                grad_up = product(hid2_t[...], grad_pre).astype(jnp.bfloat16)
                for pick in range(2):
                    for half in range(2):
                        parts[4 * index + 2 + pick, half, :, side * span : (side + 1) * span] = (
                            grad_up[half * deep : (half + 1) * deep, pick * span : (pick + 1) * span]
                        )
                acc_ref[...] += product_back(grad_pre, wu[:, cols])
            for pick in range(4):
                early[0](4 * index + pick)
            return carry

        lax.fori_loop(0, 2, down, 0)
        for index in range(5):
            if index > 1:
                y_copy(index).wait_send()
            onward(index, piece, 1, chip_next).wait_send()
            onward(index, piece, 2, sibling).wait_send()
            onward(index, jnp.bitwise_xor(piece, 2), 3, sibling).wait_send()
        pl.semaphore_signal(free_sem, inc=1, device_id={"ctx": sibling}, device_id_type=MESH)
        grad_hidden = acc_ref[...]
        normed, inverse = layer_norm(mid_ref[...])
        sums_ref[2:3, :] = jnp.sum(grad_hidden * normed, axis=0, keepdims=True)
        grad_mid = cot_ref[...].astype(jnp.float32) + norm_back(
            grad_hidden * (1.0 + scale_mlp), normed, inverse
        )
        ingrad_ref[...] = grad_mid
        sums_ref[1:2, :] = jnp.sum(grad_mid * ap_ref[...], axis=0, keepdims=True)
        gap = (grad_mid * gate_attn).astype(jnp.bfloat16)
        low_ref[...] = gap
        douts_ref[...] = product_back(wo[...], gap).astype(jnp.bfloat16).reshape(
            heads, HD, BLOCK
        )

        def send_dout(step, carry):
            send_head(lax.rem(step + 3 * plane, heads), douts_ref, got_ref, bs, br)
            return carry

        lax.fori_loop(0, heads, send_dout, 0)
        grad_out = product(att_ref[...].reshape(width, BLOCK), low_ref[...]).astype(jnp.bfloat16)
        parts[8, 0] = grad_out[:deep]
        parts[8, 1] = grad_out[deep:]
        early[0](8)

    pl.run_scoped(
        middle_part,
        pltpu.VMEM((BLOCK, 4 * width), jnp.bfloat16),
        pltpu.VMEM((BLOCK, 4 * width), jnp.float32),
        pltpu.VMEM((BLOCK, width), jnp.bfloat16),
        pltpu.VMEM((width, BLOCK), jnp.bfloat16),
        pltpu.VMEM((BLOCK, width), jnp.bfloat16),
    )

    def backward(pair_ref, total_ref, low_ref):
        @pl.when(owner)
        def _():
            def prepare(block, carry):
                rows = pl.ds(pl.multiple_of(block * BLOCK, BLOCK), BLOCK)
                pair_ref[rows, :] = transposed(buf_ref[block, HD:, :])
                total_ref[rows, :] = jnp.zeros((BLOCK, 2 * HD), jnp.float32)
                return carry

            lax.fori_loop(0, blocks, prepare, 0)

        def attend_back(block):
            landed(got_ref.at[block], br.at[block])
            dout = got_ref[block]
            query = buf_ref[block, :HD, :]
            zero = jnp.zeros((HD, BLOCK), jnp.bfloat16)
            delta = jnp.sum(dout.astype(jnp.float32) * mix_ref[block], axis=0, keepdims=True)
            lse = lse_ref[block, :1, :]
            query_down = jnp.concatenate([query, zero], axis=0)
            dout_down = jnp.concatenate([zero, dout], axis=0)
            dout_side = transposed(jnp.concatenate([dout, zero], axis=0))
            query_side = transposed(jnp.concatenate([zero, query], axis=0))

            def key_block(key, grad_query):
                key_rows = pl.ds(pl.multiple_of(key * BLOCK, BLOCK), BLOCK)
                pair = pair_ref[key_rows, :]
                probs = jnp.exp(product(pair, query_down) - lse)
                grad_scores = (probs * (product(pair, dout_down) - delta)).astype(jnp.bfloat16)
                total_ref[key_rows, :] += product(
                    probs.astype(jnp.bfloat16), dout_side
                ) + product(grad_scores, query_side)
                return grad_query + product(buf_ref[key, HD : 2 * HD, :], grad_scores)

            grad_query = lax.fori_loop(
                0, block + 1, key_block, jnp.zeros((HD, BLOCK), jnp.float32)
            )
            rows = pl.ds(pl.multiple_of(block * BLOCK, BLOCK), BLOCK)
            low_ref[block, :HD, :] = (grad_query * score_scale).astype(jnp.bfloat16)
            sums = jnp.transpose(total_ref[rows, :]).astype(jnp.bfloat16)
            low_ref[block, HD : 2 * HD, :] = sums[HD:]
            low_ref[block, 2 * HD :, :] = sums[:HD]
            return_block(me, head, block, low_ref, gland_ref, bbs, bbr)

        def visit(step, carry):
            @pl.when(owner)
            def _():
                attend_back(blocks - 1 - step)

            tick(early, 0, 9, step - FIRST_TICK)
            return carry

        lax.fori_loop(0, blocks, visit, 0)

        @pl.when(owner)
        def _():
            return_sent(me, head, blocks, low_ref, gland_ref, bbs, bbr)

        scatter_sent(me, heads, douts_ref, got_ref, bs, br)
        wait_heads(heads, gland_ref, bbr)

    pl.run_scoped(
        backward,
        pltpu.VMEM((blocks * BLOCK, 2 * HD), jnp.bfloat16),
        pltpu.VMEM((blocks * BLOCK, 2 * HD), jnp.float32),
        pltpu.VMEM((blocks, 3 * HD, BLOCK), jnp.bfloat16),
    )

    def closing(gproj, acc_ref):
        def turn_back(group, carry):
            cos, sin = cos_ref[...], sin_ref[...]
            for kind in range(3):
                pieces = []
                for inner in range(4):
                    which = group * 4 + inner
                    if kind == 2:
                        pieces.append(gland_ref[which, 2 * HD :, :])
                        continue
                    top = gland_ref[which, kind * HD : kind * HD + HD // 2, :].astype(jnp.float32)
                    bottom = gland_ref[
                        which, kind * HD + HD // 2 : (kind + 1) * HD, :
                    ].astype(jnp.float32)
                    pieces.append((top * cos + bottom * sin).astype(jnp.bfloat16))
                    pieces.append((bottom * cos - top * sin).astype(jnp.bfloat16))
                cols = pl.ds(pl.multiple_of(kind * width + group * 4 * HD, 4 * HD), 4 * HD)
                gproj[:, cols] = transposed(jnp.concatenate(pieces, axis=0))
            return carry

        lax.fori_loop(0, heads // 4, turn_back, 0)
        acc_ref[...] = jnp.zeros_like(acc_ref)
        pl.semaphore_wait(free_sem, 1)

        def gradient(index, carry):
            cols = pl.ds(pl.multiple_of(index * width, width), width)
            low = product(hid1_t[...], gproj[:, cols]).astype(jnp.bfloat16)
            wd[pl.ds(pl.multiple_of(index * width, width), width), :] = low
            late[0](9 + index)
            return carry

        lax.fori_loop(0, 3, gradient, 0)

        def back(index, carry):
            cols = pl.ds(pl.multiple_of(index * width, width), width)
            acc_ref[...] += product_back(gproj[:, cols], wq[:, cols])
            return carry

        tick(late, 9, 3, 0)
        lax.fori_loop(0, 3, back, 0)
        normed, inverse = layer_norm(tok_ref[...].astype(jnp.float32))
        grad_hidden = acc_ref[...]
        sums_ref[0:1, :] = jnp.sum(grad_hidden * normed, axis=0, keepdims=True)
        ingrad_ref[...] = ingrad_ref[...] + norm_back(
            grad_hidden * (1.0 + mod_ref[:1, :width]), normed, inverse
        )

    pl.run_scoped(
        closing,
        pltpu.VMEM((BLOCK, 3 * width), jnp.bfloat16),
        pltpu.VMEM((BLOCK, width), jnp.float32),
    )

    def slots(first, count):
        return table_ref.at[pl.ds(first, count)]

    chip_slot = core * 4 * planes + 4 * plane

    def table_row():
        ref = slots(chip_slot + 2 * xbit + row, 1)
        return [remote(ref, ref, s_t.at[0], r_t.at[0], fsdp=other)]

    def table_x():
        ref = slots(chip_slot + 2 * xbit, 2)
        return [remote(ref, ref, s_t.at[1], r_t.at[1], ctx=chip_next)]

    def table_z():
        ref = slots(chip_slot, 4)
        return [
            remote(ref, ref, s_t.at[2 + step], r_t.at[2 + step],
                   ctx=4 * lax.rem(plane + step, planes) + piece)
            for step in range(1, planes)
        ]

    def table_s():
        ref = slots(core * 4 * planes, 4 * planes)
        return [remote(ref, ref, s_t.at[2], r_t.at[2], ctx=sibling)]

    spot = chip_slot + 2 * xbit + row
    for index in range(4):
        table_ref[spot, index : index + 1, :] = sums_ref[index : index + 1, :]
    table_ref[spot, 4:5, :] = emb_ref[:1, :]
    for copy in table_row():
        copy.start()

    def finish(time, carry):
        tick(late, 9, 3, time)

        @pl.when(time == 1)
        def _():
            landed(slots(chip_slot + 2 * xbit + other, 1), r_t.at[0])
            for copy in table_x():
                copy.start()

        @pl.when(time == 2)
        def _():
            landed(slots(chip_slot + 2 * (1 - xbit), 2), r_t.at[1])
            for copy in table_z():
                copy.start()

        @pl.when(time == 4)
        def _():
            for step in range(1, planes):
                goal = lax.rem(plane + planes - step, planes)
                landed(slots(core * 4 * planes + 4 * goal, 4), r_t.at[2 + step])
            for copy in table_s():
                copy.start()

        return carry

    def rest(time, carry):
        tick(early, 0, 9, time)
        return carry

    lax.fori_loop(blocks - FIRST_TICK, 15, rest, 0)
    lax.fori_loop(1, 9, finish, 0)
    landed(slots((1 - core) * 4 * planes, 4 * planes), r_t.at[2])
    for copies in (table_row(), table_x(), table_z(), table_s()):
        for copy in copies:
            copy.wait_send()
    for which in range(2):
        pltpu.make_async_copy(
            stage_ref.at[which], og_out.at[:, pl.ds(0, span)], out_sem.at[which]
        ).wait()


FORWARD_EVENTS = (
    (1, (0, 2)),
    (4, (1, 2)),
    (8, (0, 3)),
    (11, (1, 3)),
    (13, (0, 4)),
)
AFTER_EVENTS = ((1, 4),)
FIRST_TICK = 1


def rope_constants(blocks):
    half = HD // 2
    frequency = rope_base ** (-2.0 * np.arange(half, dtype=np.float64) / HD)
    inner = frequency[:, None] * np.arange(BLOCK, dtype=np.float64)[None, :]
    outer = frequency[:, None] * (BLOCK * np.arange(128, dtype=np.float64))[None, :]
    outer = np.where(np.arange(128)[None, :] < blocks, outer, 0.0)
    return np.concatenate(
        [np.cos(inner), np.sin(inner), np.cos(outer), np.sin(outer)], axis=1
    ).astype(np.float32)


def fast_device(tokens, timestep, time_table, w_qkv, w_out, w_up, w_down, w_ada, cotangent):
    rows, width = tokens.shape[1:]
    heads = width // HD
    blocks = lax.axis_size("ctx")
    planes = blocks // 4
    deep, span = width // 2, width // 2
    embedded = lax.dynamic_slice_in_dim(time_table, timestep[0, 0], 1, 0)
    embedded = embedded.astype(jnp.bfloat16).astype(jnp.float32)
    emb_rows = jnp.broadcast_to(embedded, (8, width))
    hbm = pl.BlockSpec(memory_space=pl.ANY)
    vmem = pl.BlockSpec(memory_space=pltpu.VMEM)
    low, high = jnp.bfloat16, jnp.float32
    dma = pltpu.SemaphoreType.DMA
    steps = planes - 1
    units = 12
    scratch = [
        pltpu.VMEM((width, 3 * width), low),
        pltpu.VMEM((width, width), low),
        pltpu.VMEM((width, 4 * width), low),
        pltpu.VMEM((4 * width, width), low),
        pltpu.VMEM((8, 4 * width), high),
        pltpu.VMEM((8, width), high),
        pltpu.VMEM((8, 4 * width), high),
        pltpu.VMEM((8, 4 * width), high),
        pltpu.VMEM((width, BLOCK), low),
        pltpu.VMEM((BLOCK, width), high),
        pltpu.VMEM((BLOCK, width), high),
        pltpu.VMEM((8, width), high),
        pltpu.VMEM((HD // 2, BLOCK), high),
        pltpu.VMEM((HD // 2, BLOCK), high),
        pltpu.VMEM((heads, 3 * HD, BLOCK), low),
        pltpu.VMEM((blocks, 3 * HD, BLOCK), low),
        pltpu.VMEM((blocks, HD, BLOCK), high),
        pltpu.VMEM((blocks, 8, BLOCK), high),
        pltpu.VMEM((heads, HD, BLOCK), low),
        pltpu.VMEM((heads, HD, BLOCK), low),
        pltpu.VMEM((blocks, HD, BLOCK), low),
        pltpu.VMEM((9, 2, deep, width), low),
        pltpu.VMEM((9, 2, deep, span), low),
        pltpu.VMEM((units, deep, span), low),
        pltpu.VMEM((units, deep // 2, span), low),
        pltpu.VMEM((units, steps, deep // 2 // planes, span), low),
        pltpu.VMEM((units, deep, width), low),
        pltpu.VMEM((2, deep, span), high),
    ]
    sems = [
        (5,), (2,), (2,), (5, 4), (5, 4),
        (heads,), (blocks,), (blocks,), (heads,),
        (heads,), (blocks,), (blocks,), (heads,),
        (units, 2), (units, 2), (units,), (units,), (units,), (units,),
        (units, steps), (units, steps), (units, steps), (units, steps),
        (units,), (units,), (units,), (units,), (planes + 2,), (planes + 2,), (2,),
    ]
    scratch += [dma(shape) for shape in sems] + [pltpu.SemaphoreType.REGULAR]
    result, input_grad, table, g_qkv, g_out, g_up, g_down = pl.pallas_call(
        functools.partial(layer_kernel, blocks, heads),
        out_shape=[
            jax.ShapeDtypeStruct((rows, width), high),
            jax.ShapeDtypeStruct((rows, width), high),
            jax.ShapeDtypeStruct((2 * blocks, 8, width), high),
        ]
        + [jax.ShapeDtypeStruct(w.shape, high) for w in (w_qkv, w_out, w_up, w_down)],
        in_specs=[vmem] * 4 + [hbm] * 5,
        out_specs=[vmem] * 3 + [hbm] * 4,
        scratch_shapes=scratch,
        compiler_params=pltpu.CompilerParams(
            collective_id=1, has_side_effects=True, vmem_limit_bytes=VMEM_LIMIT
        ),
    )(tokens[0], cotangent[0], emb_rows, jnp.asarray(rope_constants(blocks)),
      w_ada, w_qkv, w_out, w_up, w_down)
    shard_width = width // 2
    embedded_part = lax.dynamic_slice_in_dim(
        table[:, 4], lax.axis_index("fsdp") * shard_width, shard_width, 1
    )
    ada_total = lax.dot_general(
        embedded_part, table[:, :4].reshape(2 * blocks, 4 * width), (((0,), (0,)), ((), ())),
        precision=lax.Precision.HIGHEST,
    )
    return (result[None], input_grad[None], g_qkv, g_out, g_up, g_down, ada_total)


def solution(mesh):
    chosen = fast_device if mesh.shape["ctx"] == 16 else on_device
    return jax.shard_map(
        chosen,
        mesh=mesh,
        in_specs=(
            P("fsdp", "ctx", None),
            P("fsdp", "ctx"),
            P(),
            P("fsdp", None),
            P("fsdp", None),
            P("fsdp", None),
            P("fsdp", None),
            P("fsdp", None),
            P("fsdp", "ctx", None),
        ),
        out_specs=(
            P("fsdp", "ctx", None),
            P("fsdp", "ctx", None),
            P("fsdp", None),
            P("fsdp", None),
            P("fsdp", None),
            P("fsdp", None),
            P("fsdp", None),
        ),
        check_vma=False,
    )
```

```python
import functools
import math

import jax
import jax.numpy as jnp
import numpy as np
from jax import lax
from jax.experimental import pallas as pl
from jax.experimental.pallas import tpu as pltpu
from jax.sharding import PartitionSpec as P

HD = 64
BLOCK = 256
VMEM_LIMIT = 62 * 1024 * 1024
MESH = pl.DeviceIdType.MESH


norm_eps = 1e-06
masked_score = -1e30
rope_base = 10000.0


def layer_norm(values):
    center = values - jnp.mean(values, axis=-1, keepdims=True)
    inverse = lax.rsqrt(jnp.mean(center * center, axis=-1, keepdims=True) + norm_eps)
    return (center * inverse, inverse)


def norm_back(grad_norm, normed, inverse):
    mean_grad = jnp.mean(grad_norm, axis=-1, keepdims=True)
    mean_cross = jnp.mean(grad_norm * normed, axis=-1, keepdims=True)
    return inverse * (grad_norm - mean_grad - normed * mean_cross)


def rope_tables(positions, head_size):
    half_size = head_size // 2
    frequency = jnp.exp(
        jnp.arange(half_size, dtype=jnp.float32) * (-2.0 * math.log(rope_base) / head_size)
    )
    angles = positions.astype(jnp.float32)[:, None] * frequency[None, :]
    cosine_table = jnp.concatenate([jnp.cos(angles), jnp.cos(angles)], axis=-1)[:, None, :]
    sine_table = jnp.concatenate([jnp.sin(angles), jnp.sin(angles)], axis=-1)[:, None, :]
    return (cosine_table, sine_table)


def rotate_half(values):
    middle = values.shape[-1] // 2
    return jnp.concatenate([-values[..., middle:], values[..., :middle]], axis=-1)


def rotate(values, cosine_table, sine_table):
    return values * cosine_table + rotate_half(values) * sine_table


def rotate_back(gradient, cosine_table, sine_table):
    return gradient * cosine_table - rotate_half(gradient * sine_table)


def gelu_tanh(values):
    return jax.nn.gelu(values, approximate=True)


def split_rows(array, sub_rows):
    return array.reshape((array.shape[0] // sub_rows, sub_rows) + array.shape[1:])


def part_starts(total_rows, sub_rows):
    return sub_rows * jnp.arange(total_rows // sub_rows, dtype=jnp.int32)


def keep_same(partial_value):
    return partial_value


def attend_forward(partial_value, pieces, queries, query_block, score_scale):
    key_rows, value_rows = pieces
    sub_rows = queries.shape[0]

    def attend_visit(running, scan_item):
        key_part, value_part, part_start = scan_item

        def attend_update(running):
            running_max, running_sum, running_out = running
            key_block = (part_start + jnp.arange(sub_rows, dtype=jnp.int32)) // BLOCK
            allowed = (key_block[None, :] <= query_block[:, None])[None]
            scores = (
                jnp.einsum("qhd,khd->hqk", queries, key_part, preferred_element_type=jnp.float32)
                * score_scale
            )
            scores = jnp.where(allowed, scores, masked_score)
            new_max = jnp.maximum(running_max, jnp.max(scores, axis=-1))
            weights = jnp.where(allowed, jnp.exp(scores - new_max[..., None]), 0.0)
            decay = jnp.exp(running_max - new_max)
            running_sum = running_sum * decay + jnp.sum(weights, axis=-1)
            running_out = running_out * decay[..., None] + jnp.einsum(
                "hqk,khd->hqd",
                weights.astype(jnp.bfloat16),
                value_part,
                preferred_element_type=jnp.float32,
            )
            return (new_max, running_sum, running_out)

        return (
            lax.cond(part_start // BLOCK <= query_block[-1], attend_update, keep_same, running),
            None,
        )

    partial_value, unused = lax.scan(
        attend_visit,
        partial_value,
        (
            split_rows(key_rows, sub_rows),
            split_rows(value_rows, sub_rows),
            part_starts(key_rows.shape[0], sub_rows),
        ),
    )
    return partial_value


def on_device(tokens, timestep, time_table, w_qkv, w_out, w_up, w_down, w_ada, cotangent):
    tok_rows = tokens.shape[1]
    model_width = tokens.shape[2]
    heads = model_width // HD
    score_scale = 1.0 / math.sqrt(HD)
    highest_precision = lax.Precision.HIGHEST
    full_weights = (
        lax.all_gather(w_qkv, "fsdp", axis=0, tiled=True),
        lax.all_gather(w_out, "fsdp", axis=0, tiled=True),
        lax.all_gather(w_up, "fsdp", axis=0, tiled=True),
        lax.all_gather(w_down, "fsdp", axis=0, tiled=True),
        lax.all_gather(w_ada, "fsdp", axis=0, tiled=True),
    )
    qkv_full, out_full, up_full, down_full, ada_full = full_weights
    steps_onehot = (
        timestep[0][:, None] == jnp.arange(time_table.shape[0], dtype=jnp.int32)[None, :]
    ).astype(jnp.float32)
    embedded = jnp.dot(steps_onehot, time_table, precision=highest_precision).astype(jnp.bfloat16)
    modulation = jnp.dot(embedded, ada_full, preferred_element_type=jnp.float32)
    per_token = jnp.repeat(modulation, BLOCK, axis=0)
    scale_attn, gate_attn, scale_mlp, gate_mlp = jnp.split(per_token, 4, axis=1)
    inputs = tokens[0].astype(jnp.float32)
    normed_one, inverse_one = layer_norm(inputs)
    residual_first = (normed_one * (1.0 + scale_attn)).astype(jnp.bfloat16)
    projected_output = jnp.dot(
        residual_first, qkv_full, preferred_element_type=jnp.float32
    ).reshape(tok_rows, 3, heads, HD)
    positions = lax.axis_index("ctx") * tok_rows + jnp.arange(tok_rows, dtype=jnp.int32)
    cosine_table, sine_table = rope_tables(positions, HD)
    queries = rotate(projected_output[:, 0], cosine_table, sine_table).astype(jnp.bfloat16)
    key_own = rotate(projected_output[:, 1], cosine_table, sine_table).astype(jnp.bfloat16)
    value_own = projected_output[:, 2].astype(jnp.bfloat16)
    query_block = positions // BLOCK
    start_state = (
        jnp.full((heads, tok_rows), masked_score, jnp.float32),
        jnp.zeros((heads, tok_rows), jnp.float32),
        jnp.zeros((heads, tok_rows, HD), jnp.float32),
    )
    running_max, running_sum, running_out = attend_forward(
        start_state,
        (
            lax.all_gather(key_own, "ctx", axis=0, tiled=True),
            lax.all_gather(value_own, "ctx", axis=0, tiled=True),
        ),
        queries,
        query_block,
        score_scale,
    )
    attn_rows = jnp.transpose(running_out / running_sum[..., None], (1, 0, 2))
    query_lse = running_max + jnp.log(running_sum)
    attn_low = attn_rows.reshape(tok_rows, model_width).astype(jnp.bfloat16)
    attention_projected = jnp.dot(attn_low, out_full, preferred_element_type=jnp.float32)
    middle = inputs + gate_attn * attention_projected
    normed_two, inverse_two = layer_norm(middle)
    residual_second = (normed_two * (1.0 + scale_mlp)).astype(jnp.bfloat16)
    before_activation = jnp.dot(residual_second, up_full, preferred_element_type=jnp.float32)
    gelu_activated, gelu_back = jax.vjp(gelu_tanh, before_activation)
    act_low = gelu_activated.astype(jnp.bfloat16)
    feedforward_output = jnp.dot(act_low, down_full, preferred_element_type=jnp.float32)
    result = middle + gate_mlp * feedforward_output
    qkv_back, out_back, up_back, down_back = (
        lax.all_gather(w_qkv, "fsdp", axis=0, tiled=True),
        lax.all_gather(w_out, "fsdp", axis=0, tiled=True),
        lax.all_gather(w_up, "fsdp", axis=0, tiled=True),
        lax.all_gather(w_down, "fsdp", axis=0, tiled=True),
    )
    upstream = cotangent[0].astype(jnp.float32)
    grad_gate_mlp = upstream * feedforward_output
    grad_mlp = (upstream * gate_mlp).astype(jnp.bfloat16)
    grad_down = jnp.einsum("tf,td->fd", act_low, grad_mlp, preferred_element_type=jnp.float32)
    grad_act = jnp.einsum("td,fd->tf", grad_mlp, down_back, preferred_element_type=jnp.float32)
    grad_pre = gelu_back(grad_act)[0].astype(jnp.bfloat16)
    grad_up = jnp.einsum("td,tf->df", residual_second, grad_pre, preferred_element_type=jnp.float32)
    grad_hidden_two = jnp.einsum("tf,df->td", grad_pre, up_back, preferred_element_type=jnp.float32)
    grad_scale_mlp = grad_hidden_two * normed_two
    grad_middle = upstream + norm_back(grad_hidden_two * (1.0 + scale_mlp), normed_two, inverse_two)
    grad_gate_attn = grad_middle * attention_projected
    grad_attn_proj = (grad_middle * gate_attn).astype(jnp.bfloat16)
    grad_out = jnp.einsum("td,te->de", attn_low, grad_attn_proj, preferred_element_type=jnp.float32)
    grad_attended = jnp.einsum(
        "te,de->td", grad_attn_proj, out_back, preferred_element_type=jnp.float32
    )
    grad_heads = grad_attended.astype(jnp.bfloat16).reshape(tok_rows, heads, HD)
    delta_rows = jnp.sum(grad_heads.astype(jnp.float32) * attn_rows, axis=-1)
    query_delta = jnp.transpose(delta_rows)
    lse_rows = jnp.transpose(query_lse)
    lse_high = lse_rows.astype(jnp.bfloat16)
    lse_rest = (lse_rows - lse_high.astype(jnp.float32)).astype(jnp.bfloat16)
    delta_high = delta_rows.astype(jnp.bfloat16)
    delta_rest = (delta_rows - delta_high.astype(jnp.float32)).astype(jnp.bfloat16)
    stat_rows = jnp.concatenate([lse_high, lse_rest, delta_high, delta_rest], axis=1)
    zero_heads = jnp.zeros((tok_rows, heads, HD), jnp.float32)
    partial_value = (zero_heads, zero_heads, zero_heads)
    grad_query = partial_value[0]
    key_rows = lax.all_gather(key_own, "ctx", axis=0, tiled=True)

    def query_visit(partial_value, scan_item):
        key_part, value_part, part_start = scan_item

        def query_update(partial_value):
            key_block = (part_start + jnp.arange(tok_rows, dtype=jnp.int32)) // BLOCK
            allowed = (key_block[None, :] <= query_block[:, None])[None]
            scores = (
                jnp.einsum("qhd,khd->hqk", queries, key_part, preferred_element_type=jnp.float32)
                * score_scale
            )
            probs = jnp.where(allowed, jnp.exp(scores - query_lse[..., None]), 0.0)
            grad_prob = jnp.einsum(
                "qhd,khd->hqk", grad_heads, value_part, preferred_element_type=jnp.float32
            )
            grad_score = (probs * (grad_prob - query_delta[..., None]) * score_scale).astype(
                jnp.bfloat16
            )
            return partial_value + jnp.einsum(
                "hqk,khd->qhd", grad_score, key_part, preferred_element_type=jnp.float32
            )

        return (
            lax.cond(
                part_start // BLOCK <= query_block[-1], query_update, keep_same, partial_value
            ),
            None,
        )

    grad_query, unused = lax.scan(
        query_visit,
        grad_query,
        (
            split_rows(key_rows, tok_rows),
            split_rows(lax.all_gather(value_own, "ctx", axis=0, tiled=True), tok_rows),
            part_starts(key_rows.shape[0], tok_rows),
        ),
    )
    key_partial_value = (partial_value[1], partial_value[2])
    query_rows = lax.all_gather(queries, "ctx", axis=0, tiled=True)

    def key_visit(running, scan_item):
        query_part, dout_part, stat_part, part_start = scan_item

        def key_update(running):
            grad_key, grad_value = running
            query_blk = (part_start + jnp.arange(tok_rows, dtype=jnp.int32)) // BLOCK
            allowed = (query_blk[:, None] >= query_block[None, :])[None]
            stat_float = stat_part.astype(jnp.float32)
            lse_part = jnp.transpose(stat_float[:, :heads] + stat_float[:, heads : 2 * heads])
            delta_part = jnp.transpose(
                stat_float[:, 2 * heads : 3 * heads] + stat_float[:, 3 * heads :]
            )
            scores = (
                jnp.einsum("qhd,khd->hqk", query_part, key_own, preferred_element_type=jnp.float32)
                * score_scale
            )
            probs = jnp.where(allowed, jnp.exp(scores - lse_part[..., None]), 0.0)
            grad_value = grad_value + jnp.einsum(
                "hqk,qhd->khd",
                probs.astype(jnp.bfloat16),
                dout_part,
                preferred_element_type=jnp.float32,
            )
            grad_prob = jnp.einsum(
                "qhd,khd->hqk", dout_part, value_own, preferred_element_type=jnp.float32
            )
            grad_score = (probs * (grad_prob - delta_part[..., None]) * score_scale).astype(
                jnp.bfloat16
            )
            grad_key = grad_key + jnp.einsum(
                "hqk,qhd->khd", grad_score, query_part, preferred_element_type=jnp.float32
            )
            return (grad_key, grad_value)

        last_seen = (part_start + tok_rows - 1) // BLOCK
        return (lax.cond(last_seen >= query_block[0], key_update, keep_same, running), None)

    key_partial_value, unused = lax.scan(
        key_visit,
        key_partial_value,
        (
            split_rows(query_rows, tok_rows),
            split_rows(lax.all_gather(grad_heads, "ctx", axis=0, tiled=True), tok_rows),
            split_rows(lax.all_gather(stat_rows, "ctx", axis=0, tiled=True), tok_rows),
            part_starts(query_rows.shape[0], tok_rows),
        ),
    )
    grad_key, grad_value = key_partial_value
    grad_query, grad_key, grad_value = (grad_query, grad_key, grad_value)
    grad_query = rotate_back(grad_query, cosine_table, sine_table)
    grad_key = rotate_back(grad_key, cosine_table, sine_table)
    grad_projected = (
        jnp.stack([grad_query, grad_key, grad_value], axis=1)
        .reshape(tok_rows, 3 * model_width)
        .astype(jnp.bfloat16)
    )
    grad_qkv = jnp.einsum(
        "td,te->de", residual_first, grad_projected, preferred_element_type=jnp.float32
    )
    grad_hidden_one = jnp.einsum(
        "te,de->td", grad_projected, qkv_back, preferred_element_type=jnp.float32
    )
    grad_scale_attn = grad_hidden_one * normed_one
    input_grad = grad_middle + norm_back(
        grad_hidden_one * (1.0 + scale_attn), normed_one, inverse_one
    )
    grad_modulation = jnp.concatenate(
        [grad_scale_attn, grad_gate_attn, grad_scale_mlp, grad_gate_mlp], axis=1
    )
    grad_blocks = jnp.sum(
        grad_modulation.reshape(tok_rows // BLOCK, BLOCK, 4 * model_width), axis=1
    )
    embedded_float = embedded.astype(jnp.float32)
    halves = (
        lax.psum_scatter(
            grad_qkv.astype(jnp.bfloat16), "fsdp", scatter_dimension=0, tiled=True
        ).astype(jnp.float32),
        lax.psum_scatter(
            grad_out.astype(jnp.bfloat16), "fsdp", scatter_dimension=0, tiled=True
        ).astype(jnp.float32),
        lax.psum_scatter(
            grad_up.astype(jnp.bfloat16), "fsdp", scatter_dimension=0, tiled=True
        ).astype(jnp.float32),
        lax.psum_scatter(
            grad_down.astype(jnp.bfloat16), "fsdp", scatter_dimension=0, tiled=True
        ).astype(jnp.float32),
    )
    totals = lax.psum((halves[0], halves[1], halves[2], halves[3]), "ctx")
    all_embedded, all_blocks = (
        lax.all_gather(embedded_float, ("ctx", "fsdp"), axis=0, tiled=True),
        lax.all_gather(grad_blocks, ("ctx", "fsdp"), axis=0, tiled=True),
    )
    shard_width = model_width // lax.axis_size("fsdp")
    row_start = lax.axis_index("fsdp") * shard_width
    embedded_part = lax.dynamic_slice_in_dim(all_embedded, row_start, shard_width, 1)
    ada_total = jnp.dot(jnp.transpose(embedded_part), all_blocks, precision=highest_precision)
    return (result[None], input_grad[None], totals[0], totals[1], totals[2], totals[3], ada_total)


def remote(source, target, send_sem, recv_sem, **where):
    return pltpu.make_async_remote_copy(
        src_ref=source,
        dst_ref=target,
        send_sem=send_sem,
        recv_sem=recv_sem,
        device_id=where,
        device_id_type=MESH,
    )


def landed(ref, sem):
    pltpu.make_async_copy(ref, ref, sem).wait()


def head_place(me):
    plane = me // 4
    spot = lax.rem(me, 4)
    odd = lax.rem(plane, 2)
    idle = 3 - 2 * odd
    head = 3 * plane + spot - odd * (spot // 2)
    return spot != idle, head


def head_owner(head):
    plane = head // 3
    rank = lax.rem(head, 3)
    odd = lax.rem(plane, 2)
    return 4 * plane + rank + odd * ((rank + 1) // 2)


def scatter_sent(me, heads, source, target, send_sem, recv_sem):
    def finish(head, carry):
        owner = head_owner(head)

        @pl.when(owner != me)
        def _():
            remote(
                source.at[head], target.at[me], send_sem.at[head], recv_sem.at[me], ctx=owner
            ).wait_send()

        return carry

    lax.fori_loop(0, heads, finish, 0)


def return_block(me, head, block, source, target, send_sem, recv_sem):
    @pl.when(block != me)
    def _():
        remote(
            source.at[block], target.at[head], send_sem.at[block], recv_sem.at[head], ctx=block
        ).start()

    @pl.when(block == me)
    def _():
        pltpu.make_async_copy(source.at[block], target.at[head], recv_sem.at[head]).start()


def return_sent(me, head, blocks, source, target, send_sem, recv_sem):
    def finish(block, carry):
        @pl.when(block != me)
        def _():
            remote(
                source.at[block], target.at[head], send_sem.at[block], recv_sem.at[head], ctx=block
            ).wait_send()

        return carry

    lax.fori_loop(0, blocks, finish, 0)


def wait_heads(heads, target, recv_sem):
    def finish(head, carry):
        landed(target.at[head], recv_sem.at[head])
        return carry

    lax.fori_loop(0, heads, finish, 0)


def transposed(values):
    return jnp.transpose(values.astype(jnp.float32)).astype(values.dtype)


def add_into(target, left, right, rows):
    step = 48

    def body(index, carry):
        spot = pl.ds(pl.multiple_of(index * step, step), step)
        total = left(spot).astype(jnp.float32) + right(spot).astype(jnp.float32)
        target(spot, total.astype(jnp.bfloat16))
        return carry

    lax.fori_loop(0, rows // step, body, 0)


def product(left, right):
    return jnp.dot(left, right, preferred_element_type=jnp.float32)


def product_back(left, right):
    return lax.dot_general(
        left, right, (((1,), (1,)), ((), ())), preferred_element_type=jnp.float32
    )


def layer_kernel(
    blocks, heads,
    tok_ref, cot_ref, emb_ref, rope_ref, ada_hbm, qkv_hbm, out_hbm, up_hbm, down_hbm,
    result_ref, ingrad_ref, eds_ref, sds_ref, og_qkv, og_out, og_up, og_down,
    wq, wo, wu, wd, mod_ref, emb_other, part_other, part_send,
    hid1_t, mid_ref, ap_ref, sums_ref, cos_ref, sin_ref,
    qs_ref, buf_ref, mix_ref, lse_ref, att_ref, douts_ref, got_ref,
    parts, sib_ref, row_ref, x_ref, z_ref, res_ref, table_ref,
    own_sem, small_send, small_recv, w_send, w_recv,
    fs, fr, fbs, fbr, bs, br, bbs, bbr,
    s_sib, r_sib, s_row, r_row, s_x, r_x, s_z, r_z, s_az, r_az, s_ax, r_ax, s_as, r_as,
    s_t, r_t, out_sem, free_sem,
):
    me = lax.axis_index("ctx")
    row = lax.axis_index("fsdp")
    other = 1 - row
    piece = lax.rem(me, 4)
    core = lax.rem(me, 2)
    xbit = lax.rem(me // 2, 2)
    plane = me // 4
    planes = blocks // 4
    chip_next = jnp.bitwise_xor(me, 2)
    sibling = jnp.bitwise_xor(me, 1)
    gland_ref = qs_ref
    owner, head = head_place(me)
    width = tok_ref.shape[1]
    score_scale = 1.0 / math.sqrt(HD)

    barrier = pltpu.get_barrier_semaphore()
    pl.semaphore_signal(barrier, inc=1, device_id={"fsdp": other}, device_id_type=MESH)

    def greet(step, carry):
        pl.semaphore_signal(
            barrier, inc=1, device_id={"ctx": lax.rem(me + step, blocks)}, device_id_type=MESH
        )
        return carry

    lax.fori_loop(1, blocks, greet, 0)
    pl.semaphore_wait(barrier, blocks)

    shards = (qkv_hbm, out_hbm, up_hbm, down_hbm)
    wholes = (wq, wo, wu, wd)
    quarter_rows = [shard.shape[0] // 4 for shard in shards]
    third = quarter_rows[0] // 3
    chunks = [
        (0, 0, third),
        (0, third, third),
        (0, 2 * third, third),
        (1, 0, quarter_rows[1]),
        (2, 0, quarter_rows[2]),
        (3, 0, 2 * quarter_rows[3]),
    ]

    def chunk_start(index, half, which):
        weight, first, count = chunks[index]
        if index == 5:
            return pl.multiple_of(half * 2 * count + lax.rem(which, 2) * count, 16)
        return pl.multiple_of((half * 4 + which) * quarter_rows[weight] + first, 16)

    def chunk_ref(index, which):
        weight, first, count = chunks[index]
        return wholes[weight].at[pl.ds(chunk_start(index, other, which), count)]

    def y_copy(index):
        weight, first, count = chunks[index]
        return remote(
            shards[weight].at[pl.ds(chunk_start(index, 0, piece), count)],
            wholes[weight].at[pl.ds(chunk_start(index, row, piece), count)],
            w_send.at[index, 0], w_recv.at[index, 0], fsdp=other,
        )

    def onward(index, which, slot, peer):
        ref = chunk_ref(index, which)
        return remote(ref, ref, w_send.at[index, slot], w_recv.at[index, slot], ctx=peer)

    def pass_on(index):
        landed(chunk_ref(index, piece), w_recv.at[index, 0])
        if index < 5:
            onward(index, piece, 1, chip_next).start()
        onward(index, piece, 2, sibling).start()

    def pass_last(index):
        across = jnp.bitwise_xor(piece, 2)
        landed(chunk_ref(index, across), w_recv.at[index, 1])
        onward(index, across, 3, sibling).start()

    def chunk_done(index):
        landed(chunk_ref(index, jnp.bitwise_xor(piece, 1)), w_recv.at[index, 2])
        if index < 5:
            landed(chunk_ref(index, jnp.bitwise_xor(piece, 3)), w_recv.at[index, 3])

    def chunk_sent(index):
        y_copy(index).wait_send()
        onward(index, piece, 2, sibling).wait_send()
        if index < 5:
            onward(index, piece, 1, chip_next).wait_send()
            onward(index, jnp.bitwise_xor(piece, 2), 3, sibling).wait_send()

    def own_copy(weight):
        half = shards[weight].shape[0]
        start = pl.multiple_of(row * half, 16)
        return pltpu.make_async_copy(
            shards[weight], wholes[weight].at[pl.ds(start, half)], own_sem.at[weight]
        )

    emb_copy = remote(emb_ref, emb_other, small_send.at[0], small_recv.at[0], fsdp=other)
    emb_copy.start()
    for index in range(5):
        y_copy(index).start()

    def opening(ada_ref, hid1):
        ada_copy = pltpu.make_async_copy(ada_hbm, ada_ref, own_sem.at[4])
        ada_copy.start()
        for weight in range(4):
            own_copy(weight).start()
        normed, unused = layer_norm(tok_ref[...].astype(jnp.float32))
        ingrad_ref[...] = normed
        half_width = width // 2
        cols = pl.ds(pl.multiple_of(row * half_width, 128), half_width)
        ada_copy.wait()
        emb_copy.wait()
        both = jnp.concatenate([emb_ref[:, cols], emb_other[:, cols]], axis=0)
        partial = product(both.astype(jnp.bfloat16), ada_ref[...])
        mod_ref[...] = partial[:8]
        part_send[...] = partial[8:]
        part_copy = remote(part_send, part_other, small_send.at[1], small_recv.at[1], fsdp=other)
        part_copy.start()
        pass_on(0)
        lanes = lax.broadcasted_iota(jnp.int32, (HD // 2, 128), 1)
        pick = lanes == me
        cos_block = jnp.sum(
            jnp.where(pick, rope_ref[:, 2 * BLOCK : 2 * BLOCK + 128], 0.0), axis=1, keepdims=True
        )
        sin_block = jnp.sum(
            jnp.where(pick, rope_ref[:, 2 * BLOCK + 128 :], 0.0), axis=1, keepdims=True
        )
        cos_row = rope_ref[:, :BLOCK]
        sin_row = rope_ref[:, BLOCK : 2 * BLOCK]
        cos_ref[...] = cos_row * cos_block - sin_row * sin_block
        sin_ref[...] = sin_row * cos_block + cos_row * sin_block
        part_copy.wait()
        mod_ref[...] += part_other[...]
        low = (ingrad_ref[...] * (1.0 + mod_ref[:1, :width])).astype(jnp.bfloat16)
        hid1[...] = low
        pass_on(1)
        hid1_t[...] = transposed(low)
        pass_on(2)
        for index in range(3):
            pass_last(index)
        own_copy(0).wait()
        for index in range(3):
            chunk_done(index)

        def project(group, carry):
            spans = []
            for kind in range(3):
                cols = pl.ds(pl.multiple_of(kind * width + group * 4 * HD, 4 * HD), 4 * HD)
                spans.append(jnp.transpose(product(hid1[...], wq[:, cols])))
            cos, sin = cos_ref[...], sin_ref[...]
            for inner in range(4):
                which = group * 4 + inner
                for kind in range(2):
                    top = spans[kind][inner * HD : inner * HD + HD // 2]
                    low_half = spans[kind][inner * HD + HD // 2 : (inner + 1) * HD]
                    turned = jnp.concatenate(
                        [top * cos - low_half * sin, low_half * cos + top * sin], axis=0
                    ).astype(jnp.bfloat16)
                    if kind == 0:
                        turned = turned * jnp.bfloat16(score_scale)
                    qs_ref[which, kind * HD : (kind + 1) * HD, :] = turned
                qs_ref[which, 2 * HD :, :] = spans[2][inner * HD : (inner + 1) * HD].astype(
                    jnp.bfloat16
                )
            return carry

        lax.fori_loop(0, heads // 4, project, 0)

        def send_block(step, carry):
            send_head(lax.rem(step + 3 * (plane + 2), heads), qs_ref, buf_ref, fs, fr)
            return carry

        lax.fori_loop(0, heads, send_block, 0)
        y_copy(5).start()
        pass_on(3)

    def send_head(which, source, target, send_sem, recv_sem):
        goal = head_owner(which)

        @pl.when(goal != me)
        def _():
            remote(
                source.at[which], target.at[me], send_sem.at[which], recv_sem.at[me], ctx=goal
            ).start()

        @pl.when(goal == me)
        def _():
            pltpu.make_async_copy(source.at[which], target.at[me], recv_sem.at[me]).start()

    pl.run_scoped(
        opening,
        pltpu.VMEM((width // 2, 4 * width), jnp.bfloat16),
        pltpu.VMEM((BLOCK, width), jnp.bfloat16),
    )

    def forward(pair_ref, low_ref):
        def value_of(key):
            ones = jnp.ones((16, BLOCK), jnp.bfloat16)
            return jnp.concatenate([buf_ref[key, 2 * HD :, :], ones], axis=0)

        def attend(group):
            first = 4 * group
            for inner in range(4):
                block = first + inner
                landed(buf_ref.at[block], fr.at[block])
                rows = pl.ds(pl.multiple_of(block * BLOCK, BLOCK), BLOCK)
                pair_ref[rows, :] = transposed(buf_ref[block, HD:, :])
            query = side_by_side(lambda block: buf_ref[block, :HD, :], first)
            query = jnp.concatenate([query, jnp.zeros_like(query)], axis=0)

            def step(state, key, count, skip):
                high, mixed = state
                rows = pl.ds(pl.multiple_of(key * BLOCK, BLOCK), count * BLOCK)
                begin = (skip or 0) * BLOCK
                scores = product(pair_ref[rows, :], query[:, begin:])
                if skip is not None:
                    scores = jnp.where(seen(scores.shape), scores, masked_score)
                new_high = jnp.maximum(high[:, begin:], jnp.max(scores, axis=0, keepdims=True))
                weights = jnp.exp(scores - new_high).astype(jnp.bfloat16)
                values = jnp.concatenate([value_of(key + index) for index in range(count)], axis=1)
                new_mixed = mixed[:, begin:] * jnp.exp(high[:, begin:] - new_high) + product(
                    values, weights
                )
                if begin:
                    new_high = jnp.concatenate([high[:, :begin], new_high], axis=1)
                    new_mixed = jnp.concatenate([mixed[:, :begin], new_mixed], axis=1)
                return new_high, new_mixed

            state = (
                jnp.full((1, 4 * BLOCK), masked_score, jnp.float32),
                jnp.zeros((HD + 16, 4 * BLOCK), jnp.float32),
            )
            state = lax.fori_loop(
                0, group, lambda index, now: step(now, 4 * index, 4, None), state
            )
            state = step(state, first, 2, 0)
            high, mixed = step(state, first + 2, 2, 2)
            total = mixed[HD : HD + 1]
            mixed = mixed[:HD] / total
            lse = high + jnp.log(total)
            for inner in range(4):
                block = first + inner
                cols = slice(inner * BLOCK, (inner + 1) * BLOCK)
                mix_ref[block] = mixed[:, cols]
                low_ref[block] = mixed[:, cols].astype(jnp.bfloat16)
                lse_ref[block] = jnp.broadcast_to(lse[:, cols], (8, BLOCK))
                return_block(me, head, block, low_ref, att_ref, fbs, fbr)

        def visit(group, carry):
            @pl.when(owner)
            def _():
                attend(group)

            for when, event in FORWARD_EVENTS:
                @pl.when(group == when)
                def _(event=event):
                    (pass_on, pass_last)[event[0]](event[1])

            return carry

        lax.fori_loop(0, blocks // 4, visit, 0)

        @pl.when(owner)
        def _():
            return_sent(me, head, blocks, low_ref, att_ref, fbs, fbr)

        scatter_sent(me, heads, qs_ref, buf_ref, fs, fr)
        wait_heads(heads, att_ref, fbr)

    pl.run_scoped(
        forward,
        pltpu.VMEM((blocks * BLOCK, 2 * HD), jnp.bfloat16),
        pltpu.VMEM((blocks, HD, BLOCK), jnp.bfloat16),
    )

    span = width // 2
    mine = pl.ds(pl.multiple_of(core * span, 128), span)
    theirs = pl.ds(pl.multiple_of((1 - core) * span, 128), span)
    deep = width // 2
    half_deep = deep // 2
    small = half_deep // planes

    def part_of(unit, half, cols):
        return parts.at[unit, half, :, cols]

    def qkv_part(unit, half, cols):
        return wd.at[pl.ds(pl.multiple_of(((unit - 9) * 2 + half) * deep, 16), deep), cols]

    def sib_of(unit, half):
        return sib_ref.at[unit, half]

    def qkv_sib(unit, half):
        cols = pl.ds(pl.multiple_of(((unit - 9) * 2 + half) * span, 128), span)
        return wu.at[pl.ds(0, deep), cols]

    def pipeline(part, sib):
        def to_sibling(unit):
            return [
                remote(part(unit, half, theirs), sib(unit, half),
                       s_sib.at[unit, half], r_sib.at[unit, half], ctx=sibling)
                for half in range(2)
            ]

        def to_row(unit):
            return [remote(sib(unit, other), row_ref.at[unit],
                           s_row.at[unit], r_row.at[unit], fsdp=other)]

        def to_x(unit):
            rows = pl.ds(pl.multiple_of((1 - xbit) * half_deep, 16), half_deep)
            return [remote(row_ref.at[unit, rows], x_ref.at[unit],
                           s_x.at[unit], r_x.at[unit], ctx=chip_next)]

        def to_z(unit):
            copies = []
            for step in range(1, planes):
                goal = lax.rem(plane + step, planes)
                rows = pl.ds(pl.multiple_of(goal * small, 16), small)
                copies.append(
                    remote(x_ref.at[unit, rows], z_ref.at[unit, step - 1],
                           s_z.at[unit, step - 1], r_z.at[unit, step - 1], ctx=4 * goal + piece)
                )
            return copies

        def slab(unit, which):
            rows = pl.ds(pl.multiple_of(xbit * half_deep + which * small, 16), small)
            return res_ref.at[unit, rows, mine]

        def along_z(unit):
            return [
                remote(slab(unit, plane), slab(unit, plane),
                       s_az.at[unit, step - 1], r_az.at[unit, step - 1],
                       ctx=4 * lax.rem(plane + step, planes) + piece)
                for step in range(1, planes)
            ]

        def along_x(unit):
            rows = pl.ds(pl.multiple_of(xbit * half_deep, 16), half_deep)
            ref = res_ref.at[unit, rows, mine]
            return [remote(ref, ref, s_ax.at[unit], r_ax.at[unit], ctx=chip_next)]

        def along_s(unit):
            ref = res_ref.at[unit, :, mine]
            return [remote(ref, ref, s_as.at[unit], r_as.at[unit], ctx=sibling)]

        def launch(copies):
            for copy in copies:
                copy.start()

        def write_out(unit, which, cols):
            side = core if which == 0 else 1 - core
            kind = lax.rem(unit, 4)
            order = 2 * (unit // 4) + lax.rem(kind, 2)

            def save(target):
                pltpu.make_async_copy(
                    res_ref.at[unit, :, cols], target, out_sem.at[unit, which]
                ).start()

            @pl.when((unit < 8) & (kind < 2))
            def _():
                save(og_down.at[pl.ds(pl.multiple_of(order * deep, 16), deep),
                                pl.ds(pl.multiple_of(side * span, 128), span)])

            @pl.when((unit < 8) & (kind >= 2))
            def _():
                start = side * 4 * span + order * span
                save(og_up.at[:, pl.ds(pl.multiple_of(start, 128), span)])

            @pl.when(unit == 8)
            def _():
                save(og_out.at[:, pl.ds(pl.multiple_of(side * span, 128), span)])

            @pl.when(unit > 8)
            def _():
                start = (unit - 9) * width + side * span
                save(og_qkv.at[:, pl.ds(pl.multiple_of(start, 128), span)])

        def stage0(unit):
            launch(to_sibling(unit))

        def stage1(unit):
            for half in range(2):
                landed(sib(unit, half), r_sib.at[unit, half])
                ref, part_ref = sib(unit, half), part(unit, half, mine)

                def put(spot, value, ref=ref):
                    ref[spot, :] = value

                add_into(put, lambda spot, ref=ref: ref[spot, :],
                         lambda spot, part_ref=part_ref: part_ref[spot, :], deep)
            launch(to_row(unit))

        def stage2(unit):
            landed(row_ref.at[unit], r_row.at[unit])
            ref = sib(unit, row)

            def put(spot, value):
                row_ref[unit, spot, :] = value

            add_into(put, lambda spot: row_ref[unit, spot, :], lambda spot: ref[spot, :], deep)
            launch(to_x(unit))
            for make in (to_sibling, to_row):
                for copy in make(unit):
                    copy.wait_send()

        def stage3(unit):
            landed(x_ref.at[unit], r_x.at[unit])
            ref = row_ref.at[unit, pl.ds(pl.multiple_of(xbit * half_deep, 16), half_deep)]

            def put(spot, value):
                x_ref[unit, spot, :] = value

            add_into(put, lambda spot: x_ref[unit, spot, :], lambda spot: ref[spot, :], half_deep)
            launch(to_z(unit))

        def stage4(unit):
            rows = pl.ds(pl.multiple_of(plane * small, 16), small)
            total = x_ref[unit, rows, :].astype(jnp.float32)
            for step in range(1, planes):
                landed(z_ref.at[unit, step - 1], r_z.at[unit, step - 1])
                total += z_ref[unit, step - 1].astype(jnp.float32)
            spots = pl.ds(pl.multiple_of(xbit * half_deep + plane * small, 16), small)
            res_ref[unit, spots, mine] = total.astype(jnp.bfloat16)
            launch(along_z(unit))

        def stage5(unit):
            for step in range(1, planes):
                landed(slab(unit, lax.rem(plane + planes - step, planes)), r_az.at[unit, step - 1])
            launch(along_x(unit))

        def stage6(unit):
            rows = pl.ds(pl.multiple_of((1 - xbit) * half_deep, 16), half_deep)
            landed(res_ref.at[unit, rows, mine], r_ax.at[unit])
            launch(along_s(unit))
            write_out(unit, 0, mine)

        def stage7(unit):
            landed(res_ref.at[unit, :, theirs], r_as.at[unit])
            write_out(unit, 1, theirs)
            for make in (to_x, to_z, along_z, along_x, along_s):
                for copy in make(unit):
                    copy.wait_send()

        return stage0, stage1, stage2, stage3, stage4, stage5, stage6, stage7

    early = pipeline(part_of, sib_of)
    late = pipeline(qkv_part, qkv_sib)

    def tick(time, carry):
        for stage, lag in ((1, 0), (2, 2)):
            unit = time - lag

            @pl.when((unit >= 0) & (unit < 9))
            def _(stage=stage, unit=unit):
                early[stage](unit)

            @pl.when((unit >= 9) & (unit < 12))
            def _(stage=stage, unit=unit):
                late[stage](unit)

        for stage in range(3, 8):
            unit = time - stage

            @pl.when((unit >= 0) & (unit < 12))
            def _(stage=stage, unit=unit):
                early[stage](unit)

        return carry

    def ticks(first, last):
        lax.fori_loop(first, last, tick, 0)

    def middle_part(act_ref, slope_ref, hid2, hid2_t, low_ref):
        acc_ref = ingrad_ref
        own_copy(1).wait()
        chunk_done(3)
        att_t = att_ref[...].reshape(width, BLOCK)
        ap_ref[...] = product(transposed(att_t), wo[...])
        gate_attn = mod_ref[:1, width : 2 * width]
        scale_mlp = mod_ref[:1, 2 * width : 3 * width]
        gate_mlp = mod_ref[:1, 3 * width :]
        mid_ref[...] = tok_ref[...].astype(jnp.float32) + gate_attn * ap_ref[...]
        normed, unused = layer_norm(mid_ref[...])
        low = (normed * (1.0 + scale_mlp)).astype(jnp.bfloat16)
        hid2[...] = low
        hid2_t[...] = transposed(low)
        acc_ref[...] = jnp.zeros_like(acc_ref)
        own_copy(2).wait()
        chunk_done(4)
        own_copy(3).wait()
        chunk_done(5)
        curve = math.sqrt(2.0 / math.pi)

        def up(index, carry):
            cols = pl.ds(pl.multiple_of(index * width, width), width)
            before = product(hid2[...], wu[:, cols])
            square = before * before
            bent = jnp.tanh(curve * (before + 0.044715 * (square * before)))
            after = (0.5 * before * (1.0 + bent)).astype(jnp.bfloat16)
            act_ref[:, cols] = after
            slope_ref[:, cols] = 0.5 * (1.0 + bent) + 0.5 * before * (1.0 - bent * bent) * (
                curve * (1.0 + 3.0 * 0.044715 * square)
            )
            acc_ref[...] += product(after, wd[cols, :])
            return carry

        lax.fori_loop(0, 4, up, 0)
        grad = cot_ref[...].astype(jnp.float32)
        mlp_out = acc_ref[...]
        result_ref[...] = mid_ref[...] + gate_mlp * mlp_out
        sums_ref[3:4, :] = jnp.sum(grad * mlp_out, axis=0, keepdims=True)
        low_ref[...] = (grad * gate_mlp).astype(jnp.bfloat16)
        acc_ref[...] = jnp.zeros_like(acc_ref)

        def down(index, carry):
            for side in range(2):
                cols = pl.ds(pl.multiple_of(side * 2 * width + index * width, width), width)
                grad_act = product_back(low_ref[...], wd[cols, :])
                grad_pre = (grad_act * slope_ref[:, cols]).astype(jnp.bfloat16)
                grad_down = product(transposed(act_ref[:, cols]), low_ref[...])
                for pick in range(2):
                    parts[4 * index + pick, side] = grad_down[
                        pick * deep : (pick + 1) * deep
                    ].astype(jnp.bfloat16)
                grad_up = product(hid2_t[...], grad_pre).astype(jnp.bfloat16)
                for pick in range(2):
                    for half in range(2):
                        parts[4 * index + 2 + pick, half, :, side * span : (side + 1) * span] = (
                            grad_up[half * deep : (half + 1) * deep, pick * span : (pick + 1) * span]
                        )
                acc_ref[...] += product_back(grad_pre, wu[:, cols])
            for pick in range(4):
                early[0](4 * index + pick)
            return carry

        lax.fori_loop(0, 2, down, 0)
        for index in range(len(chunks)):
            chunk_sent(index)
        pl.semaphore_signal(free_sem, inc=1, device_id={"ctx": sibling}, device_id_type=MESH)
        grad_hidden = acc_ref[...]
        normed, inverse = layer_norm(mid_ref[...])
        sums_ref[2:3, :] = jnp.sum(grad_hidden * normed, axis=0, keepdims=True)
        grad_mid = cot_ref[...].astype(jnp.float32) + norm_back(
            grad_hidden * (1.0 + scale_mlp), normed, inverse
        )
        ingrad_ref[...] = grad_mid
        sums_ref[1:2, :] = jnp.sum(grad_mid * ap_ref[...], axis=0, keepdims=True)
        gap = (grad_mid * gate_attn).astype(jnp.bfloat16)
        low_ref[...] = gap
        douts_ref[...] = product_back(wo[...], gap).astype(jnp.bfloat16).reshape(
            heads, HD, BLOCK
        )

        def send_dout(step, carry):
            send_head(lax.rem(step + 3 * (plane + 2), heads), douts_ref, got_ref, bs, br)
            return carry

        early[1](0)
        lax.fori_loop(0, heads, send_dout, 0)
        early[1](1)
        grad_out = product(att_ref[...].reshape(width, BLOCK), low_ref[...]).astype(jnp.bfloat16)
        parts[8, 0] = grad_out[:deep]
        parts[8, 1] = grad_out[deep:]
        early[0](8)

    pl.run_scoped(
        middle_part,
        pltpu.VMEM((BLOCK, 4 * width), jnp.bfloat16),
        pltpu.VMEM((BLOCK, 4 * width), jnp.float32),
        pltpu.VMEM((BLOCK, width), jnp.bfloat16),
        pltpu.VMEM((width, BLOCK), jnp.bfloat16),
        pltpu.VMEM((BLOCK, width), jnp.bfloat16),
    )

    def backward(both_ref, side_ref, grad_ref, lse_wide, delta_wide, low_ref):
        @pl.when(owner)
        def _():
            def prepare(group, carry):
                first = 4 * group
                for inner in range(4):
                    landed(got_ref.at[first + inner], br.at[first + inner])
                dout = side_by_side(lambda block: got_ref[block], first)
                query = side_by_side(lambda block: buf_ref[block, :HD, :], first)
                mixed = side_by_side(lambda block: mix_ref[block], first)
                both = jnp.concatenate([query, dout], axis=0)
                both_ref[group] = both
                side_ref[group] = transposed(both)
                grad_ref[group] = jnp.zeros((HD, 4 * BLOCK), jnp.float32)
                lse_wide[group] = side_by_side(lambda block: lse_ref[block], first)
                delta = jnp.sum(dout.astype(jnp.float32) * mixed, axis=0, keepdims=True)
                delta_wide[group] = jnp.broadcast_to(delta, (8, 4 * BLOCK))
                return carry

            lax.fori_loop(0, blocks // 4, prepare, 0)

        def key_back(group, inner):
            key = 4 * group + inner
            pair = transposed(buf_ref[key, HD:, :])
            left = lax.broadcasted_iota(jnp.int32, pair.shape, 1) < HD
            none = jnp.zeros_like(pair)
            key_side, value_side = jnp.where(left, pair, none), jnp.where(left, none, pair)
            key_low = buf_ref[key, HD : 2 * HD, :]

            def visit_queries(which, skip, state):
                begin = skip * BLOCK
                both = both_ref[which, :, begin:]
                probs = jnp.exp(product(key_side, both) - lse_wide[which, :1, begin:])
                grad_scores = (
                    probs * (product(value_side, both) - delta_wide[which, :1, begin:])
                ).astype(jnp.bfloat16)
                side = side_ref[which, begin:, :]
                grad_ref[which, :, begin:] += product(key_low, grad_scores)
                return (
                    state[0] + product(grad_scores, side),
                    state[1] + product(probs.astype(jnp.bfloat16), side),
                )

            zero = jnp.zeros((BLOCK, 2 * HD), jnp.float32)
            state = visit_queries(group, inner, (zero, zero))
            state = lax.fori_loop(
                group + 1, blocks // 4, lambda which, now: visit_queries(which, 0, now), state
            )
            low_ref[key, HD : 2 * HD, :] = jnp.transpose(state[0])[:HD].astype(jnp.bfloat16)
            low_ref[key, 2 * HD :, :] = jnp.transpose(state[1])[HD:].astype(jnp.bfloat16)
            return_rows(key, HD, 2 * HD, 0)

        def part_copy_of(block, first, count, slot):
            return remote(
                low_ref.at[block, pl.ds(first, count)], gland_ref.at[head, pl.ds(first, count)],
                bbs.at[block, slot], bbr.at[head, slot], ctx=block,
            )

        def return_rows(block, first, count, slot):
            @pl.when(block != me)
            def _():
                part_copy_of(block, first, count, slot).start()

            @pl.when(block == me)
            def _():
                pltpu.make_async_copy(
                    low_ref.at[block, pl.ds(first, count)],
                    gland_ref.at[head, pl.ds(first, count)],
                    bbr.at[head, slot],
                ).start()

        begun = 2
        for inner in range(4):
            def visit(group, carry, inner=inner):
                @pl.when(owner)
                def _():
                    key_back(group, inner)

                return carry

            for edge in range(len(TICKS[inner])):
                low, high = SPLITS[edge], SPLITS[edge + 1]
                lax.fori_loop(low, high, visit, 0)
                ticks(begun, begun + TICKS[inner][edge])
                begun += TICKS[inner][edge]

        @pl.when(owner)
        def _():
            def finish_query(group, carry):
                grad_query = (grad_ref[group] * score_scale).astype(jnp.bfloat16)
                for inner in range(4):
                    block = 4 * group + inner
                    low_ref[block, :HD, :] = grad_query[:, inner * BLOCK : (inner + 1) * BLOCK]
                    return_rows(block, 0, HD, 1)
                return carry

            lax.fori_loop(0, blocks // 4, finish_query, 0)

        ticks(begun, begun + TICKS[4][0])

        @pl.when(owner)
        def _():
            def sent(block, carry):
                @pl.when(block != me)
                def _():
                    part_copy_of(block, HD, 2 * HD, 0).wait_send()
                    part_copy_of(block, 0, HD, 1).wait_send()

                return carry

            lax.fori_loop(0, blocks, sent, 0)

        scatter_sent(me, heads, douts_ref, got_ref, bs, br)

        def arrived(which, carry):
            landed(gland_ref.at[which, pl.ds(HD, 2 * HD)], bbr.at[which, 0])
            landed(gland_ref.at[which, pl.ds(0, HD)], bbr.at[which, 1])
            return carry

        lax.fori_loop(0, heads, arrived, 0)

    pl.run_scoped(
        backward,
        pltpu.VMEM((blocks // 4, 2 * HD, 4 * BLOCK), jnp.bfloat16),
        pltpu.VMEM((blocks // 4, 4 * BLOCK, 2 * HD), jnp.bfloat16),
        pltpu.VMEM((blocks // 4, HD, 4 * BLOCK), jnp.float32),
        pltpu.VMEM((blocks // 4, 8, 4 * BLOCK), jnp.float32),
        pltpu.VMEM((blocks // 4, 8, 4 * BLOCK), jnp.float32),
        pltpu.VMEM((blocks, 3 * HD, BLOCK), jnp.bfloat16),
    )

    def closing(gproj, acc_ref):
        def turn_back(group, carry):
            cos, sin = cos_ref[...], sin_ref[...]
            for kind in range(3):
                pieces = []
                for inner in range(4):
                    which = group * 4 + inner
                    if kind == 2:
                        pieces.append(gland_ref[which, 2 * HD :, :])
                        continue
                    top = gland_ref[which, kind * HD : kind * HD + HD // 2, :].astype(jnp.float32)
                    bottom = gland_ref[
                        which, kind * HD + HD // 2 : (kind + 1) * HD, :
                    ].astype(jnp.float32)
                    pieces.append((top * cos + bottom * sin).astype(jnp.bfloat16))
                    pieces.append((bottom * cos - top * sin).astype(jnp.bfloat16))
                cols = pl.ds(pl.multiple_of(kind * width + group * 4 * HD, 4 * HD), 4 * HD)
                gproj[:, cols] = transposed(jnp.concatenate(pieces, axis=0))
            return carry

        lax.fori_loop(0, heads // 4, turn_back, 0)
        acc_ref[...] = jnp.zeros_like(acc_ref)
        pl.semaphore_wait(free_sem, 1)

        def gradient(index, carry):
            cols = pl.ds(pl.multiple_of(index * width, width), width)
            low = product(hid1_t[...], gproj[:, cols]).astype(jnp.bfloat16)
            wd[pl.ds(pl.multiple_of(index * width, width), width), :] = low
            late[0](9 + index)
            return carry

        lax.fori_loop(0, 3, gradient, 0)

        def back(index, carry):
            cols = pl.ds(pl.multiple_of(index * width, width), width)
            acc_ref[...] += product_back(gproj[:, cols], wq[:, cols])
            return carry

        lax.fori_loop(0, 3, back, 0)
        normed, inverse = layer_norm(tok_ref[...].astype(jnp.float32))
        grad_hidden = acc_ref[...]
        sums_ref[0:1, :] = jnp.sum(grad_hidden * normed, axis=0, keepdims=True)
        ingrad_ref[...] = ingrad_ref[...] + norm_back(
            grad_hidden * (1.0 + mod_ref[:1, :width]), normed, inverse
        )

    pl.run_scoped(
        closing,
        pltpu.VMEM((BLOCK, 3 * width), jnp.bfloat16),
        pltpu.VMEM((BLOCK, width), jnp.float32),
    )

    def slots(first, count):
        return table_ref.at[pl.ds(first, count)]

    chip_slot = core * 4 * planes + 4 * plane

    def table_row():
        ref = slots(chip_slot + 2 * xbit + row, 1)
        return [remote(ref, ref, s_t.at[0], r_t.at[0], fsdp=other)]

    def table_x():
        ref = slots(chip_slot + 2 * xbit, 2)
        return [remote(ref, ref, s_t.at[1], r_t.at[1], ctx=chip_next)]

    def table_z():
        ref = slots(chip_slot, 4)
        return [
            remote(ref, ref, s_t.at[2 + step], r_t.at[2 + step],
                   ctx=4 * lax.rem(plane + step, planes) + piece)
            for step in range(1, planes)
        ]

    def table_s():
        ref = slots(core * 4 * planes, 4 * planes)
        return [remote(ref, ref, s_t.at[2], r_t.at[2], ctx=sibling)]

    spot = chip_slot + 2 * xbit + row
    for index in range(4):
        table_ref[spot, index : index + 1, :] = sums_ref[index : index + 1, :]
    table_ref[spot, 4:5, :] = emb_ref[:1, :]
    for copy in table_row():
        copy.start()

    begun = 2 + sum(sum(counts) for counts in TICKS)

    def finish(time, carry):
        tick(time, carry)

        @pl.when(time == begun + 1)
        def _():
            landed(slots(chip_slot + 2 * xbit + other, 1), r_t.at[0])
            for copy in table_x():
                copy.start()

        @pl.when(time == begun + 3)
        def _():
            landed(slots(chip_slot + 2 * (1 - xbit), 2), r_t.at[1])
            for copy in table_z():
                copy.start()

        @pl.when(time == begun + 5)
        def _():
            for step in range(1, planes):
                goal = lax.rem(plane + planes - step, planes)
                landed(slots(core * 4 * planes + 4 * goal, 4), r_t.at[2 + step])
            for copy in table_s():
                copy.start()

        return carry

    lax.fori_loop(begun, 19, finish, 0)
    landed(slots((1 - core) * 4 * planes, 4 * planes), r_t.at[2])
    count = 2 * blocks
    emb_cols = pl.ds(pl.multiple_of(row * (width // 2), 128), width // 2)
    eds = table_ref[:, 4, emb_cols].astype(jnp.bfloat16)
    for third_part in range(3):
        eds_ref[third_part * count : (third_part + 1) * count, :] = eds
    for index in range(4):
        left = table_ref[:, index, :]
        for third_part in range(3):
            low = left.astype(jnp.bfloat16)
            left = left - low.astype(jnp.float32)
            sds_ref[
                third_part * count : (third_part + 1) * count, index * width : (index + 1) * width
            ] = low
    for copies in (table_row(), table_x(), table_z(), table_s()):
        for copy in copies:
            copy.wait_send()

    def saved(unit, carry):
        for which in range(2):
            pltpu.make_async_copy(
                res_ref.at[unit, :, pl.ds(0, span)], og_out.at[:, pl.ds(0, span)],
                out_sem.at[unit, which],
            ).wait()
        return carry

    lax.fori_loop(0, 12, saved, 0)


def side_by_side(pick, first):
    return jnp.concatenate([pick(first + inner) for inner in range(4)], axis=1)


def seen(shape):
    keys = lax.broadcasted_iota(jnp.int32, shape, 0) // BLOCK
    return keys <= lax.broadcasted_iota(jnp.int32, shape, 1) // BLOCK


FORWARD_EVENTS = (
    (0, (0, 4)),
    (1, (1, 3)),
    (2, (1, 4)),
    (3, (0, 5)),
)
TICKS = ((1, 1), (1, 1), (1, 0), (1, 0), (1,))
SPLITS = (0, 1, 4)


def rope_constants(blocks):
    half = HD // 2
    frequency = rope_base ** (-2.0 * np.arange(half, dtype=np.float64) / HD)
    inner = frequency[:, None] * np.arange(BLOCK, dtype=np.float64)[None, :]
    outer = frequency[:, None] * (BLOCK * np.arange(128, dtype=np.float64))[None, :]
    outer = np.where(np.arange(128)[None, :] < blocks, outer, 0.0)
    return np.concatenate(
        [np.cos(inner), np.sin(inner), np.cos(outer), np.sin(outer)], axis=1
    ).astype(np.float32)


def fast_device(tokens, timestep, time_table, w_qkv, w_out, w_up, w_down, w_ada, cotangent):
    rows, width = tokens.shape[1:]
    heads = width // HD
    blocks = lax.axis_size("ctx")
    planes = blocks // 4
    deep, span = width // 2, width // 2
    embedded = lax.dynamic_slice_in_dim(time_table, timestep[0, 0], 1, 0)
    embedded = embedded.astype(jnp.bfloat16).astype(jnp.float32)
    emb_rows = jnp.broadcast_to(embedded, (8, width))
    hbm = pl.BlockSpec(memory_space=pl.ANY)
    vmem = pl.BlockSpec(memory_space=pltpu.VMEM)
    low, high = jnp.bfloat16, jnp.float32
    dma = pltpu.SemaphoreType.DMA
    steps = planes - 1
    units = 12
    scratch = [
        pltpu.VMEM((width, 3 * width), low),
        pltpu.VMEM((width, width), low),
        pltpu.VMEM((width, 4 * width), low),
        pltpu.VMEM((4 * width, width), low),
        pltpu.VMEM((8, 4 * width), high),
        pltpu.VMEM((8, width), high),
        pltpu.VMEM((8, 4 * width), high),
        pltpu.VMEM((8, 4 * width), high),
        pltpu.VMEM((width, BLOCK), low),
        pltpu.VMEM((BLOCK, width), high),
        pltpu.VMEM((BLOCK, width), high),
        pltpu.VMEM((8, width), high),
        pltpu.VMEM((HD // 2, BLOCK), high),
        pltpu.VMEM((HD // 2, BLOCK), high),
        pltpu.VMEM((heads, 3 * HD, BLOCK), low),
        pltpu.VMEM((blocks, 3 * HD, BLOCK), low),
        pltpu.VMEM((blocks, HD, BLOCK), high),
        pltpu.VMEM((blocks, 8, BLOCK), high),
        pltpu.VMEM((heads, HD, BLOCK), low),
        pltpu.VMEM((heads, HD, BLOCK), low),
        pltpu.VMEM((blocks, HD, BLOCK), low),
        pltpu.VMEM((9, 2, deep, width), low),
        pltpu.VMEM((9, 2, deep, span), low),
        pltpu.VMEM((units, deep, span), low),
        pltpu.VMEM((units, deep // 2, span), low),
        pltpu.VMEM((units, steps, deep // 2 // planes, span), low),
        pltpu.VMEM((units, deep, width), low),
        pltpu.VMEM((2 * blocks, 8, width), high),
    ]
    sems = [
        (5,), (2,), (2,), (6, 4), (6, 4),
        (heads,), (blocks,), (blocks,), (heads,),
        (heads,), (blocks,), (blocks, 2), (heads, 2),
        (units, 2), (units, 2), (units,), (units,), (units,), (units,),
        (units, steps), (units, steps), (units, steps), (units, steps),
        (units,), (units,), (units,), (units,), (planes + 2,), (planes + 2,), (units, 2),
    ]
    scratch += [dma(shape) for shape in sems] + [pltpu.SemaphoreType.REGULAR]
    result, input_grad, eds, sds, *sums = pl.pallas_call(
        functools.partial(layer_kernel, blocks, heads),
        out_shape=[
            jax.ShapeDtypeStruct((rows, width), high),
            jax.ShapeDtypeStruct((rows, width), high),
            jax.ShapeDtypeStruct((6 * blocks, deep), low),
            jax.ShapeDtypeStruct((6 * blocks, 4 * width), low),
        ]
        + [jax.ShapeDtypeStruct(w.shape, low) for w in (w_qkv, w_out, w_up, w_down)],
        in_specs=[vmem] * 4 + [hbm] * 5,
        out_specs=[vmem] * 4 + [hbm] * 4,
        scratch_shapes=scratch,
        compiler_params=pltpu.CompilerParams(
            collective_id=1, has_side_effects=True, vmem_limit_bytes=VMEM_LIMIT
        ),
    )(tokens[0], cotangent[0], emb_rows, jnp.asarray(rope_constants(blocks)),
      w_ada, w_qkv, w_out, w_up, w_down)
    ada_total = lax.dot_general(
        eds, sds, (((0,), (0,)), ((), ())), preferred_element_type=jnp.float32
    )
    return (result[None], input_grad[None], *[total.astype(high) for total in sums], ada_total)


def solution(mesh):
    chosen = fast_device if mesh.shape["ctx"] == 16 else on_device
    return jax.shard_map(
        chosen,
        mesh=mesh,
        in_specs=(
            P("fsdp", "ctx", None),
            P("fsdp", "ctx"),
            P(),
            P("fsdp", None),
            P("fsdp", None),
            P("fsdp", None),
            P("fsdp", None),
            P("fsdp", None),
            P("fsdp", "ctx", None),
        ),
        out_specs=(
            P("fsdp", "ctx", None),
            P("fsdp", "ctx", None),
            P("fsdp", None),
            P("fsdp", None),
            P("fsdp", None),
            P("fsdp", None),
            P("fsdp", None),
        ),
        check_vma=False,
    )
```

```python
import functools
import math

import jax
import jax.numpy as jnp
import numpy as np
from jax import lax
from jax.experimental import pallas as pl
from jax.experimental.pallas import tpu as pltpu
from jax.sharding import PartitionSpec as P

HD = 64
BLOCK = 256
VMEM_LIMIT = 63 * 1024 * 1024
MESH = pl.DeviceIdType.MESH


norm_eps = 1e-06
masked_score = -1e30
rope_base = 10000.0


def layer_norm(values):
    center = values - jnp.mean(values, axis=-1, keepdims=True)
    inverse = lax.rsqrt(jnp.mean(center * center, axis=-1, keepdims=True) + norm_eps)
    return (center * inverse, inverse)


def norm_back(grad_norm, normed, inverse):
    mean_grad = jnp.mean(grad_norm, axis=-1, keepdims=True)
    mean_cross = jnp.mean(grad_norm * normed, axis=-1, keepdims=True)
    return inverse * (grad_norm - mean_grad - normed * mean_cross)


def rope_tables(positions, head_size):
    half_size = head_size // 2
    frequency = jnp.exp(
        jnp.arange(half_size, dtype=jnp.float32) * (-2.0 * math.log(rope_base) / head_size)
    )
    angles = positions.astype(jnp.float32)[:, None] * frequency[None, :]
    cosine_table = jnp.concatenate([jnp.cos(angles), jnp.cos(angles)], axis=-1)[:, None, :]
    sine_table = jnp.concatenate([jnp.sin(angles), jnp.sin(angles)], axis=-1)[:, None, :]
    return (cosine_table, sine_table)


def rotate_half(values):
    middle = values.shape[-1] // 2
    return jnp.concatenate([-values[..., middle:], values[..., :middle]], axis=-1)


def rotate(values, cosine_table, sine_table):
    return values * cosine_table + rotate_half(values) * sine_table


def rotate_back(gradient, cosine_table, sine_table):
    return gradient * cosine_table - rotate_half(gradient * sine_table)


def gelu_tanh(values):
    return jax.nn.gelu(values, approximate=True)


def split_rows(array, sub_rows):
    return array.reshape((array.shape[0] // sub_rows, sub_rows) + array.shape[1:])


def part_starts(total_rows, sub_rows):
    return sub_rows * jnp.arange(total_rows // sub_rows, dtype=jnp.int32)


def keep_same(partial_value):
    return partial_value


def attend_forward(partial_value, pieces, queries, query_block, score_scale):
    key_rows, value_rows = pieces
    sub_rows = queries.shape[0]

    def attend_visit(running, scan_item):
        key_part, value_part, part_start = scan_item

        def attend_update(running):
            running_max, running_sum, running_out = running
            key_block = (part_start + jnp.arange(sub_rows, dtype=jnp.int32)) // BLOCK
            allowed = (key_block[None, :] <= query_block[:, None])[None]
            scores = (
                jnp.einsum("qhd,khd->hqk", queries, key_part, preferred_element_type=jnp.float32)
                * score_scale
            )
            scores = jnp.where(allowed, scores, masked_score)
            new_max = jnp.maximum(running_max, jnp.max(scores, axis=-1))
            weights = jnp.where(allowed, jnp.exp(scores - new_max[..., None]), 0.0)
            decay = jnp.exp(running_max - new_max)
            running_sum = running_sum * decay + jnp.sum(weights, axis=-1)
            running_out = running_out * decay[..., None] + jnp.einsum(
                "hqk,khd->hqd",
                weights.astype(jnp.bfloat16),
                value_part,
                preferred_element_type=jnp.float32,
            )
            return (new_max, running_sum, running_out)

        return (
            lax.cond(part_start // BLOCK <= query_block[-1], attend_update, keep_same, running),
            None,
        )

    partial_value, unused = lax.scan(
        attend_visit,
        partial_value,
        (
            split_rows(key_rows, sub_rows),
            split_rows(value_rows, sub_rows),
            part_starts(key_rows.shape[0], sub_rows),
        ),
    )
    return partial_value


def on_device(tokens, timestep, time_table, w_qkv, w_out, w_up, w_down, w_ada, cotangent):
    tok_rows = tokens.shape[1]
    model_width = tokens.shape[2]
    heads = model_width // HD
    score_scale = 1.0 / math.sqrt(HD)
    highest_precision = lax.Precision.HIGHEST
    full_weights = (
        lax.all_gather(w_qkv, "fsdp", axis=0, tiled=True),
        lax.all_gather(w_out, "fsdp", axis=0, tiled=True),
        lax.all_gather(w_up, "fsdp", axis=0, tiled=True),
        lax.all_gather(w_down, "fsdp", axis=0, tiled=True),
        lax.all_gather(w_ada, "fsdp", axis=0, tiled=True),
    )
    qkv_full, out_full, up_full, down_full, ada_full = full_weights
    steps_onehot = (
        timestep[0][:, None] == jnp.arange(time_table.shape[0], dtype=jnp.int32)[None, :]
    ).astype(jnp.float32)
    embedded = jnp.dot(steps_onehot, time_table, precision=highest_precision).astype(jnp.bfloat16)
    modulation = jnp.dot(embedded, ada_full, preferred_element_type=jnp.float32)
    per_token = jnp.repeat(modulation, BLOCK, axis=0)
    scale_attn, gate_attn, scale_mlp, gate_mlp = jnp.split(per_token, 4, axis=1)
    inputs = tokens[0].astype(jnp.float32)
    normed_one, inverse_one = layer_norm(inputs)
    residual_first = (normed_one * (1.0 + scale_attn)).astype(jnp.bfloat16)
    projected_output = jnp.dot(
        residual_first, qkv_full, preferred_element_type=jnp.float32
    ).reshape(tok_rows, 3, heads, HD)
    positions = lax.axis_index("ctx") * tok_rows + jnp.arange(tok_rows, dtype=jnp.int32)
    cosine_table, sine_table = rope_tables(positions, HD)
    queries = rotate(projected_output[:, 0], cosine_table, sine_table).astype(jnp.bfloat16)
    key_own = rotate(projected_output[:, 1], cosine_table, sine_table).astype(jnp.bfloat16)
    value_own = projected_output[:, 2].astype(jnp.bfloat16)
    query_block = positions // BLOCK
    start_state = (
        jnp.full((heads, tok_rows), masked_score, jnp.float32),
        jnp.zeros((heads, tok_rows), jnp.float32),
        jnp.zeros((heads, tok_rows, HD), jnp.float32),
    )
    running_max, running_sum, running_out = attend_forward(
        start_state,
        (
            lax.all_gather(key_own, "ctx", axis=0, tiled=True),
            lax.all_gather(value_own, "ctx", axis=0, tiled=True),
        ),
        queries,
        query_block,
        score_scale,
    )
    attn_rows = jnp.transpose(running_out / running_sum[..., None], (1, 0, 2))
    query_lse = running_max + jnp.log(running_sum)
    attn_low = attn_rows.reshape(tok_rows, model_width).astype(jnp.bfloat16)
    attention_projected = jnp.dot(attn_low, out_full, preferred_element_type=jnp.float32)
    middle = inputs + gate_attn * attention_projected
    normed_two, inverse_two = layer_norm(middle)
    residual_second = (normed_two * (1.0 + scale_mlp)).astype(jnp.bfloat16)
    before_activation = jnp.dot(residual_second, up_full, preferred_element_type=jnp.float32)
    gelu_activated, gelu_back = jax.vjp(gelu_tanh, before_activation)
    act_low = gelu_activated.astype(jnp.bfloat16)
    feedforward_output = jnp.dot(act_low, down_full, preferred_element_type=jnp.float32)
    result = middle + gate_mlp * feedforward_output
    qkv_back, out_back, up_back, down_back = (
        lax.all_gather(w_qkv, "fsdp", axis=0, tiled=True),
        lax.all_gather(w_out, "fsdp", axis=0, tiled=True),
        lax.all_gather(w_up, "fsdp", axis=0, tiled=True),
        lax.all_gather(w_down, "fsdp", axis=0, tiled=True),
    )
    upstream = cotangent[0].astype(jnp.float32)
    grad_gate_mlp = upstream * feedforward_output
    grad_mlp = (upstream * gate_mlp).astype(jnp.bfloat16)
    grad_down = jnp.einsum("tf,td->fd", act_low, grad_mlp, preferred_element_type=jnp.float32)
    grad_act = jnp.einsum("td,fd->tf", grad_mlp, down_back, preferred_element_type=jnp.float32)
    grad_pre = gelu_back(grad_act)[0].astype(jnp.bfloat16)
    grad_up = jnp.einsum("td,tf->df", residual_second, grad_pre, preferred_element_type=jnp.float32)
    grad_hidden_two = jnp.einsum("tf,df->td", grad_pre, up_back, preferred_element_type=jnp.float32)
    grad_scale_mlp = grad_hidden_two * normed_two
    grad_middle = upstream + norm_back(grad_hidden_two * (1.0 + scale_mlp), normed_two, inverse_two)
    grad_gate_attn = grad_middle * attention_projected
    grad_attn_proj = (grad_middle * gate_attn).astype(jnp.bfloat16)
    grad_out = jnp.einsum("td,te->de", attn_low, grad_attn_proj, preferred_element_type=jnp.float32)
    grad_attended = jnp.einsum(
        "te,de->td", grad_attn_proj, out_back, preferred_element_type=jnp.float32
    )
    grad_heads = grad_attended.astype(jnp.bfloat16).reshape(tok_rows, heads, HD)
    delta_rows = jnp.sum(grad_heads.astype(jnp.float32) * attn_rows, axis=-1)
    query_delta = jnp.transpose(delta_rows)
    lse_rows = jnp.transpose(query_lse)
    lse_high = lse_rows.astype(jnp.bfloat16)
    lse_rest = (lse_rows - lse_high.astype(jnp.float32)).astype(jnp.bfloat16)
    delta_high = delta_rows.astype(jnp.bfloat16)
    delta_rest = (delta_rows - delta_high.astype(jnp.float32)).astype(jnp.bfloat16)
    stat_rows = jnp.concatenate([lse_high, lse_rest, delta_high, delta_rest], axis=1)
    zero_heads = jnp.zeros((tok_rows, heads, HD), jnp.float32)
    partial_value = (zero_heads, zero_heads, zero_heads)
    grad_query = partial_value[0]
    key_rows = lax.all_gather(key_own, "ctx", axis=0, tiled=True)

    def query_visit(partial_value, scan_item):
        key_part, value_part, part_start = scan_item

        def query_update(partial_value):
            key_block = (part_start + jnp.arange(tok_rows, dtype=jnp.int32)) // BLOCK
            allowed = (key_block[None, :] <= query_block[:, None])[None]
            scores = (
                jnp.einsum("qhd,khd->hqk", queries, key_part, preferred_element_type=jnp.float32)
                * score_scale
            )
            probs = jnp.where(allowed, jnp.exp(scores - query_lse[..., None]), 0.0)
            grad_prob = jnp.einsum(
                "qhd,khd->hqk", grad_heads, value_part, preferred_element_type=jnp.float32
            )
            grad_score = (probs * (grad_prob - query_delta[..., None]) * score_scale).astype(
                jnp.bfloat16
            )
            return partial_value + jnp.einsum(
                "hqk,khd->qhd", grad_score, key_part, preferred_element_type=jnp.float32
            )

        return (
            lax.cond(
                part_start // BLOCK <= query_block[-1], query_update, keep_same, partial_value
            ),
            None,
        )

    grad_query, unused = lax.scan(
        query_visit,
        grad_query,
        (
            split_rows(key_rows, tok_rows),
            split_rows(lax.all_gather(value_own, "ctx", axis=0, tiled=True), tok_rows),
            part_starts(key_rows.shape[0], tok_rows),
        ),
    )
    key_partial_value = (partial_value[1], partial_value[2])
    query_rows = lax.all_gather(queries, "ctx", axis=0, tiled=True)

    def key_visit(running, scan_item):
        query_part, dout_part, stat_part, part_start = scan_item

        def key_update(running):
            grad_key, grad_value = running
            query_blk = (part_start + jnp.arange(tok_rows, dtype=jnp.int32)) // BLOCK
            allowed = (query_blk[:, None] >= query_block[None, :])[None]
            stat_float = stat_part.astype(jnp.float32)
            lse_part = jnp.transpose(stat_float[:, :heads] + stat_float[:, heads : 2 * heads])
            delta_part = jnp.transpose(
                stat_float[:, 2 * heads : 3 * heads] + stat_float[:, 3 * heads :]
            )
            scores = (
                jnp.einsum("qhd,khd->hqk", query_part, key_own, preferred_element_type=jnp.float32)
                * score_scale
            )
            probs = jnp.where(allowed, jnp.exp(scores - lse_part[..., None]), 0.0)
            grad_value = grad_value + jnp.einsum(
                "hqk,qhd->khd",
                probs.astype(jnp.bfloat16),
                dout_part,
                preferred_element_type=jnp.float32,
            )
            grad_prob = jnp.einsum(
                "qhd,khd->hqk", dout_part, value_own, preferred_element_type=jnp.float32
            )
            grad_score = (probs * (grad_prob - delta_part[..., None]) * score_scale).astype(
                jnp.bfloat16
            )
            grad_key = grad_key + jnp.einsum(
                "hqk,qhd->khd", grad_score, query_part, preferred_element_type=jnp.float32
            )
            return (grad_key, grad_value)

        last_seen = (part_start + tok_rows - 1) // BLOCK
        return (lax.cond(last_seen >= query_block[0], key_update, keep_same, running), None)

    key_partial_value, unused = lax.scan(
        key_visit,
        key_partial_value,
        (
            split_rows(query_rows, tok_rows),
            split_rows(lax.all_gather(grad_heads, "ctx", axis=0, tiled=True), tok_rows),
            split_rows(lax.all_gather(stat_rows, "ctx", axis=0, tiled=True), tok_rows),
            part_starts(query_rows.shape[0], tok_rows),
        ),
    )
    grad_key, grad_value = key_partial_value
    grad_query, grad_key, grad_value = (grad_query, grad_key, grad_value)
    grad_query = rotate_back(grad_query, cosine_table, sine_table)
    grad_key = rotate_back(grad_key, cosine_table, sine_table)
    grad_projected = (
        jnp.stack([grad_query, grad_key, grad_value], axis=1)
        .reshape(tok_rows, 3 * model_width)
        .astype(jnp.bfloat16)
    )
    grad_qkv = jnp.einsum(
        "td,te->de", residual_first, grad_projected, preferred_element_type=jnp.float32
    )
    grad_hidden_one = jnp.einsum(
        "te,de->td", grad_projected, qkv_back, preferred_element_type=jnp.float32
    )
    grad_scale_attn = grad_hidden_one * normed_one
    input_grad = grad_middle + norm_back(
        grad_hidden_one * (1.0 + scale_attn), normed_one, inverse_one
    )
    grad_modulation = jnp.concatenate(
        [grad_scale_attn, grad_gate_attn, grad_scale_mlp, grad_gate_mlp], axis=1
    )
    grad_blocks = jnp.sum(
        grad_modulation.reshape(tok_rows // BLOCK, BLOCK, 4 * model_width), axis=1
    )
    embedded_float = embedded.astype(jnp.float32)
    halves = (
        lax.psum_scatter(
            grad_qkv.astype(jnp.bfloat16), "fsdp", scatter_dimension=0, tiled=True
        ).astype(jnp.float32),
        lax.psum_scatter(
            grad_out.astype(jnp.bfloat16), "fsdp", scatter_dimension=0, tiled=True
        ).astype(jnp.float32),
        lax.psum_scatter(
            grad_up.astype(jnp.bfloat16), "fsdp", scatter_dimension=0, tiled=True
        ).astype(jnp.float32),
        lax.psum_scatter(
            grad_down.astype(jnp.bfloat16), "fsdp", scatter_dimension=0, tiled=True
        ).astype(jnp.float32),
    )
    totals = lax.psum((halves[0], halves[1], halves[2], halves[3]), "ctx")
    all_embedded, all_blocks = (
        lax.all_gather(embedded_float, ("ctx", "fsdp"), axis=0, tiled=True),
        lax.all_gather(grad_blocks, ("ctx", "fsdp"), axis=0, tiled=True),
    )
    shard_width = model_width // lax.axis_size("fsdp")
    row_start = lax.axis_index("fsdp") * shard_width
    embedded_part = lax.dynamic_slice_in_dim(all_embedded, row_start, shard_width, 1)
    ada_total = jnp.dot(jnp.transpose(embedded_part), all_blocks, precision=highest_precision)
    return (result[None], input_grad[None], totals[0], totals[1], totals[2], totals[3], ada_total)


def remote(source, target, send_sem, recv_sem, **where):
    return pltpu.make_async_remote_copy(
        src_ref=source,
        dst_ref=target,
        send_sem=send_sem,
        recv_sem=recv_sem,
        device_id=where,
        device_id_type=MESH,
    )


def landed(ref, sem):
    pltpu.make_async_copy(ref, ref, sem).wait()


def head_place(me):
    plane = me // 4
    spot = lax.rem(me, 4)
    odd = lax.rem(plane, 2)
    idle = 3 - 2 * odd
    head = 3 * plane + spot - odd * (spot // 2)
    return spot != idle, head


def head_owner(head):
    plane = head // 3
    rank = lax.rem(head, 3)
    odd = lax.rem(plane, 2)
    return 4 * plane + rank + odd * ((rank + 1) // 2)


def scatter_sent(me, heads, source, target, send_sem, recv_sem):
    def finish(head, carry):
        owner = head_owner(head)

        @pl.when(owner != me)
        def _():
            remote(
                source.at[head], target.at[me], send_sem.at[head], recv_sem.at[me], ctx=owner
            ).wait_send()

        return carry

    lax.fori_loop(0, heads, finish, 0)


def return_block(me, head, block, source, target, send_sem, recv_sem):
    @pl.when(block != me)
    def _():
        remote(
            source.at[block], target.at[head], send_sem.at[block], recv_sem.at[head], ctx=block
        ).start()

    @pl.when(block == me)
    def _():
        pltpu.make_async_copy(source.at[block], target.at[head], recv_sem.at[head]).start()


def return_sent(me, head, blocks, source, target, send_sem, recv_sem):
    def finish(block, carry):
        @pl.when(block != me)
        def _():
            remote(
                source.at[block], target.at[head], send_sem.at[block], recv_sem.at[head], ctx=block
            ).wait_send()

        return carry

    lax.fori_loop(0, blocks, finish, 0)


def wait_heads(heads, target, recv_sem):
    def finish(head, carry):
        landed(target.at[head], recv_sem.at[head])
        return carry

    lax.fori_loop(0, heads, finish, 0)


def transposed(values):
    return jnp.transpose(values.astype(jnp.float32)).astype(values.dtype)


def add_into(target, left, right, rows):
    step = 48

    def body(index, carry):
        spot = pl.ds(pl.multiple_of(index * step, step), step)
        total = left(spot).astype(jnp.float32) + right(spot).astype(jnp.float32)
        target(spot, total.astype(jnp.bfloat16))
        return carry

    lax.fori_loop(0, rows // step, body, 0)


def product(left, right):
    return jnp.dot(left, right, preferred_element_type=jnp.float32)


def product_back(left, right):
    return lax.dot_general(
        left, right, (((1,), (1,)), ((), ())), preferred_element_type=jnp.float32
    )


def layer_kernel(
    blocks, heads,
    tok_ref, cot_ref, emb_ref, rope_ref, ada_hbm, qkv_hbm, out_hbm, up_hbm, down_hbm,
    result_ref, ingrad_ref, eds_ref, sds_ref, og_qkv, og_out, og_up, og_down,
    wq, wo, wu, wd, mod_ref, emb_other, part_other, part_send,
    hid1_t, mid_ref, ap_ref, sums_ref, cos_ref, sin_ref,
    qs_ref, buf_ref, mix_ref, lse_ref, att_ref, douts_ref, got_ref,
    parts, sib_ref, row_ref, x_ref, z_ref, line_ref, res_ref, table_ref,
    own_sem, small_send, small_recv, w_send, w_recv,
    fs, fr, fbs, fbr, bs, br, bbs, bbr,
    s_sib, r_sib, s_row, r_row, s_x, r_x, s_z, r_z, s_az, r_az, s_ax, r_ax, s_as, r_as,
    s_t, r_t, out_sem, free_sem,
):
    me = lax.axis_index("ctx")
    row = lax.axis_index("fsdp")
    other = 1 - row
    piece = lax.rem(me, 4)
    core = lax.rem(me, 2)
    xbit = lax.rem(me // 2, 2)
    plane = me // 4
    planes = blocks // 4
    chip_next = jnp.bitwise_xor(me, 2)
    sibling = jnp.bitwise_xor(me, 1)
    gland_ref = qs_ref
    owner, head = head_place(me)
    width = tok_ref.shape[1]
    score_scale = 1.0 / math.sqrt(HD)

    barrier = pltpu.get_barrier_semaphore()
    pl.semaphore_signal(barrier, inc=1, device_id={"fsdp": other}, device_id_type=MESH)

    def greet(step, carry):
        pl.semaphore_signal(
            barrier, inc=1, device_id={"ctx": lax.rem(me + step, blocks)}, device_id_type=MESH
        )
        return carry

    lax.fori_loop(1, blocks, greet, 0)
    pl.semaphore_wait(barrier, blocks)

    shards = (qkv_hbm, out_hbm, up_hbm, down_hbm)
    wholes = (wq, wo, wu, wd)
    quarter_rows = [shard.shape[0] // 4 for shard in shards]
    third = quarter_rows[0] // 3
    chunks = [
        (0, 0, third),
        (0, third, third),
        (0, 2 * third, third),
        (1, 0, 2 * quarter_rows[1]),
        (2, 0, 2 * quarter_rows[2]),
        (3, 0, 2 * quarter_rows[3]),
    ]

    def chunk_start(index, half, which):
        weight, first, count = chunks[index]
        if index > 2:
            return pl.multiple_of(half * 2 * count + lax.rem(which, 2) * count, 16)
        return pl.multiple_of((half * 4 + which) * quarter_rows[weight] + first, 16)

    def chunk_ref(index, which):
        weight, first, count = chunks[index]
        return wholes[weight].at[pl.ds(chunk_start(index, other, which), count)]

    def y_copy(index):
        weight, first, count = chunks[index]
        return remote(
            shards[weight].at[pl.ds(chunk_start(index, 0, piece), count)],
            wholes[weight].at[pl.ds(chunk_start(index, row, piece), count)],
            w_send.at[index, 0], w_recv.at[index, 0], fsdp=other,
        )

    def onward(index, which, slot, peer):
        ref = chunk_ref(index, which)
        return remote(ref, ref, w_send.at[index, slot], w_recv.at[index, slot], ctx=peer)

    def pass_on(index):
        landed(chunk_ref(index, piece), w_recv.at[index, 0])
        if index < 3:
            onward(index, piece, 1, chip_next).start()
        onward(index, piece, 2, sibling).start()

    def pass_last(index):
        across = jnp.bitwise_xor(piece, 2)
        landed(chunk_ref(index, across), w_recv.at[index, 1])
        onward(index, across, 3, sibling).start()

    def chunk_done(index):
        landed(chunk_ref(index, jnp.bitwise_xor(piece, 1)), w_recv.at[index, 2])
        if index < 3:
            landed(chunk_ref(index, jnp.bitwise_xor(piece, 3)), w_recv.at[index, 3])

    def chunk_sent(index):
        y_copy(index).wait_send()
        onward(index, piece, 2, sibling).wait_send()
        if index < 3:
            onward(index, piece, 1, chip_next).wait_send()
            onward(index, jnp.bitwise_xor(piece, 2), 3, sibling).wait_send()

    def own_copy(weight):
        half = shards[weight].shape[0]
        start = pl.multiple_of(row * half, 16)
        return pltpu.make_async_copy(
            shards[weight], wholes[weight].at[pl.ds(start, half)], own_sem.at[weight]
        )

    emb_copy = remote(emb_ref, emb_other, small_send.at[0], small_recv.at[0], fsdp=other)
    emb_copy.start()
    for index in range(3):
        y_copy(index).start()

    def opening(ada_ref, hid1):
        ada_copy = pltpu.make_async_copy(ada_hbm, ada_ref, own_sem.at[4])
        ada_copy.start()
        for weight in range(4):
            own_copy(weight).start()
        normed, unused = layer_norm(tok_ref[...].astype(jnp.float32))
        ingrad_ref[...] = normed
        half_width = width // 2
        cols = pl.ds(pl.multiple_of(row * half_width, 128), half_width)
        ada_copy.wait()
        emb_copy.wait()
        both = jnp.concatenate([emb_ref[:, cols], emb_other[:, cols]], axis=0)
        partial = product(both.astype(jnp.bfloat16), ada_ref[...])
        mod_ref[...] = partial[:8]
        part_send[...] = partial[8:]
        part_copy = remote(part_send, part_other, small_send.at[1], small_recv.at[1], fsdp=other)
        part_copy.start()
        for index in (3, 4, 5):
            y_copy(index).start()
        pass_on(0)
        lanes = lax.broadcasted_iota(jnp.int32, (HD // 2, 128), 1)
        pick = lanes == me
        cos_block = jnp.sum(
            jnp.where(pick, rope_ref[:, 2 * BLOCK : 2 * BLOCK + 128], 0.0), axis=1, keepdims=True
        )
        sin_block = jnp.sum(
            jnp.where(pick, rope_ref[:, 2 * BLOCK + 128 :], 0.0), axis=1, keepdims=True
        )
        cos_row = rope_ref[:, :BLOCK]
        sin_row = rope_ref[:, BLOCK : 2 * BLOCK]
        cos_ref[...] = cos_row * cos_block - sin_row * sin_block
        sin_ref[...] = sin_row * cos_block + cos_row * sin_block
        part_copy.wait()
        mod_ref[...] += part_other[...]
        low = (ingrad_ref[...] * (1.0 + mod_ref[:1, :width])).astype(jnp.bfloat16)
        hid1[...] = low
        pass_on(1)
        hid1_t[...] = transposed(low)
        pass_on(2)
        for index in range(3):
            pass_last(index)
        own_copy(0).wait()
        for index in range(3):
            chunk_done(index)

        def project(group, carry):
            spans = []
            for kind in range(3):
                cols = pl.ds(pl.multiple_of(kind * width + group * 4 * HD, 4 * HD), 4 * HD)
                spans.append(jnp.transpose(product(hid1[...], wq[:, cols])))
            cos, sin = cos_ref[...], sin_ref[...]
            for inner in range(4):
                which = group * 4 + inner
                for kind in range(2):
                    top = spans[kind][inner * HD : inner * HD + HD // 2]
                    low_half = spans[kind][inner * HD + HD // 2 : (inner + 1) * HD]
                    turned = jnp.concatenate(
                        [top * cos - low_half * sin, low_half * cos + top * sin], axis=0
                    ).astype(jnp.bfloat16)
                    if kind == 0:
                        turned = turned * jnp.bfloat16(score_scale)
                    qs_ref[which, kind * HD : (kind + 1) * HD, :] = turned
                qs_ref[which, 2 * HD :, :] = spans[2][inner * HD : (inner + 1) * HD].astype(
                    jnp.bfloat16
                )
            return carry

        lax.fori_loop(0, heads // 4, project, 0)

        def send_block(step, carry):
            send_head(lax.rem(step + 3 * (plane + 2), heads), qs_ref, buf_ref, fs, fr)
            return carry

        lax.fori_loop(0, heads, send_block, 0)

    def send_head(which, source, target, send_sem, recv_sem):
        goal = head_owner(which)

        @pl.when(goal != me)
        def _():
            remote(
                source.at[which], target.at[me], send_sem.at[which], recv_sem.at[me], ctx=goal
            ).start()

        @pl.when(goal == me)
        def _():
            pltpu.make_async_copy(source.at[which], target.at[me], recv_sem.at[me]).start()

    pl.run_scoped(
        opening,
        pltpu.VMEM((width // 2, 4 * width), jnp.bfloat16),
        pltpu.VMEM((BLOCK, width), jnp.bfloat16),
    )

    def forward(pair_ref, low_ref):
        def value_of(key):
            ones = jnp.ones((16, BLOCK), jnp.bfloat16)
            return jnp.concatenate([buf_ref[key, 2 * HD :, :], ones], axis=0)

        def attend(group):
            first = 4 * group
            for inner in range(4):
                block = first + inner
                landed(buf_ref.at[block], fr.at[block])
                rows = pl.ds(pl.multiple_of(block * BLOCK, BLOCK), BLOCK)
                pair_ref[rows, :] = transposed(buf_ref[block, HD:, :])
            query = side_by_side(lambda block: buf_ref[block, :HD, :], first)
            query = jnp.concatenate([query, jnp.zeros_like(query)], axis=0)

            def step(state, key, count, skip):
                high, mixed = state
                rows = pl.ds(pl.multiple_of(key * BLOCK, BLOCK), count * BLOCK)
                begin = (skip or 0) * BLOCK
                scores = product(pair_ref[rows, :], query[:, begin:])
                if skip is not None:
                    scores = jnp.where(seen(scores.shape), scores, masked_score)
                new_high = jnp.maximum(high[:, begin:], jnp.max(scores, axis=0, keepdims=True))
                weights = jnp.exp(scores - new_high).astype(jnp.bfloat16)
                values = jnp.concatenate([value_of(key + index) for index in range(count)], axis=1)
                new_mixed = mixed[:, begin:] * jnp.exp(high[:, begin:] - new_high) + product(
                    values, weights
                )
                if begin:
                    new_high = jnp.concatenate([high[:, :begin], new_high], axis=1)
                    new_mixed = jnp.concatenate([mixed[:, :begin], new_mixed], axis=1)
                return new_high, new_mixed

            state = (
                jnp.full((1, 4 * BLOCK), masked_score, jnp.float32),
                jnp.zeros((HD + 16, 4 * BLOCK), jnp.float32),
            )
            state = lax.fori_loop(
                0, group, lambda index, now: step(now, 4 * index, 4, None), state
            )
            state = step(state, first, 2, 0)
            high, mixed = step(state, first + 2, 2, 2)
            total = mixed[HD : HD + 1]
            mixed = mixed[:HD] / total
            lse = high + jnp.log(total)
            for inner in range(4):
                block = first + inner
                cols = slice(inner * BLOCK, (inner + 1) * BLOCK)
                mix_ref[block] = mixed[:, cols]
                low_ref[block] = mixed[:, cols].astype(jnp.bfloat16)
                lse_ref[block] = jnp.broadcast_to(lse[:, cols], (8, BLOCK))
                return_block(me, head, block, low_ref, att_ref, fbs, fbr)

        def visit(group, carry):
            @pl.when(owner)
            def _():
                attend(group)

            for when in range(2):
                @pl.when(group == when)
                def _(when=when):
                    pass_on(3 + when)

            return carry

        lax.fori_loop(0, blocks // 4, visit, 0)
        pass_on(5)

        @pl.when(owner)
        def _():
            return_sent(me, head, blocks, low_ref, att_ref, fbs, fbr)

        scatter_sent(me, heads, qs_ref, buf_ref, fs, fr)
        wait_heads(heads, att_ref, fbr)

    pl.run_scoped(
        forward,
        pltpu.VMEM((blocks * BLOCK, 2 * HD), jnp.bfloat16),
        pltpu.VMEM((blocks, HD, BLOCK), jnp.bfloat16),
    )

    span = width // 2
    mine = pl.ds(pl.multiple_of(core * span, 128), span)
    theirs = pl.ds(pl.multiple_of((1 - core) * span, 128), span)
    deep = width // 2
    half_deep = deep // 2
    small = half_deep // planes

    def part_of(unit, half, cols):
        return parts.at[unit, half, :, cols]

    def qkv_part(unit, half, cols):
        return wd.at[pl.ds(pl.multiple_of(((unit - 9) * 2 + half) * deep, 16), deep), cols]

    def sib_of(unit, half):
        return sib_ref.at[unit, half]

    def qkv_sib(unit, half):
        cols = pl.ds(pl.multiple_of(((unit - 9) * 2 + half) * span, 128), span)
        return wu.at[pl.ds(0, deep), cols]

    def pipeline(part, sib):
        def to_sibling(unit):
            return [
                remote(part(unit, half, theirs), sib(unit, half),
                       s_sib.at[unit, half], r_sib.at[unit, half], ctx=sibling)
                for half in range(2)
            ]

        def to_row(unit):
            return [remote(sib(unit, other), row_ref.at[unit],
                           s_row.at[unit], r_row.at[unit], fsdp=other)]

        def to_x(unit):
            rows = pl.ds(pl.multiple_of((1 - xbit) * half_deep, 16), half_deep)
            return [remote(row_ref.at[unit, rows], x_ref.at[unit],
                           s_x.at[unit], r_x.at[unit], ctx=chip_next)]

        def to_z(unit):
            copies = []
            for step in range(1, planes):
                goal = lax.rem(plane + step, planes)
                rows = pl.ds(pl.multiple_of(goal * small, 16), small)
                copies.append(
                    remote(x_ref.at[unit, rows], z_ref.at[unit - 9, step - 1],
                           s_z.at[unit, step - 1], r_z.at[unit, step - 1], ctx=4 * goal + piece)
                )
            return copies

        def slab(unit, which):
            rows = pl.ds(pl.multiple_of(xbit * half_deep + which * small, 16), small)
            return res_ref.at[unit, rows, mine]

        def along_z(unit):
            return [
                remote(slab(unit, plane), slab(unit, plane),
                       s_az.at[unit, step - 1], r_az.at[unit, step - 1],
                       ctx=4 * lax.rem(plane + step, planes) + piece)
                for step in range(1, planes)
            ]

        def along_x(unit):
            rows = pl.ds(pl.multiple_of(xbit * half_deep, 16), half_deep)
            ref = res_ref.at[unit, rows, mine]
            return [remote(ref, ref, s_ax.at[unit], r_ax.at[unit], ctx=chip_next)]

        def along_s(unit):
            ref = res_ref.at[unit, :, mine]
            return [remote(ref, ref, s_as.at[unit], r_as.at[unit], ctx=sibling)]

        def launch(copies):
            for copy in copies:
                copy.start()

        def write_out(unit, which, cols):
            side = core if which == 0 else 1 - core
            kind = lax.rem(unit, 4)
            order = 2 * (unit // 4) + lax.rem(kind, 2)

            def save(target):
                pltpu.make_async_copy(
                    res_ref.at[unit, :, cols], target, out_sem.at[unit, which]
                ).start()

            @pl.when((unit < 8) & (kind < 2))
            def _():
                save(og_down.at[pl.ds(pl.multiple_of(order * deep, 16), deep),
                                pl.ds(pl.multiple_of(side * span, 128), span)])

            @pl.when((unit < 8) & (kind >= 2))
            def _():
                start = side * 4 * span + order * span
                save(og_up.at[:, pl.ds(pl.multiple_of(start, 128), span)])

            @pl.when(unit == 8)
            def _():
                save(og_out.at[:, pl.ds(pl.multiple_of(side * span, 128), span)])

            @pl.when(unit > 8)
            def _():
                start = (unit - 9) * width + side * span
                save(og_qkv.at[:, pl.ds(pl.multiple_of(start, 128), span)])

        def stage0(unit):
            launch(to_sibling(unit))

        def stage1(unit):
            for half in range(2):
                landed(sib(unit, half), r_sib.at[unit, half])
                ref, part_ref = sib(unit, half), part(unit, half, mine)

                def put(spot, value, ref=ref):
                    ref[spot, :] = value

                add_into(put, lambda spot, ref=ref: ref[spot, :],
                         lambda spot, part_ref=part_ref: part_ref[spot, :], deep)
            launch(to_row(unit))

        def stage2(unit):
            landed(row_ref.at[unit], r_row.at[unit])
            ref = sib(unit, row)

            def put(spot, value):
                row_ref[unit, spot, :] = value

            add_into(put, lambda spot: row_ref[unit, spot, :], lambda spot: ref[spot, :], deep)
            launch(to_x(unit))
            for make in (to_sibling, to_row):
                for copy in make(unit):
                    copy.wait_send()

        def stage3(unit):
            landed(x_ref.at[unit], r_x.at[unit])
            ref = row_ref.at[unit, pl.ds(pl.multiple_of(xbit * half_deep, 16), half_deep)]

            def put(spot, value):
                x_ref[unit, spot, :] = value

            add_into(put, lambda spot: x_ref[unit, spot, :], lambda spot: ref[spot, :], half_deep)

        def stage3_direct(unit):
            stage3(unit)
            launch(to_z(unit))

        def stage4(unit):
            rows = pl.ds(pl.multiple_of(plane * small, 16), small)
            total = x_ref[unit, rows, :].astype(jnp.float32)
            for step in range(1, planes):
                landed(z_ref.at[unit - 9, step - 1], r_z.at[unit, step - 1])
                total += z_ref[unit - 9, step - 1].astype(jnp.float32)
            spots = pl.ds(pl.multiple_of(xbit * half_deep + plane * small, 16), small)
            res_ref[unit, spots, mine] = total.astype(jnp.bfloat16)
            launch(along_z(unit))

        def stage5(unit):
            for step in range(1, planes):
                landed(slab(unit, lax.rem(plane + planes - step, planes)), r_az.at[unit, step - 1])
            launch(along_x(unit))

        def stage6(unit):
            rows = pl.ds(pl.multiple_of((1 - xbit) * half_deep, 16), half_deep)
            landed(res_ref.at[unit, rows, mine], r_ax.at[unit])
            launch(along_s(unit))
            write_out(unit, 0, mine)

        line_rows = half_deep // 2

        def line_spots(way):
            return pl.ds(way * line_rows, line_rows)

        def line_slab(unit, way):
            rows = pl.ds(pl.multiple_of(xbit * half_deep + way * line_rows, 16), line_rows)
            return res_ref.at[unit, rows, mine]

        def line_sum(unit, way):
            goal = me - 4 if way == 0 else me + 4
            return remote(x_ref.at[unit, line_spots(way)], line_ref.at[unit, way],
                          s_z.at[unit, way], r_z.at[unit, way], ctx=goal)

        def line_back(unit, way):
            goal = me + 4 if way == 0 else me - 4
            return remote(line_slab(unit, way), line_slab(unit, way),
                          s_az.at[unit, way], r_az.at[unit, way], ctx=goal)

        def line_place(way):
            return planes - 1 - plane if way == 0 else plane

        def line_add(unit, way):
            landed(line_ref.at[unit, way], r_z.at[unit, way])
            total = x_ref[unit, line_spots(way), :].astype(jnp.float32)
            return (total + line_ref[unit, way].astype(jnp.float32)).astype(jnp.bfloat16)

        def towards(hop):
            def stage(unit):
                if hop == 0:
                    stage3(unit)
                for way in range(2):
                    @pl.when(line_place(way) == hop)
                    def _(way=way):
                        if hop == planes - 1:
                            line_slab(unit, way)[...] = line_add(unit, way)
                            line_back(unit, way).start()
                            return
                        if hop:
                            x_ref[unit, line_spots(way), :] = line_add(unit, way)
                        line_sum(unit, way).start()

            return stage

        def homewards(hop):
            def stage(unit):
                for way in range(2):
                    @pl.when(line_place(way) == planes - 1 - hop)
                    def _(way=way):
                        landed(line_slab(unit, way), r_az.at[unit, way])
                        if hop < planes - 1:
                            line_back(unit, way).start()

                if hop == planes - 1:
                    launch(along_x(unit))

            return stage

        def close(unit):
            landed(res_ref.at[unit, :, theirs], r_as.at[unit])
            write_out(unit, 1, theirs)
            for make in (to_x, along_x, along_s):
                for copy in make(unit):
                    copy.wait_send()

        def line_close(unit):
            close(unit)
            for way in range(2):
                @pl.when(line_place(way) < planes - 1)
                def _(way=way):
                    line_sum(unit, way).wait_send()

                @pl.when(line_place(way) > 0)
                def _(way=way):
                    line_back(unit, way).wait_send()

        def stage7(unit):
            close(unit)
            for make in (to_z, along_z):
                for copy in make(unit):
                    copy.wait_send()

        line = [towards(hop) for hop in range(planes)]
        line += [homewards(hop) for hop in range(1, planes)]
        direct = [stage3_direct, stage4, stage5, stage6, stage7]
        return stage0, stage1, stage2, line + [stage6, line_close], direct

    early = pipeline(part_of, sib_of)
    late = pipeline(qkv_part, qkv_sib)

    def tick(time, carry):
        @pl.when((time >= 0) & (time < 9))
        def _():
            early[2](time)

        @pl.when((time >= 9) & (time < 12))
        def _():
            late[2](time)

        for lag, stage in enumerate(early[3]):
            unit = time - lag - 1

            @pl.when((unit >= 0) & (unit < 9))
            def _(stage=stage, unit=unit):
                stage(unit)

        for lag, stage in enumerate(late[4]):
            unit = time - lag - 1

            @pl.when((unit >= 9) & (unit < 12))
            def _(stage=stage, unit=unit):
                stage(unit)

        return carry

    def begin(stages, first, last):
        def one(unit, carry):
            stages[1](unit)
            return carry

        lax.fori_loop(first, last, one, 0)

    def ticks(first, last):
        lax.fori_loop(first, last, tick, 0)

    def middle_part(act_ref, slope_ref, hid2, hid2_t, low_ref):
        acc_ref = ingrad_ref
        own_copy(1).wait()
        chunk_done(3)
        att_t = att_ref[...].reshape(width, BLOCK)
        ap_ref[...] = product(transposed(att_t), wo[...])
        gate_attn = mod_ref[:1, width : 2 * width]
        scale_mlp = mod_ref[:1, 2 * width : 3 * width]
        gate_mlp = mod_ref[:1, 3 * width :]
        mid_ref[...] = tok_ref[...].astype(jnp.float32) + gate_attn * ap_ref[...]
        normed, unused = layer_norm(mid_ref[...])
        low = (normed * (1.0 + scale_mlp)).astype(jnp.bfloat16)
        hid2[...] = low
        hid2_t[...] = transposed(low)
        acc_ref[...] = jnp.zeros_like(acc_ref)
        own_copy(2).wait()
        chunk_done(4)
        own_copy(3).wait()
        chunk_done(5)
        curve = math.sqrt(2.0 / math.pi)

        def up(index, carry):
            cols = pl.ds(pl.multiple_of(index * width, width), width)
            before = product(hid2[...], wu[:, cols])
            square = before * before
            bent = jnp.tanh(curve * (before + 0.044715 * (square * before)))
            after = (0.5 * before * (1.0 + bent)).astype(jnp.bfloat16)
            act_ref[:, cols] = after
            slope_ref[:, cols] = 0.5 * (1.0 + bent) + 0.5 * before * (1.0 - bent * bent) * (
                curve * (1.0 + 3.0 * 0.044715 * square)
            )
            acc_ref[...] += product(after, wd[cols, :])
            return carry

        lax.fori_loop(0, 4, up, 0)
        grad = cot_ref[...].astype(jnp.float32)
        mlp_out = acc_ref[...]
        result_ref[...] = mid_ref[...] + gate_mlp * mlp_out
        sums_ref[3:4, :] = jnp.sum(grad * mlp_out, axis=0, keepdims=True)
        low_ref[...] = (grad * gate_mlp).astype(jnp.bfloat16)
        acc_ref[...] = jnp.zeros_like(acc_ref)

        def down(index, carry):
            for side in range(2):
                cols = pl.ds(pl.multiple_of(side * 2 * width + index * width, width), width)
                grad_act = product_back(low_ref[...], wd[cols, :])
                grad_pre = (grad_act * slope_ref[:, cols]).astype(jnp.bfloat16)
                grad_down = product(transposed(act_ref[:, cols]), low_ref[...])
                for pick in range(2):
                    parts[4 * index + pick, side] = grad_down[
                        pick * deep : (pick + 1) * deep
                    ].astype(jnp.bfloat16)
                grad_up = product(hid2_t[...], grad_pre).astype(jnp.bfloat16)
                for pick in range(2):
                    for half in range(2):
                        parts[4 * index + 2 + pick, half, :, side * span : (side + 1) * span] = (
                            grad_up[half * deep : (half + 1) * deep, pick * span : (pick + 1) * span]
                        )
                acc_ref[...] += product_back(grad_pre, wu[:, cols])
            for pick in range(4):
                early[0](4 * index + pick)
            begin(early, 0, 4 * index)
            return carry

        lax.fori_loop(0, 2, down, 0)
        for index in range(len(chunks)):
            chunk_sent(index)
        pl.semaphore_signal(free_sem, inc=1, device_id={"ctx": sibling}, device_id_type=MESH)
        grad_hidden = acc_ref[...]
        normed, inverse = layer_norm(mid_ref[...])
        sums_ref[2:3, :] = jnp.sum(grad_hidden * normed, axis=0, keepdims=True)
        grad_mid = cot_ref[...].astype(jnp.float32) + norm_back(
            grad_hidden * (1.0 + scale_mlp), normed, inverse
        )
        ingrad_ref[...] = grad_mid
        sums_ref[1:2, :] = jnp.sum(grad_mid * ap_ref[...], axis=0, keepdims=True)
        gap = (grad_mid * gate_attn).astype(jnp.bfloat16)
        low_ref[...] = gap
        douts_ref[...] = product_back(wo[...], gap).astype(jnp.bfloat16).reshape(
            heads, HD, BLOCK
        )

        def send_dout(step, carry):
            send_head(lax.rem(step + 3 * (plane + 2), heads), douts_ref, got_ref, bs, br)
            return carry

        lax.fori_loop(0, heads, send_dout, 0)
        begin(early, 4, 8)
        grad_out = product(att_ref[...].reshape(width, BLOCK), low_ref[...]).astype(jnp.bfloat16)
        parts[8, 0] = grad_out[:deep]
        parts[8, 1] = grad_out[deep:]
        early[0](8)
        begin(early, 8, 9)
        ticks(0, FIRST_TICKS)

    pl.run_scoped(
        middle_part,
        pltpu.VMEM((BLOCK, 4 * width), jnp.bfloat16),
        pltpu.VMEM((BLOCK, 4 * width), jnp.float32),
        pltpu.VMEM((BLOCK, width), jnp.bfloat16),
        pltpu.VMEM((width, BLOCK), jnp.bfloat16),
        pltpu.VMEM((BLOCK, width), jnp.bfloat16),
    )

    def backward(both_ref, side_ref, grad_ref, lse_wide, delta_wide, low_ref):
        @pl.when(owner)
        def _():
            def prepare(group, carry):
                first = 4 * group
                for inner in range(4):
                    landed(got_ref.at[first + inner], br.at[first + inner])
                dout = side_by_side(lambda block: got_ref[block], first)
                query = side_by_side(lambda block: buf_ref[block, :HD, :], first)
                mixed = side_by_side(lambda block: mix_ref[block], first)
                both = jnp.concatenate([query, dout], axis=0)
                both_ref[group] = both
                side_ref[group] = transposed(both)
                grad_ref[group] = jnp.zeros((HD, 4 * BLOCK), jnp.float32)
                lse_wide[group] = side_by_side(lambda block: lse_ref[block], first)
                delta = jnp.sum(dout.astype(jnp.float32) * mixed, axis=0, keepdims=True)
                delta_wide[group] = jnp.broadcast_to(delta, (8, 4 * BLOCK))
                return carry

            lax.fori_loop(0, blocks // 4, prepare, 0)

        def key_back(group, inner):
            key = 4 * group + inner
            pair = transposed(buf_ref[key, HD:, :])
            left = lax.broadcasted_iota(jnp.int32, pair.shape, 1) < HD
            none = jnp.zeros_like(pair)
            key_side, value_side = jnp.where(left, pair, none), jnp.where(left, none, pair)
            key_low = buf_ref[key, HD : 2 * HD, :]

            def visit_queries(which, skip, state):
                begin = skip * BLOCK
                both = both_ref[which, :, begin:]
                probs = jnp.exp(product(key_side, both) - lse_wide[which, :1, begin:])
                grad_scores = (
                    probs * (product(value_side, both) - delta_wide[which, :1, begin:])
                ).astype(jnp.bfloat16)
                side = side_ref[which, begin:, :]
                grad_ref[which, :, begin:] += product(key_low, grad_scores)
                return (
                    state[0] + product(grad_scores, side),
                    state[1] + product(probs.astype(jnp.bfloat16), side),
                )

            zero = jnp.zeros((BLOCK, 2 * HD), jnp.float32)
            state = visit_queries(group, inner, (zero, zero))
            state = lax.fori_loop(
                group + 1, blocks // 4, lambda which, now: visit_queries(which, 0, now), state
            )
            low_ref[key, HD : 2 * HD, :] = jnp.transpose(state[0])[:HD].astype(jnp.bfloat16)
            low_ref[key, 2 * HD :, :] = jnp.transpose(state[1])[HD:].astype(jnp.bfloat16)
            return_rows(key, HD, 2 * HD, 0)

        def part_copy_of(block, first, count, slot):
            return remote(
                low_ref.at[block, pl.ds(first, count)], gland_ref.at[head, pl.ds(first, count)],
                bbs.at[block, slot], bbr.at[head, slot], ctx=block,
            )

        def return_rows(block, first, count, slot):
            @pl.when(block != me)
            def _():
                part_copy_of(block, first, count, slot).start()

            @pl.when(block == me)
            def _():
                pltpu.make_async_copy(
                    low_ref.at[block, pl.ds(first, count)],
                    gland_ref.at[head, pl.ds(first, count)],
                    bbr.at[head, slot],
                ).start()

        def visit(step, carry):
            for inner in range(4):
                for edge in range(len(SPLITS) - 1):
                    @pl.when(owner & (step == (len(SPLITS) - 1) * inner + edge))
                    def _(inner=inner, edge=edge):
                        def one(group, carry):
                            key_back(group, inner)
                            return carry

                        lax.fori_loop(SPLITS[edge], SPLITS[edge + 1], one, 0)

            low = sum(jnp.where(step > index, count, 0) for index, count in enumerate(TICKS))
            high = sum(jnp.where(step >= index, count, 0) for index, count in enumerate(TICKS))
            ticks(low + FIRST_TICKS, high + FIRST_TICKS)

            @pl.when(owner & (step == len(TICKS) - 2))
            def _():
                finish_queries()

            return carry

        def finish_queries():
            def finish_query(group, carry):
                grad_query = (grad_ref[group] * score_scale).astype(jnp.bfloat16)
                for inner in range(4):
                    block = 4 * group + inner
                    low_ref[block, :HD, :] = grad_query[:, inner * BLOCK : (inner + 1) * BLOCK]
                    return_rows(block, 0, HD, 1)
                return carry

            lax.fori_loop(0, blocks // 4, finish_query, 0)

        lax.fori_loop(0, len(TICKS), visit, 0)

        @pl.when(owner)
        def _():
            def sent(block, carry):
                @pl.when(block != me)
                def _():
                    part_copy_of(block, HD, 2 * HD, 0).wait_send()
                    part_copy_of(block, 0, HD, 1).wait_send()

                return carry

            lax.fori_loop(0, blocks, sent, 0)

        scatter_sent(me, heads, douts_ref, got_ref, bs, br)

        def arrived(which, carry):
            landed(gland_ref.at[which, pl.ds(HD, 2 * HD)], bbr.at[which, 0])
            landed(gland_ref.at[which, pl.ds(0, HD)], bbr.at[which, 1])
            return carry

        lax.fori_loop(0, heads, arrived, 0)

    pl.run_scoped(
        backward,
        pltpu.VMEM((blocks // 4, 2 * HD, 4 * BLOCK), jnp.bfloat16),
        pltpu.VMEM((blocks // 4, 4 * BLOCK, 2 * HD), jnp.bfloat16),
        pltpu.VMEM((blocks // 4, HD, 4 * BLOCK), jnp.float32),
        pltpu.VMEM((blocks // 4, 8, 4 * BLOCK), jnp.float32),
        pltpu.VMEM((blocks // 4, 8, 4 * BLOCK), jnp.float32),
        pltpu.VMEM((blocks, 3 * HD, BLOCK), jnp.bfloat16),
    )

    def closing(gproj, acc_ref):
        def turn_back(group, carry):
            cos, sin = cos_ref[...], sin_ref[...]
            for kind in range(3):
                pieces = []
                for inner in range(4):
                    which = group * 4 + inner
                    if kind == 2:
                        pieces.append(gland_ref[which, 2 * HD :, :])
                        continue
                    top = gland_ref[which, kind * HD : kind * HD + HD // 2, :].astype(jnp.float32)
                    bottom = gland_ref[
                        which, kind * HD + HD // 2 : (kind + 1) * HD, :
                    ].astype(jnp.float32)
                    pieces.append((top * cos + bottom * sin).astype(jnp.bfloat16))
                    pieces.append((bottom * cos - top * sin).astype(jnp.bfloat16))
                cols = pl.ds(pl.multiple_of(kind * width + group * 4 * HD, 4 * HD), 4 * HD)
                gproj[:, cols] = transposed(jnp.concatenate(pieces, axis=0))
            return carry

        lax.fori_loop(0, heads // 4, turn_back, 0)
        acc_ref[...] = jnp.zeros_like(acc_ref)
        pl.semaphore_wait(free_sem, 1)

        def gradient(index, carry):
            cols = pl.ds(pl.multiple_of(index * width, width), width)
            low = product(hid1_t[...], gproj[:, cols]).astype(jnp.bfloat16)
            wd[pl.ds(pl.multiple_of(index * width, width), width), :] = low
            late[0](9 + index)
            return carry

        lax.fori_loop(0, 3, gradient, 0)

        def back(index, carry):
            cols = pl.ds(pl.multiple_of(index * width, width), width)
            acc_ref[...] += product_back(gproj[:, cols], wq[:, cols])
            return carry

        begin(late, 9, 12)
        lax.fori_loop(0, 3, back, 0)
        normed, inverse = layer_norm(tok_ref[...].astype(jnp.float32))
        grad_hidden = acc_ref[...]
        sums_ref[0:1, :] = jnp.sum(grad_hidden * normed, axis=0, keepdims=True)
        ingrad_ref[...] = ingrad_ref[...] + norm_back(
            grad_hidden * (1.0 + mod_ref[:1, :width]), normed, inverse
        )

    pl.run_scoped(
        closing,
        pltpu.VMEM((BLOCK, 3 * width), jnp.bfloat16),
        pltpu.VMEM((BLOCK, width), jnp.float32),
    )

    def slots(first, count):
        return table_ref.at[pl.ds(first, count)]

    chip_slot = core * 4 * planes + 4 * plane

    def table_row():
        ref = slots(chip_slot + 2 * xbit + row, 1)
        return [remote(ref, ref, s_t.at[0], r_t.at[0], fsdp=other)]

    def table_x():
        ref = slots(chip_slot + 2 * xbit, 2)
        return [remote(ref, ref, s_t.at[1], r_t.at[1], ctx=chip_next)]

    def table_z():
        ref = slots(chip_slot, 4)
        return [
            remote(ref, ref, s_t.at[2 + step], r_t.at[2 + step],
                   ctx=4 * lax.rem(plane + step, planes) + piece)
            for step in range(1, planes)
        ]

    def table_s():
        ref = slots(core * 4 * planes, 4 * planes)
        return [remote(ref, ref, s_t.at[2], r_t.at[2], ctx=sibling)]

    spot = chip_slot + 2 * xbit + row
    for index in range(4):
        table_ref[spot, index : index + 1, :] = sums_ref[index : index + 1, :]
    table_ref[spot, 4:5, :] = emb_ref[:1, :]
    for copy in table_row():
        copy.start()

    begun = FIRST_TICKS + sum(TICKS)

    def finish(time, carry):
        tick(time, carry)

        @pl.when(time == begun + 1)
        def _():
            landed(slots(chip_slot + 2 * xbit + other, 1), r_t.at[0])
            for copy in table_x():
                copy.start()

        @pl.when(time == begun + 3)
        def _():
            landed(slots(chip_slot + 2 * (1 - xbit), 2), r_t.at[1])
            for copy in table_z():
                copy.start()

        @pl.when(time == begun + 5)
        def _():
            for step in range(1, planes):
                goal = lax.rem(plane + planes - step, planes)
                landed(slots(core * 4 * planes + 4 * goal, 4), r_t.at[2 + step])
            for copy in table_s():
                copy.start()

        return carry

    lax.fori_loop(begun, 9 + len(early[3]), finish, 0)
    landed(slots((1 - core) * 4 * planes, 4 * planes), r_t.at[2])
    count = 2 * blocks
    emb_cols = pl.ds(pl.multiple_of(row * (width // 2), 128), width // 2)
    eds = table_ref[:, 4, emb_cols].astype(jnp.bfloat16)
    for third_part in range(3):
        eds_ref[third_part * count : (third_part + 1) * count, :] = eds
    for index in range(4):
        left = table_ref[:, index, :]
        for third_part in range(3):
            low = left.astype(jnp.bfloat16)
            left = left - low.astype(jnp.float32)
            sds_ref[
                third_part * count : (third_part + 1) * count, index * width : (index + 1) * width
            ] = low
    for copies in (table_row(), table_x(), table_z(), table_s()):
        for copy in copies:
            copy.wait_send()

    def saved(unit, carry):
        for which in range(2):
            pltpu.make_async_copy(
                res_ref.at[unit, :, pl.ds(0, span)], og_out.at[:, pl.ds(0, span)],
                out_sem.at[unit, which],
            ).wait()
        return carry

    lax.fori_loop(0, 12, saved, 0)


def side_by_side(pick, first):
    return jnp.concatenate([pick(first + inner) for inner in range(4)], axis=1)


def seen(shape):
    keys = lax.broadcasted_iota(jnp.int32, shape, 0) // BLOCK
    return keys <= lax.broadcasted_iota(jnp.int32, shape, 1) // BLOCK


FIRST_TICKS = 1
TICKS = (1, 1, 1, 1, 1, 0, 1, 0, 2)
SPLITS = (0, 1, 4)


def rope_constants(blocks):
    half = HD // 2
    frequency = rope_base ** (-2.0 * np.arange(half, dtype=np.float64) / HD)
    inner = frequency[:, None] * np.arange(BLOCK, dtype=np.float64)[None, :]
    outer = frequency[:, None] * (BLOCK * np.arange(128, dtype=np.float64))[None, :]
    outer = np.where(np.arange(128)[None, :] < blocks, outer, 0.0)
    return np.concatenate(
        [np.cos(inner), np.sin(inner), np.cos(outer), np.sin(outer)], axis=1
    ).astype(np.float32)


def fast_device(tokens, timestep, time_table, w_qkv, w_out, w_up, w_down, w_ada, cotangent):
    rows, width = tokens.shape[1:]
    heads = width // HD
    blocks = lax.axis_size("ctx")
    planes = blocks // 4
    deep, span = width // 2, width // 2
    embedded = lax.dynamic_slice_in_dim(time_table, timestep[0, 0], 1, 0)
    embedded = embedded.astype(jnp.bfloat16).astype(jnp.float32)
    emb_rows = jnp.broadcast_to(embedded, (8, width))
    hbm = pl.BlockSpec(memory_space=pl.ANY)
    vmem = pl.BlockSpec(memory_space=pltpu.VMEM)
    low, high = jnp.bfloat16, jnp.float32
    dma = pltpu.SemaphoreType.DMA
    steps = planes - 1
    units = 12
    scratch = [
        pltpu.VMEM((width, 3 * width), low),
        pltpu.VMEM((width, width), low),
        pltpu.VMEM((width, 4 * width), low),
        pltpu.VMEM((4 * width, width), low),
        pltpu.VMEM((8, 4 * width), high),
        pltpu.VMEM((8, width), high),
        pltpu.VMEM((8, 4 * width), high),
        pltpu.VMEM((8, 4 * width), high),
        pltpu.VMEM((width, BLOCK), low),
        pltpu.VMEM((BLOCK, width), high),
        pltpu.VMEM((BLOCK, width), high),
        pltpu.VMEM((8, width), high),
        pltpu.VMEM((HD // 2, BLOCK), high),
        pltpu.VMEM((HD // 2, BLOCK), high),
        pltpu.VMEM((heads, 3 * HD, BLOCK), low),
        pltpu.VMEM((blocks, 3 * HD, BLOCK), low),
        pltpu.VMEM((blocks, HD, BLOCK), high),
        pltpu.VMEM((blocks, 8, BLOCK), high),
        pltpu.VMEM((heads, HD, BLOCK), low),
        pltpu.VMEM((heads, HD, BLOCK), low),
        pltpu.VMEM((blocks, HD, BLOCK), low),
        pltpu.VMEM((9, 2, deep, width), low),
        pltpu.VMEM((9, 2, deep, span), low),
        pltpu.VMEM((units, deep, span), low),
        pltpu.VMEM((units, deep // 2, span), low),
        pltpu.VMEM((3, steps, deep // 2 // planes, span), low),
        pltpu.VMEM((9, 2, deep // 4, span), low),
        pltpu.VMEM((units, deep, width), low),
        pltpu.VMEM((2 * blocks, 8, width), high),
    ]
    sems = [
        (5,), (2,), (2,), (6, 4), (6, 4),
        (heads,), (blocks,), (blocks,), (heads,),
        (heads,), (blocks,), (blocks, 2), (heads, 2),
        (units, 2), (units, 2), (units,), (units,), (units,), (units,),
        (units, steps), (units, steps), (units, steps), (units, steps),
        (units,), (units,), (units,), (units,), (planes + 2,), (planes + 2,), (units, 2),
    ]
    scratch += [dma(shape) for shape in sems] + [pltpu.SemaphoreType.REGULAR]
    result, input_grad, eds, sds, *sums = pl.pallas_call(
        functools.partial(layer_kernel, blocks, heads),
        out_shape=[
            jax.ShapeDtypeStruct((rows, width), high),
            jax.ShapeDtypeStruct((rows, width), high),
            jax.ShapeDtypeStruct((6 * blocks, deep), low),
            jax.ShapeDtypeStruct((6 * blocks, 4 * width), low),
        ]
        + [jax.ShapeDtypeStruct(w.shape, low) for w in (w_qkv, w_out, w_up, w_down)],
        in_specs=[vmem] * 4 + [hbm] * 5,
        out_specs=[vmem] * 4 + [hbm] * 4,
        scratch_shapes=scratch,
        compiler_params=pltpu.CompilerParams(
            collective_id=1, has_side_effects=True, vmem_limit_bytes=VMEM_LIMIT
        ),
    )(tokens[0], cotangent[0], emb_rows, jnp.asarray(rope_constants(blocks)),
      w_ada, w_qkv, w_out, w_up, w_down)
    ada_total = lax.dot_general(
        eds, sds, (((0,), (0,)), ((), ())), preferred_element_type=jnp.float32
    )
    return (result[None], input_grad[None], *[total.astype(high) for total in sums], ada_total)


def solution(mesh):
    chosen = fast_device if mesh.shape["ctx"] == 16 else on_device
    return jax.shard_map(
        chosen,
        mesh=mesh,
        in_specs=(
            P("fsdp", "ctx", None),
            P("fsdp", "ctx"),
            P(),
            P("fsdp", None),
            P("fsdp", None),
            P("fsdp", None),
            P("fsdp", None),
            P("fsdp", None),
            P("fsdp", "ctx", None),
        ),
        out_specs=(
            P("fsdp", "ctx", None),
            P("fsdp", "ctx", None),
            P("fsdp", None),
            P("fsdp", None),
            P("fsdp", None),
            P("fsdp", None),
            P("fsdp", None),
        ),
        check_vma=False,
    )
```

```python
import functools
import math

import jax
import jax.numpy as jnp
import numpy as np
from jax import lax
from jax.experimental import pallas as pl
from jax.experimental.pallas import tpu as pltpu
from jax.sharding import PartitionSpec as P

HD = 64
BLOCK = 256
VMEM_LIMIT = 65152 * 1024
MESH = pl.DeviceIdType.MESH


norm_eps = 1e-06
masked_score = -1e30
rope_base = 10000.0


def layer_norm(values):
    center = values - jnp.mean(values, axis=-1, keepdims=True)
    inverse = lax.rsqrt(jnp.mean(center * center, axis=-1, keepdims=True) + norm_eps)
    return (center * inverse, inverse)


def norm_back(grad_norm, normed, inverse):
    mean_grad = jnp.mean(grad_norm, axis=-1, keepdims=True)
    mean_cross = jnp.mean(grad_norm * normed, axis=-1, keepdims=True)
    return inverse * (grad_norm - mean_grad - normed * mean_cross)


def rope_tables(positions, head_size):
    half_size = head_size // 2
    frequency = jnp.exp(
        jnp.arange(half_size, dtype=jnp.float32) * (-2.0 * math.log(rope_base) / head_size)
    )
    angles = positions.astype(jnp.float32)[:, None] * frequency[None, :]
    cosine_table = jnp.concatenate([jnp.cos(angles), jnp.cos(angles)], axis=-1)[:, None, :]
    sine_table = jnp.concatenate([jnp.sin(angles), jnp.sin(angles)], axis=-1)[:, None, :]
    return (cosine_table, sine_table)


def rotate_half(values):
    middle = values.shape[-1] // 2
    return jnp.concatenate([-values[..., middle:], values[..., :middle]], axis=-1)


def rotate(values, cosine_table, sine_table):
    return values * cosine_table + rotate_half(values) * sine_table


def rotate_back(gradient, cosine_table, sine_table):
    return gradient * cosine_table - rotate_half(gradient * sine_table)


def gelu_tanh(values):
    return jax.nn.gelu(values, approximate=True)


def split_rows(array, sub_rows):
    return array.reshape((array.shape[0] // sub_rows, sub_rows) + array.shape[1:])


def part_starts(total_rows, sub_rows):
    return sub_rows * jnp.arange(total_rows // sub_rows, dtype=jnp.int32)


def keep_same(partial_value):
    return partial_value


def attend_forward(partial_value, pieces, queries, query_block, score_scale):
    key_rows, value_rows = pieces
    sub_rows = queries.shape[0]

    def attend_visit(running, scan_item):
        key_part, value_part, part_start = scan_item

        def attend_update(running):
            running_max, running_sum, running_out = running
            key_block = (part_start + jnp.arange(sub_rows, dtype=jnp.int32)) // BLOCK
            allowed = (key_block[None, :] <= query_block[:, None])[None]
            scores = (
                jnp.einsum("qhd,khd->hqk", queries, key_part, preferred_element_type=jnp.float32)
                * score_scale
            )
            scores = jnp.where(allowed, scores, masked_score)
            new_max = jnp.maximum(running_max, jnp.max(scores, axis=-1))
            weights = jnp.where(allowed, jnp.exp(scores - new_max[..., None]), 0.0)
            decay = jnp.exp(running_max - new_max)
            running_sum = running_sum * decay + jnp.sum(weights, axis=-1)
            running_out = running_out * decay[..., None] + jnp.einsum(
                "hqk,khd->hqd",
                weights.astype(jnp.bfloat16),
                value_part,
                preferred_element_type=jnp.float32,
            )
            return (new_max, running_sum, running_out)

        return (
            lax.cond(part_start // BLOCK <= query_block[-1], attend_update, keep_same, running),
            None,
        )

    partial_value, unused = lax.scan(
        attend_visit,
        partial_value,
        (
            split_rows(key_rows, sub_rows),
            split_rows(value_rows, sub_rows),
            part_starts(key_rows.shape[0], sub_rows),
        ),
    )
    return partial_value


def on_device(tokens, timestep, time_table, w_qkv, w_out, w_up, w_down, w_ada, cotangent):
    tok_rows = tokens.shape[1]
    model_width = tokens.shape[2]
    heads = model_width // HD
    score_scale = 1.0 / math.sqrt(HD)
    highest_precision = lax.Precision.HIGHEST
    full_weights = (
        lax.all_gather(w_qkv, "fsdp", axis=0, tiled=True),
        lax.all_gather(w_out, "fsdp", axis=0, tiled=True),
        lax.all_gather(w_up, "fsdp", axis=0, tiled=True),
        lax.all_gather(w_down, "fsdp", axis=0, tiled=True),
        lax.all_gather(w_ada, "fsdp", axis=0, tiled=True),
    )
    qkv_full, out_full, up_full, down_full, ada_full = full_weights
    steps_onehot = (
        timestep[0][:, None] == jnp.arange(time_table.shape[0], dtype=jnp.int32)[None, :]
    ).astype(jnp.float32)
    embedded = jnp.dot(steps_onehot, time_table, precision=highest_precision).astype(jnp.bfloat16)
    modulation = jnp.dot(embedded, ada_full, preferred_element_type=jnp.float32)
    per_token = jnp.repeat(modulation, BLOCK, axis=0)
    scale_attn, gate_attn, scale_mlp, gate_mlp = jnp.split(per_token, 4, axis=1)
    inputs = tokens[0].astype(jnp.float32)
    normed_one, inverse_one = layer_norm(inputs)
    residual_first = (normed_one * (1.0 + scale_attn)).astype(jnp.bfloat16)
    projected_output = jnp.dot(
        residual_first, qkv_full, preferred_element_type=jnp.float32
    ).reshape(tok_rows, 3, heads, HD)
    positions = lax.axis_index("ctx") * tok_rows + jnp.arange(tok_rows, dtype=jnp.int32)
    cosine_table, sine_table = rope_tables(positions, HD)
    queries = rotate(projected_output[:, 0], cosine_table, sine_table).astype(jnp.bfloat16)
    key_own = rotate(projected_output[:, 1], cosine_table, sine_table).astype(jnp.bfloat16)
    value_own = projected_output[:, 2].astype(jnp.bfloat16)
    query_block = positions // BLOCK
    start_state = (
        jnp.full((heads, tok_rows), masked_score, jnp.float32),
        jnp.zeros((heads, tok_rows), jnp.float32),
        jnp.zeros((heads, tok_rows, HD), jnp.float32),
    )
    running_max, running_sum, running_out = attend_forward(
        start_state,
        (
            lax.all_gather(key_own, "ctx", axis=0, tiled=True),
            lax.all_gather(value_own, "ctx", axis=0, tiled=True),
        ),
        queries,
        query_block,
        score_scale,
    )
    attn_rows = jnp.transpose(running_out / running_sum[..., None], (1, 0, 2))
    query_lse = running_max + jnp.log(running_sum)
    attn_low = attn_rows.reshape(tok_rows, model_width).astype(jnp.bfloat16)
    attention_projected = jnp.dot(attn_low, out_full, preferred_element_type=jnp.float32)
    middle = inputs + gate_attn * attention_projected
    normed_two, inverse_two = layer_norm(middle)
    residual_second = (normed_two * (1.0 + scale_mlp)).astype(jnp.bfloat16)
    before_activation = jnp.dot(residual_second, up_full, preferred_element_type=jnp.float32)
    gelu_activated, gelu_back = jax.vjp(gelu_tanh, before_activation)
    act_low = gelu_activated.astype(jnp.bfloat16)
    feedforward_output = jnp.dot(act_low, down_full, preferred_element_type=jnp.float32)
    result = middle + gate_mlp * feedforward_output
    qkv_back, out_back, up_back, down_back = (
        lax.all_gather(w_qkv, "fsdp", axis=0, tiled=True),
        lax.all_gather(w_out, "fsdp", axis=0, tiled=True),
        lax.all_gather(w_up, "fsdp", axis=0, tiled=True),
        lax.all_gather(w_down, "fsdp", axis=0, tiled=True),
    )
    upstream = cotangent[0].astype(jnp.float32)
    grad_gate_mlp = upstream * feedforward_output
    grad_mlp = (upstream * gate_mlp).astype(jnp.bfloat16)
    grad_down = jnp.einsum("tf,td->fd", act_low, grad_mlp, preferred_element_type=jnp.float32)
    grad_act = jnp.einsum("td,fd->tf", grad_mlp, down_back, preferred_element_type=jnp.float32)
    grad_pre = gelu_back(grad_act)[0].astype(jnp.bfloat16)
    grad_up = jnp.einsum("td,tf->df", residual_second, grad_pre, preferred_element_type=jnp.float32)
    grad_hidden_two = jnp.einsum("tf,df->td", grad_pre, up_back, preferred_element_type=jnp.float32)
    grad_scale_mlp = grad_hidden_two * normed_two
    grad_middle = upstream + norm_back(grad_hidden_two * (1.0 + scale_mlp), normed_two, inverse_two)
    grad_gate_attn = grad_middle * attention_projected
    grad_attn_proj = (grad_middle * gate_attn).astype(jnp.bfloat16)
    grad_out = jnp.einsum("td,te->de", attn_low, grad_attn_proj, preferred_element_type=jnp.float32)
    grad_attended = jnp.einsum(
        "te,de->td", grad_attn_proj, out_back, preferred_element_type=jnp.float32
    )
    grad_heads = grad_attended.astype(jnp.bfloat16).reshape(tok_rows, heads, HD)
    delta_rows = jnp.sum(grad_heads.astype(jnp.float32) * attn_rows, axis=-1)
    query_delta = jnp.transpose(delta_rows)
    lse_rows = jnp.transpose(query_lse)
    lse_high = lse_rows.astype(jnp.bfloat16)
    lse_rest = (lse_rows - lse_high.astype(jnp.float32)).astype(jnp.bfloat16)
    delta_high = delta_rows.astype(jnp.bfloat16)
    delta_rest = (delta_rows - delta_high.astype(jnp.float32)).astype(jnp.bfloat16)
    stat_rows = jnp.concatenate([lse_high, lse_rest, delta_high, delta_rest], axis=1)
    zero_heads = jnp.zeros((tok_rows, heads, HD), jnp.float32)
    partial_value = (zero_heads, zero_heads, zero_heads)
    grad_query = partial_value[0]
    key_rows = lax.all_gather(key_own, "ctx", axis=0, tiled=True)

    def query_visit(partial_value, scan_item):
        key_part, value_part, part_start = scan_item

        def query_update(partial_value):
            key_block = (part_start + jnp.arange(tok_rows, dtype=jnp.int32)) // BLOCK
            allowed = (key_block[None, :] <= query_block[:, None])[None]
            scores = (
                jnp.einsum("qhd,khd->hqk", queries, key_part, preferred_element_type=jnp.float32)
                * score_scale
            )
            probs = jnp.where(allowed, jnp.exp(scores - query_lse[..., None]), 0.0)
            grad_prob = jnp.einsum(
                "qhd,khd->hqk", grad_heads, value_part, preferred_element_type=jnp.float32
            )
            grad_score = (probs * (grad_prob - query_delta[..., None]) * score_scale).astype(
                jnp.bfloat16
            )
            return partial_value + jnp.einsum(
                "hqk,khd->qhd", grad_score, key_part, preferred_element_type=jnp.float32
            )

        return (
            lax.cond(
                part_start // BLOCK <= query_block[-1], query_update, keep_same, partial_value
            ),
            None,
        )

    grad_query, unused = lax.scan(
        query_visit,
        grad_query,
        (
            split_rows(key_rows, tok_rows),
            split_rows(lax.all_gather(value_own, "ctx", axis=0, tiled=True), tok_rows),
            part_starts(key_rows.shape[0], tok_rows),
        ),
    )
    key_partial_value = (partial_value[1], partial_value[2])
    query_rows = lax.all_gather(queries, "ctx", axis=0, tiled=True)

    def key_visit(running, scan_item):
        query_part, dout_part, stat_part, part_start = scan_item

        def key_update(running):
            grad_key, grad_value = running
            query_blk = (part_start + jnp.arange(tok_rows, dtype=jnp.int32)) // BLOCK
            allowed = (query_blk[:, None] >= query_block[None, :])[None]
            stat_float = stat_part.astype(jnp.float32)
            lse_part = jnp.transpose(stat_float[:, :heads] + stat_float[:, heads : 2 * heads])
            delta_part = jnp.transpose(
                stat_float[:, 2 * heads : 3 * heads] + stat_float[:, 3 * heads :]
            )
            scores = (
                jnp.einsum("qhd,khd->hqk", query_part, key_own, preferred_element_type=jnp.float32)
                * score_scale
            )
            probs = jnp.where(allowed, jnp.exp(scores - lse_part[..., None]), 0.0)
            grad_value = grad_value + jnp.einsum(
                "hqk,qhd->khd",
                probs.astype(jnp.bfloat16),
                dout_part,
                preferred_element_type=jnp.float32,
            )
            grad_prob = jnp.einsum(
                "qhd,khd->hqk", dout_part, value_own, preferred_element_type=jnp.float32
            )
            grad_score = (probs * (grad_prob - delta_part[..., None]) * score_scale).astype(
                jnp.bfloat16
            )
            grad_key = grad_key + jnp.einsum(
                "hqk,qhd->khd", grad_score, query_part, preferred_element_type=jnp.float32
            )
            return (grad_key, grad_value)

        last_seen = (part_start + tok_rows - 1) // BLOCK
        return (lax.cond(last_seen >= query_block[0], key_update, keep_same, running), None)

    key_partial_value, unused = lax.scan(
        key_visit,
        key_partial_value,
        (
            split_rows(query_rows, tok_rows),
            split_rows(lax.all_gather(grad_heads, "ctx", axis=0, tiled=True), tok_rows),
            split_rows(lax.all_gather(stat_rows, "ctx", axis=0, tiled=True), tok_rows),
            part_starts(query_rows.shape[0], tok_rows),
        ),
    )
    grad_key, grad_value = key_partial_value
    grad_query, grad_key, grad_value = (grad_query, grad_key, grad_value)
    grad_query = rotate_back(grad_query, cosine_table, sine_table)
    grad_key = rotate_back(grad_key, cosine_table, sine_table)
    grad_projected = (
        jnp.stack([grad_query, grad_key, grad_value], axis=1)
        .reshape(tok_rows, 3 * model_width)
        .astype(jnp.bfloat16)
    )
    grad_qkv = jnp.einsum(
        "td,te->de", residual_first, grad_projected, preferred_element_type=jnp.float32
    )
    grad_hidden_one = jnp.einsum(
        "te,de->td", grad_projected, qkv_back, preferred_element_type=jnp.float32
    )
    grad_scale_attn = grad_hidden_one * normed_one
    input_grad = grad_middle + norm_back(
        grad_hidden_one * (1.0 + scale_attn), normed_one, inverse_one
    )
    grad_modulation = jnp.concatenate(
        [grad_scale_attn, grad_gate_attn, grad_scale_mlp, grad_gate_mlp], axis=1
    )
    grad_blocks = jnp.sum(
        grad_modulation.reshape(tok_rows // BLOCK, BLOCK, 4 * model_width), axis=1
    )
    embedded_float = embedded.astype(jnp.float32)
    halves = (
        lax.psum_scatter(
            grad_qkv.astype(jnp.bfloat16), "fsdp", scatter_dimension=0, tiled=True
        ).astype(jnp.float32),
        lax.psum_scatter(
            grad_out.astype(jnp.bfloat16), "fsdp", scatter_dimension=0, tiled=True
        ).astype(jnp.float32),
        lax.psum_scatter(
            grad_up.astype(jnp.bfloat16), "fsdp", scatter_dimension=0, tiled=True
        ).astype(jnp.float32),
        lax.psum_scatter(
            grad_down.astype(jnp.bfloat16), "fsdp", scatter_dimension=0, tiled=True
        ).astype(jnp.float32),
    )
    totals = lax.psum((halves[0], halves[1], halves[2], halves[3]), "ctx")
    all_embedded, all_blocks = (
        lax.all_gather(embedded_float, ("ctx", "fsdp"), axis=0, tiled=True),
        lax.all_gather(grad_blocks, ("ctx", "fsdp"), axis=0, tiled=True),
    )
    shard_width = model_width // lax.axis_size("fsdp")
    row_start = lax.axis_index("fsdp") * shard_width
    embedded_part = lax.dynamic_slice_in_dim(all_embedded, row_start, shard_width, 1)
    ada_total = jnp.dot(jnp.transpose(embedded_part), all_blocks, precision=highest_precision)
    return (result[None], input_grad[None], totals[0], totals[1], totals[2], totals[3], ada_total)


def remote(source, target, send_sem, recv_sem, **where):
    return pltpu.make_async_remote_copy(
        src_ref=source,
        dst_ref=target,
        send_sem=send_sem,
        recv_sem=recv_sem,
        device_id=where,
        device_id_type=MESH,
    )


def landed(ref, sem):
    pltpu.make_async_copy(ref, ref, sem).wait()


def head_place(me):
    plane = me // 4
    spot = lax.rem(me, 4)
    odd = lax.rem(plane, 2)
    idle = 3 - 2 * odd
    head = 3 * plane + spot - odd * (spot // 2)
    return spot != idle, head


def head_owner(head):
    plane = head // 3
    rank = lax.rem(head, 3)
    odd = lax.rem(plane, 2)
    return 4 * plane + rank + odd * ((rank + 1) // 2)


def scatter_sent(me, heads, source, target, send_sem, recv_sem):
    def finish(head, carry):
        owner = head_owner(head)

        @pl.when(owner != me)
        def _():
            remote(
                source.at[head], target.at[me], send_sem.at[head], recv_sem.at[me], ctx=owner
            ).wait_send()

        return carry

    lax.fori_loop(0, heads, finish, 0)


def return_block(me, head, block, source, target, send_sem, recv_sem):
    @pl.when(block != me)
    def _():
        remote(
            source.at[block], target.at[head], send_sem.at[block], recv_sem.at[head], ctx=block
        ).start()

    @pl.when(block == me)
    def _():
        pltpu.make_async_copy(source.at[block], target.at[head], recv_sem.at[head]).start()


def return_sent(me, head, blocks, source, target, send_sem, recv_sem):
    def finish(block, carry):
        @pl.when(block != me)
        def _():
            remote(
                source.at[block], target.at[head], send_sem.at[block], recv_sem.at[head], ctx=block
            ).wait_send()

        return carry

    lax.fori_loop(0, blocks, finish, 0)


def wait_heads(heads, target, recv_sem):
    def finish(head, carry):
        landed(target.at[head], recv_sem.at[head])
        return carry

    lax.fori_loop(0, heads, finish, 0)


def transposed(values):
    return jnp.transpose(values.astype(jnp.float32)).astype(values.dtype)


def add_into(target, left, right, rows):
    step = 48

    def body(index, carry):
        spot = pl.ds(pl.multiple_of(index * step, step), step)
        total = left(spot).astype(jnp.float32) + right(spot).astype(jnp.float32)
        target(spot, total.astype(jnp.bfloat16))
        return carry

    lax.fori_loop(0, rows // step, body, 0)


def product(left, right):
    return jnp.dot(left, right, preferred_element_type=jnp.float32)


def product_back(left, right):
    return lax.dot_general(
        left, right, (((1,), (1,)), ((), ())), preferred_element_type=jnp.float32
    )


def layer_kernel(
    blocks, heads,
    tok_ref, cot_ref, emb_ref, rope_ref, ada_hbm, qkv_hbm, out_hbm, up_hbm, down_hbm,
    result_ref, ingrad_ref, eds_ref, sds_ref, og_qkv, og_out, og_up, og_down,
    wq, wo, wu, wd, mod_ref, emb_other, part_other, part_send,
    hid1_t, mid_ref, ap_ref, sums_ref, cos_ref, sin_ref,
    qs_ref, buf_ref, mix_ref, lse_ref, att_ref, douts_ref, got_ref,
    parts, sib_ref, row_ref, x_ref, z_ref, line_ref, res_ref, table_ref,
    own_sem, small_send, small_recv, w_send, w_recv,
    fs, fr, fbs, fbr, bs, br, bbs, bbr,
    s_sib, r_sib, s_row, r_row, s_x, r_x, s_z, r_z, s_az, r_az, s_ax, r_ax, s_as, r_as,
    s_t, r_t, out_sem, free_sem,
):
    me = lax.axis_index("ctx")
    row = lax.axis_index("fsdp")
    other = 1 - row
    piece = lax.rem(me, 4)
    core = lax.rem(me, 2)
    xbit = lax.rem(me // 2, 2)
    plane = me // 4
    planes = blocks // 4
    chip_next = jnp.bitwise_xor(me, 2)
    sibling = jnp.bitwise_xor(me, 1)
    gland_ref = qs_ref
    owner, head = head_place(me)
    width = tok_ref.shape[1]
    score_scale = 1.0 / math.sqrt(HD)

    barrier = pltpu.get_barrier_semaphore()
    pl.semaphore_signal(barrier, inc=1, device_id={"fsdp": other}, device_id_type=MESH)

    def greet(step, carry):
        pl.semaphore_signal(
            barrier, inc=1, device_id={"ctx": lax.rem(me + step, blocks)}, device_id_type=MESH
        )
        return carry

    lax.fori_loop(1, blocks, greet, 0)
    pl.semaphore_wait(barrier, blocks)

    shards = (qkv_hbm, out_hbm, up_hbm, down_hbm)
    wholes = (wq, wo, wu, wd)
    quarter_rows = [shard.shape[0] // 4 for shard in shards]
    third = quarter_rows[0] // 3
    chunks = [
        (0, 0, third),
        (0, third, third),
        (0, 2 * third, third),
        (1, 0, 2 * quarter_rows[1]),
        (2, 0, 2 * quarter_rows[2]),
        (3, 0, 2 * quarter_rows[3]),
    ]

    def chunk_start(index, half, which):
        weight, first, count = chunks[index]
        if index > 2:
            return pl.multiple_of(half * 2 * count + lax.rem(which, 2) * count, 16)
        return pl.multiple_of((half * 4 + which) * quarter_rows[weight] + first, 16)

    def chunk_ref(index, which):
        weight, first, count = chunks[index]
        return wholes[weight].at[pl.ds(chunk_start(index, other, which), count)]

    def y_copy(index):
        weight, first, count = chunks[index]
        return remote(
            shards[weight].at[pl.ds(chunk_start(index, 0, piece), count)],
            wholes[weight].at[pl.ds(chunk_start(index, row, piece), count)],
            w_send.at[index, 0], w_recv.at[index, 0], fsdp=other,
        )

    def onward(index, which, slot, peer):
        ref = chunk_ref(index, which)
        return remote(ref, ref, w_send.at[index, slot], w_recv.at[index, slot], ctx=peer)

    def pass_on(index):
        landed(chunk_ref(index, piece), w_recv.at[index, 0])
        if index < 3:
            onward(index, piece, 1, chip_next).start()
        onward(index, piece, 2, sibling).start()

    def pass_last(index):
        across = jnp.bitwise_xor(piece, 2)
        landed(chunk_ref(index, across), w_recv.at[index, 1])
        onward(index, across, 3, sibling).start()

    def chunk_done(index):
        landed(chunk_ref(index, jnp.bitwise_xor(piece, 1)), w_recv.at[index, 2])
        if index < 3:
            landed(chunk_ref(index, jnp.bitwise_xor(piece, 3)), w_recv.at[index, 3])

    def chunk_sent(index):
        y_copy(index).wait_send()
        onward(index, piece, 2, sibling).wait_send()
        if index < 3:
            onward(index, piece, 1, chip_next).wait_send()
            onward(index, jnp.bitwise_xor(piece, 2), 3, sibling).wait_send()

    def own_copy(weight):
        half = shards[weight].shape[0]
        start = pl.multiple_of(row * half, 16)
        return pltpu.make_async_copy(
            shards[weight], wholes[weight].at[pl.ds(start, half)], own_sem.at[weight]
        )

    emb_copy = remote(emb_ref, emb_other, small_send.at[0], small_recv.at[0], fsdp=other)
    emb_copy.start()
    for index in range(3):
        y_copy(index).start()

    def opening(ada_ref, hid1):
        ada_copy = pltpu.make_async_copy(ada_hbm, ada_ref, own_sem.at[4])
        ada_copy.start()
        for weight in range(4):
            own_copy(weight).start()
        normed, unused = layer_norm(tok_ref[...].astype(jnp.float32))
        ingrad_ref[...] = normed
        half_width = width // 2
        cols = pl.ds(pl.multiple_of(row * half_width, 128), half_width)
        ada_copy.wait()
        emb_copy.wait()
        both = jnp.concatenate([emb_ref[:, cols], emb_other[:, cols]], axis=0)
        partial = product(both.astype(jnp.bfloat16), ada_ref[...])
        mod_ref[...] = partial[:8]
        part_send[...] = partial[8:]
        part_copy = remote(part_send, part_other, small_send.at[1], small_recv.at[1], fsdp=other)
        part_copy.start()
        for index in (3, 4, 5):
            y_copy(index).start()
        pass_on(0)
        lanes = lax.broadcasted_iota(jnp.int32, (HD // 2, 128), 1)
        pick = lanes == me
        cos_block = jnp.sum(
            jnp.where(pick, rope_ref[:, 2 * BLOCK : 2 * BLOCK + 128], 0.0), axis=1, keepdims=True
        )
        sin_block = jnp.sum(
            jnp.where(pick, rope_ref[:, 2 * BLOCK + 128 :], 0.0), axis=1, keepdims=True
        )
        cos_row = rope_ref[:, :BLOCK]
        sin_row = rope_ref[:, BLOCK : 2 * BLOCK]
        cos_ref[...] = cos_row * cos_block - sin_row * sin_block
        sin_ref[...] = sin_row * cos_block + cos_row * sin_block
        part_copy.wait()
        mod_ref[...] += part_other[...]
        low = (ingrad_ref[...] * (1.0 + mod_ref[:1, :width])).astype(jnp.bfloat16)
        hid1[...] = low
        pass_on(1)
        hid1_t[...] = transposed(low)
        pass_on(2)
        for index in range(3):
            pass_last(index)
        own_copy(0).wait()
        for index in range(3):
            chunk_done(index)

        def project(group, carry):
            spans = []
            for kind in range(3):
                cols = pl.ds(pl.multiple_of(kind * width + group * 4 * HD, 4 * HD), 4 * HD)
                spans.append(jnp.transpose(product(hid1[...], wq[:, cols])))
            cos, sin = cos_ref[...], sin_ref[...]
            for inner in range(4):
                which = group * 4 + inner
                for kind in range(2):
                    top = spans[kind][inner * HD : inner * HD + HD // 2]
                    low_half = spans[kind][inner * HD + HD // 2 : (inner + 1) * HD]
                    turned = jnp.concatenate(
                        [top * cos - low_half * sin, low_half * cos + top * sin], axis=0
                    ).astype(jnp.bfloat16)
                    if kind == 0:
                        turned = turned * jnp.bfloat16(score_scale)
                    qs_ref[which, kind * HD : (kind + 1) * HD, :] = turned
                qs_ref[which, 2 * HD :, :] = spans[2][inner * HD : (inner + 1) * HD].astype(
                    jnp.bfloat16
                )
            return carry

        lax.fori_loop(0, heads // 4, project, 0)

        def send_block(step, carry):
            send_head(lax.rem(step + 3 * (plane + 2), heads), qs_ref, buf_ref, fs, fr)
            return carry

        lax.fori_loop(0, heads, send_block, 0)

    def send_head(which, source, target, send_sem, recv_sem):
        goal = head_owner(which)

        @pl.when(goal != me)
        def _():
            remote(
                source.at[which], target.at[me], send_sem.at[which], recv_sem.at[me], ctx=goal
            ).start()

        @pl.when(goal == me)
        def _():
            pltpu.make_async_copy(source.at[which], target.at[me], recv_sem.at[me]).start()

    pl.run_scoped(
        opening,
        pltpu.VMEM((width // 2, 4 * width), jnp.bfloat16),
        pltpu.VMEM((BLOCK, width), jnp.bfloat16),
    )

    def forward(pair_ref, low_ref):
        def value_of(key):
            ones = jnp.ones((16, BLOCK), jnp.bfloat16)
            return jnp.concatenate([buf_ref[key, 2 * HD :, :], ones], axis=0)

        def attend(group):
            first = 4 * group
            for inner in range(4):
                block = first + inner
                landed(buf_ref.at[block], fr.at[block])
                rows = pl.ds(pl.multiple_of(block * BLOCK, BLOCK), BLOCK)
                pair_ref[rows, :] = transposed(buf_ref[block, HD:, :])
            query = side_by_side(lambda block: buf_ref[block, :HD, :], first)
            query = jnp.concatenate([query, jnp.zeros_like(query)], axis=0)

            def step(state, key, count, skip):
                high, mixed = state
                rows = pl.ds(pl.multiple_of(key * BLOCK, BLOCK), count * BLOCK)
                begin = (skip or 0) * BLOCK
                scores = product(pair_ref[rows, :], query[:, begin:])
                if skip is not None:
                    scores = jnp.where(seen(scores.shape), scores, masked_score)
                new_high = jnp.maximum(high[:, begin:], jnp.max(scores, axis=0, keepdims=True))
                weights = jnp.exp(scores - new_high).astype(jnp.bfloat16)
                values = jnp.concatenate([value_of(key + index) for index in range(count)], axis=1)
                new_mixed = mixed[:, begin:] * jnp.exp(high[:, begin:] - new_high) + product(
                    values, weights
                )
                if begin:
                    new_high = jnp.concatenate([high[:, :begin], new_high], axis=1)
                    new_mixed = jnp.concatenate([mixed[:, :begin], new_mixed], axis=1)
                return new_high, new_mixed

            state = (
                jnp.full((1, 4 * BLOCK), masked_score, jnp.float32),
                jnp.zeros((HD + 16, 4 * BLOCK), jnp.float32),
            )
            state = lax.fori_loop(
                0, group, lambda index, now: step(now, 4 * index, 4, None), state
            )
            state = step(state, first, 2, 0)
            high, mixed = step(state, first + 2, 2, 2)
            total = mixed[HD : HD + 1]
            mixed = mixed[:HD] / total
            lse = high + jnp.log(total)
            for inner in range(4):
                block = first + inner
                cols = slice(inner * BLOCK, (inner + 1) * BLOCK)
                mix_ref[block] = mixed[:, cols]
                low_ref[block] = mixed[:, cols].astype(jnp.bfloat16)
                lse_ref[block] = jnp.broadcast_to(lse[:, cols], (8, BLOCK))
                return_block(me, head, block, low_ref, att_ref, fbs, fbr)

        def visit(group, carry):
            @pl.when(owner)
            def _():
                attend(group)

            for when in range(2):
                @pl.when(group == when)
                def _(when=when):
                    pass_on(3 + when)

            return carry

        lax.fori_loop(0, blocks // 4, visit, 0)
        pass_on(5)

        @pl.when(owner)
        def _():
            return_sent(me, head, blocks, low_ref, att_ref, fbs, fbr)

        scatter_sent(me, heads, qs_ref, buf_ref, fs, fr)
        wait_heads(heads, att_ref, fbr)

    pl.run_scoped(
        forward,
        pltpu.VMEM((blocks * BLOCK, 2 * HD), jnp.bfloat16),
        pltpu.VMEM((blocks, HD, BLOCK), jnp.bfloat16),
    )

    span = width // 2
    mine = pl.ds(pl.multiple_of(core * span, 128), span)
    theirs = pl.ds(pl.multiple_of((1 - core) * span, 128), span)
    deep = width // 2
    half_deep = deep // 2
    small = half_deep // planes

    def part_of(unit, half, cols):
        return parts.at[unit, half, :, cols]

    def qkv_part(unit, half, cols):
        return wd.at[pl.ds(pl.multiple_of(((unit - 9) * 2 + half) * deep, 16), deep), cols]

    def sib_of(unit, half):
        return sib_ref.at[unit, half]

    def qkv_sib(unit, half):
        cols = pl.ds(pl.multiple_of(((unit - 9) * 2 + half) * span, 128), span)
        return wu.at[pl.ds(0, deep), cols]

    def pipeline(part, sib):
        def to_sibling(unit):
            return [
                remote(part(unit, half, theirs), sib(unit, half),
                       s_sib.at[unit, half], r_sib.at[unit, half], ctx=sibling)
                for half in range(2)
            ]

        def to_row(unit):
            return [remote(sib(unit, other), row_ref.at[unit],
                           s_row.at[unit], r_row.at[unit], fsdp=other)]

        def to_x(unit):
            rows = pl.ds(pl.multiple_of((1 - xbit) * half_deep, 16), half_deep)
            return [remote(row_ref.at[unit, rows], x_ref.at[unit],
                           s_x.at[unit], r_x.at[unit], ctx=chip_next)]

        def to_z(unit):
            copies = []
            for step in range(1, planes):
                goal = lax.rem(plane + step, planes)
                rows = pl.ds(pl.multiple_of(goal * small, 16), small)
                copies.append(
                    remote(x_ref.at[unit, rows], z_ref.at[unit - 9, step - 1],
                           s_z.at[unit, step - 1], r_z.at[unit, step - 1], ctx=4 * goal + piece)
                )
            return copies

        def slab(unit, which):
            rows = pl.ds(pl.multiple_of(xbit * half_deep + which * small, 16), small)
            return res_ref.at[unit, rows, mine]

        def along_z(unit):
            return [
                remote(slab(unit, plane), slab(unit, plane),
                       s_az.at[unit, step - 1], r_az.at[unit, step - 1],
                       ctx=4 * lax.rem(plane + step, planes) + piece)
                for step in range(1, planes)
            ]

        def along_x(unit):
            rows = pl.ds(pl.multiple_of(xbit * half_deep, 16), half_deep)
            ref = res_ref.at[unit, rows, mine]
            return [remote(ref, ref, s_ax.at[unit], r_ax.at[unit], ctx=chip_next)]

        def along_s(unit):
            ref = res_ref.at[unit, :, mine]
            return [remote(ref, ref, s_as.at[unit], r_as.at[unit], ctx=sibling)]

        def launch(copies):
            for copy in copies:
                copy.start()

        def write_out(unit, which, cols):
            side = core if which == 0 else 1 - core
            kind = lax.rem(unit, 4)
            order = 2 * (unit // 4) + lax.rem(kind, 2)

            def save(target):
                pltpu.make_async_copy(
                    res_ref.at[unit, :, cols], target, out_sem.at[unit, which]
                ).start()

            @pl.when((unit < 8) & (kind < 2))
            def _():
                save(og_down.at[pl.ds(pl.multiple_of(order * deep, 16), deep),
                                pl.ds(pl.multiple_of(side * span, 128), span)])

            @pl.when((unit < 8) & (kind >= 2))
            def _():
                start = side * 4 * span + order * span
                save(og_up.at[:, pl.ds(pl.multiple_of(start, 128), span)])

            @pl.when(unit == 8)
            def _():
                save(og_out.at[:, pl.ds(pl.multiple_of(side * span, 128), span)])

            @pl.when(unit > 8)
            def _():
                start = (unit - 9) * width + side * span
                save(og_qkv.at[:, pl.ds(pl.multiple_of(start, 128), span)])

        def stage0(unit):
            launch(to_sibling(unit))

        def stage1(unit):
            for half in range(2):
                landed(sib(unit, half), r_sib.at[unit, half])
                ref, part_ref = sib(unit, half), part(unit, half, mine)

                def put(spot, value, ref=ref):
                    ref[spot, :] = value

                add_into(put, lambda spot, ref=ref: ref[spot, :],
                         lambda spot, part_ref=part_ref: part_ref[spot, :], deep)
            launch(to_row(unit))

        def stage2(unit):
            landed(row_ref.at[unit], r_row.at[unit])
            ref = sib(unit, row)

            def put(spot, value):
                row_ref[unit, spot, :] = value

            add_into(put, lambda spot: row_ref[unit, spot, :], lambda spot: ref[spot, :], deep)
            launch(to_x(unit))
            for make in (to_sibling, to_row):
                for copy in make(unit):
                    copy.wait_send()

        def stage3(unit):
            landed(x_ref.at[unit], r_x.at[unit])
            ref = row_ref.at[unit, pl.ds(pl.multiple_of(xbit * half_deep, 16), half_deep)]

            def put(spot, value):
                x_ref[unit, spot, :] = value

            add_into(put, lambda spot: x_ref[unit, spot, :], lambda spot: ref[spot, :], half_deep)

        def stage3_direct(unit):
            stage3(unit)
            launch(to_z(unit))

        def stage4(unit):
            rows = pl.ds(pl.multiple_of(plane * small, 16), small)
            total = x_ref[unit, rows, :].astype(jnp.float32)
            for step in range(1, planes):
                landed(z_ref.at[unit - 9, step - 1], r_z.at[unit, step - 1])
                total += z_ref[unit - 9, step - 1].astype(jnp.float32)
            spots = pl.ds(pl.multiple_of(xbit * half_deep + plane * small, 16), small)
            res_ref[unit, spots, mine] = total.astype(jnp.bfloat16)
            launch(along_z(unit))

        def stage5(unit):
            for step in range(1, planes):
                landed(slab(unit, lax.rem(plane + planes - step, planes)), r_az.at[unit, step - 1])
            launch(along_x(unit))

        def stage6(unit):
            rows = pl.ds(pl.multiple_of((1 - xbit) * half_deep, 16), half_deep)
            landed(res_ref.at[unit, rows, mine], r_ax.at[unit])
            launch(along_s(unit))
            write_out(unit, 0, mine)

        line_rows = half_deep // 2

        def line_spots(way):
            return pl.ds(way * line_rows, line_rows)

        def line_slab(unit, way):
            rows = pl.ds(pl.multiple_of(xbit * half_deep + way * line_rows, 16), line_rows)
            return res_ref.at[unit, rows, mine]

        def line_sum(unit, way):
            goal = me - 4 if way == 0 else me + 4
            return remote(x_ref.at[unit, line_spots(way)], line_ref.at[unit, way],
                          s_z.at[unit, way], r_z.at[unit, way], ctx=goal)

        def line_back(unit, way):
            goal = me + 4 if way == 0 else me - 4
            return remote(line_slab(unit, way), line_slab(unit, way),
                          s_az.at[unit, way], r_az.at[unit, way], ctx=goal)

        def line_place(way):
            return planes - 1 - plane if way == 0 else plane

        def line_add(unit, way):
            landed(line_ref.at[unit, way], r_z.at[unit, way])
            total = x_ref[unit, line_spots(way), :].astype(jnp.float32)
            return (total + line_ref[unit, way].astype(jnp.float32)).astype(jnp.bfloat16)

        def towards(hop):
            def stage(unit):
                if hop == 0:
                    stage3(unit)
                for way in range(2):
                    @pl.when(line_place(way) == hop)
                    def _(way=way):
                        if hop == planes - 1:
                            line_slab(unit, way)[...] = line_add(unit, way)
                            line_back(unit, way).start()
                            return
                        if hop:
                            x_ref[unit, line_spots(way), :] = line_add(unit, way)
                        line_sum(unit, way).start()

            return stage

        def homewards(hop):
            def stage(unit):
                for way in range(2):
                    @pl.when(line_place(way) == planes - 1 - hop)
                    def _(way=way):
                        landed(line_slab(unit, way), r_az.at[unit, way])
                        if hop < planes - 1:
                            line_back(unit, way).start()

                if hop == planes - 1:
                    launch(along_x(unit))

            return stage

        def close(unit):
            landed(res_ref.at[unit, :, theirs], r_as.at[unit])
            write_out(unit, 1, theirs)
            for make in (to_x, along_x, along_s):
                for copy in make(unit):
                    copy.wait_send()

        def line_close(unit):
            close(unit)
            for way in range(2):
                @pl.when(line_place(way) < planes - 1)
                def _(way=way):
                    line_sum(unit, way).wait_send()

                @pl.when(line_place(way) > 0)
                def _(way=way):
                    line_back(unit, way).wait_send()

        def stage7(unit):
            close(unit)
            for make in (to_z, along_z):
                for copy in make(unit):
                    copy.wait_send()

        line = [towards(hop) for hop in range(planes)]
        line += [homewards(hop) for hop in range(1, planes)]
        direct = [stage3_direct, stage4, stage5, stage6, stage7]
        return stage0, stage1, stage2, line + [stage6, line_close], direct

    early = pipeline(part_of, sib_of)
    late = pipeline(qkv_part, qkv_sib)

    def tick(time, carry):
        @pl.when((time >= 0) & (time < 9))
        def _():
            early[2](time)

        @pl.when((time >= 9) & (time < 12))
        def _():
            late[2](time)

        for lag, stage in enumerate(early[3]):
            unit = time - lag - 1

            @pl.when((unit >= 0) & (unit < 9))
            def _(stage=stage, unit=unit):
                stage(unit)

        for lag, stage in enumerate(late[4]):
            unit = time - lag - 1

            @pl.when((unit >= 9) & (unit < 12))
            def _(stage=stage, unit=unit):
                stage(unit)

        return carry

    def begin(stages, first, last):
        def one(unit, carry):
            stages[1](unit)
            return carry

        lax.fori_loop(first, last, one, 0)

    def ticks(first, last):
        lax.fori_loop(first, last, tick, 0)

    def middle_part(act_ref, slope_ref, hid2, hid2_t, low_ref):
        acc_ref = ingrad_ref
        own_copy(1).wait()
        chunk_done(3)
        att_t = att_ref[...].reshape(width, BLOCK)
        ap_ref[...] = product(transposed(att_t), wo[...])
        gate_attn = mod_ref[:1, width : 2 * width]
        scale_mlp = mod_ref[:1, 2 * width : 3 * width]
        gate_mlp = mod_ref[:1, 3 * width :]
        mid_ref[...] = tok_ref[...].astype(jnp.float32) + gate_attn * ap_ref[...]
        normed, unused = layer_norm(mid_ref[...])
        low = (normed * (1.0 + scale_mlp)).astype(jnp.bfloat16)
        hid2[...] = low
        hid2_t[...] = transposed(low)
        acc_ref[...] = jnp.zeros_like(acc_ref)
        own_copy(2).wait()
        chunk_done(4)
        own_copy(3).wait()
        chunk_done(5)
        curve = math.sqrt(2.0 / math.pi)

        def up(index, carry):
            cols = pl.ds(pl.multiple_of(index * width, width), width)
            before = product(hid2[...], wu[:, cols])
            square = before * before
            bent = jnp.tanh(curve * (before + 0.044715 * (square * before)))
            after = (0.5 * before * (1.0 + bent)).astype(jnp.bfloat16)
            act_ref[:, cols] = after
            slope_ref[:, cols] = 0.5 * (1.0 + bent) + 0.5 * before * (1.0 - bent * bent) * (
                curve * (1.0 + 3.0 * 0.044715 * square)
            )
            acc_ref[...] += product(after, wd[cols, :])
            return carry

        lax.fori_loop(0, 4, up, 0)
        grad = cot_ref[...].astype(jnp.float32)
        mlp_out = acc_ref[...]
        result_ref[...] = mid_ref[...] + gate_mlp * mlp_out
        sums_ref[3:4, :] = jnp.sum(grad * mlp_out, axis=0, keepdims=True)
        low_ref[...] = (grad * gate_mlp).astype(jnp.bfloat16)
        acc_ref[...] = jnp.zeros_like(acc_ref)

        def down(index, carry):
            for side in range(2):
                cols = pl.ds(pl.multiple_of(side * 2 * width + index * width, width), width)
                grad_act = product_back(low_ref[...], wd[cols, :])
                grad_pre = (grad_act * slope_ref[:, cols]).astype(jnp.bfloat16)
                grad_down = product(transposed(act_ref[:, cols]), low_ref[...])
                for pick in range(2):
                    parts[4 * index + pick, side] = grad_down[
                        pick * deep : (pick + 1) * deep
                    ].astype(jnp.bfloat16)
                grad_up = product(hid2_t[...], grad_pre).astype(jnp.bfloat16)
                for pick in range(2):
                    for half in range(2):
                        parts[4 * index + 2 + pick, half, :, side * span : (side + 1) * span] = (
                            grad_up[half * deep : (half + 1) * deep, pick * span : (pick + 1) * span]
                        )
                acc_ref[...] += product_back(grad_pre, wu[:, cols])
            for pick in range(4):
                early[0](4 * index + pick)
            begin(early, 0, 4 * index)
            return carry

        lax.fori_loop(0, 2, down, 0)
        for index in range(len(chunks)):
            chunk_sent(index)
        pl.semaphore_signal(free_sem, inc=1, device_id={"ctx": sibling}, device_id_type=MESH)
        grad_hidden = acc_ref[...]
        normed, inverse = layer_norm(mid_ref[...])
        sums_ref[2:3, :] = jnp.sum(grad_hidden * normed, axis=0, keepdims=True)
        grad_mid = cot_ref[...].astype(jnp.float32) + norm_back(
            grad_hidden * (1.0 + scale_mlp), normed, inverse
        )
        ingrad_ref[...] = grad_mid
        sums_ref[1:2, :] = jnp.sum(grad_mid * ap_ref[...], axis=0, keepdims=True)
        gap = (grad_mid * gate_attn).astype(jnp.bfloat16)
        low_ref[...] = gap
        douts_ref[...] = product_back(wo[...], gap).astype(jnp.bfloat16).reshape(
            heads, HD, BLOCK
        )

        def send_dout(step, carry):
            send_head(lax.rem(step + 3 * (plane + 2), heads), douts_ref, got_ref, bs, br)
            return carry

        lax.fori_loop(0, heads, send_dout, 0)
        begin(early, 4, 8)
        grad_out = product(att_ref[...].reshape(width, BLOCK), low_ref[...]).astype(jnp.bfloat16)
        parts[8, 0] = grad_out[:deep]
        parts[8, 1] = grad_out[deep:]
        early[0](8)
        begin(early, 8, 9)
        ticks(0, FIRST_TICKS)

    pl.run_scoped(
        middle_part,
        pltpu.VMEM((BLOCK, 4 * width), jnp.bfloat16),
        pltpu.VMEM((BLOCK, 4 * width), jnp.float32),
        pltpu.VMEM((BLOCK, width), jnp.bfloat16),
        pltpu.VMEM((width, BLOCK), jnp.bfloat16),
        pltpu.VMEM((BLOCK, width), jnp.bfloat16),
    )

    def backward(both_ref, side_ref, grad_ref, lse_wide, delta_wide, low_ref):
        @pl.when(owner)
        def _():
            def prepare(group, carry):
                first = 4 * group
                for inner in range(4):
                    landed(got_ref.at[first + inner], br.at[first + inner])
                dout = side_by_side(lambda block: got_ref[block], first)
                query = side_by_side(lambda block: buf_ref[block, :HD, :], first)
                mixed = side_by_side(lambda block: mix_ref[block], first)
                both = jnp.concatenate([query, dout], axis=0)
                both_ref[group] = both
                side_ref[group] = transposed(both)
                grad_ref[group] = jnp.zeros((HD, 4 * BLOCK), jnp.float32)
                lse_wide[group] = side_by_side(lambda block: lse_ref[block], first)
                delta = jnp.sum(dout.astype(jnp.float32) * mixed, axis=0, keepdims=True)
                delta_wide[group] = jnp.broadcast_to(delta, (8, 4 * BLOCK))
                return carry

            lax.fori_loop(0, blocks // 4, prepare, 0)

        def key_back(group, inner):
            key = 4 * group + inner
            pair = transposed(buf_ref[key, HD:, :])
            left = lax.broadcasted_iota(jnp.int32, pair.shape, 1) < HD
            none = jnp.zeros_like(pair)
            key_side, value_side = jnp.where(left, pair, none), jnp.where(left, none, pair)
            key_low = buf_ref[key, HD : 2 * HD, :]

            def visit_queries(which, skip, state):
                begin = skip * BLOCK
                both = both_ref[which, :, begin:]
                probs = jnp.exp(product(key_side, both) - lse_wide[which, :1, begin:])
                grad_scores = (
                    probs * (product(value_side, both) - delta_wide[which, :1, begin:])
                ).astype(jnp.bfloat16)
                side = side_ref[which, begin:, :]
                grad_ref[which, :, begin:] += product(key_low, grad_scores)
                return (
                    state[0] + product(grad_scores, side),
                    state[1] + product(probs.astype(jnp.bfloat16), side),
                )

            zero = jnp.zeros((BLOCK, 2 * HD), jnp.float32)
            state = visit_queries(group, inner, (zero, zero))
            state = lax.fori_loop(
                group + 1, blocks // 4, lambda which, now: visit_queries(which, 0, now), state
            )
            low_ref[key, HD : 2 * HD, :] = jnp.transpose(state[0])[:HD].astype(jnp.bfloat16)
            low_ref[key, 2 * HD :, :] = jnp.transpose(state[1])[HD:].astype(jnp.bfloat16)
            return_rows(key, HD, 2 * HD, 0)

        def part_copy_of(block, first, count, slot):
            return remote(
                low_ref.at[block, pl.ds(first, count)], gland_ref.at[head, pl.ds(first, count)],
                bbs.at[block, slot], bbr.at[head, slot], ctx=block,
            )

        def return_rows(block, first, count, slot):
            @pl.when(block != me)
            def _():
                part_copy_of(block, first, count, slot).start()

            @pl.when(block == me)
            def _():
                pltpu.make_async_copy(
                    low_ref.at[block, pl.ds(first, count)],
                    gland_ref.at[head, pl.ds(first, count)],
                    bbr.at[head, slot],
                ).start()

        def visit(step, carry):
            for inner in range(4):
                for edge in range(len(SPLITS) - 1):
                    @pl.when(owner & (step == (len(SPLITS) - 1) * inner + edge))
                    def _(inner=inner, edge=edge):
                        def one(group, carry):
                            key_back(group, inner)
                            return carry

                        lax.fori_loop(SPLITS[edge], SPLITS[edge + 1], one, 0)

            low = sum(jnp.where(step > index, count, 0) for index, count in enumerate(TICKS))
            high = sum(jnp.where(step >= index, count, 0) for index, count in enumerate(TICKS))
            ticks(low + FIRST_TICKS, high + FIRST_TICKS)

            @pl.when(owner & (step == len(TICKS) - 2))
            def _():
                finish_queries()

            return carry

        def finish_queries():
            def finish_query(group, carry):
                grad_query = (grad_ref[group] * score_scale).astype(jnp.bfloat16)
                for inner in range(4):
                    block = 4 * group + inner
                    low_ref[block, :HD, :] = grad_query[:, inner * BLOCK : (inner + 1) * BLOCK]
                    return_rows(block, 0, HD, 1)
                return carry

            lax.fori_loop(0, blocks // 4, finish_query, 0)

        lax.fori_loop(0, len(TICKS), visit, 0)

        @pl.when(owner)
        def _():
            def sent(block, carry):
                @pl.when(block != me)
                def _():
                    part_copy_of(block, HD, 2 * HD, 0).wait_send()
                    part_copy_of(block, 0, HD, 1).wait_send()

                return carry

            lax.fori_loop(0, blocks, sent, 0)

        scatter_sent(me, heads, douts_ref, got_ref, bs, br)

        def arrived(which, carry):
            landed(gland_ref.at[which, pl.ds(HD, 2 * HD)], bbr.at[which, 0])
            landed(gland_ref.at[which, pl.ds(0, HD)], bbr.at[which, 1])
            return carry

        lax.fori_loop(0, heads, arrived, 0)

    pl.run_scoped(
        backward,
        pltpu.VMEM((blocks // 4, 2 * HD, 4 * BLOCK), jnp.bfloat16),
        pltpu.VMEM((blocks // 4, 4 * BLOCK, 2 * HD), jnp.bfloat16),
        pltpu.VMEM((blocks // 4, HD, 4 * BLOCK), jnp.float32),
        pltpu.VMEM((blocks // 4, 8, 4 * BLOCK), jnp.float32),
        pltpu.VMEM((blocks // 4, 8, 4 * BLOCK), jnp.float32),
        pltpu.VMEM((blocks, 3 * HD, BLOCK), jnp.bfloat16),
    )

    def closing(gproj, acc_ref):
        def turn_back(group, carry):
            cos, sin = cos_ref[...], sin_ref[...]
            for kind in range(3):
                pieces = []
                for inner in range(4):
                    which = group * 4 + inner
                    if kind == 2:
                        pieces.append(gland_ref[which, 2 * HD :, :])
                        continue
                    top = gland_ref[which, kind * HD : kind * HD + HD // 2, :].astype(jnp.float32)
                    bottom = gland_ref[
                        which, kind * HD + HD // 2 : (kind + 1) * HD, :
                    ].astype(jnp.float32)
                    pieces.append((top * cos + bottom * sin).astype(jnp.bfloat16))
                    pieces.append((bottom * cos - top * sin).astype(jnp.bfloat16))
                cols = pl.ds(pl.multiple_of(kind * width + group * 4 * HD, 4 * HD), 4 * HD)
                gproj[:, cols] = transposed(jnp.concatenate(pieces, axis=0))
            return carry

        lax.fori_loop(0, heads // 4, turn_back, 0)
        acc_ref[...] = jnp.zeros_like(acc_ref)
        pl.semaphore_wait(free_sem, 1)

        def gradient(index, carry):
            cols = pl.ds(pl.multiple_of(index * width, width), width)
            low = product(hid1_t[...], gproj[:, cols]).astype(jnp.bfloat16)
            wd[pl.ds(pl.multiple_of(index * width, width), width), :] = low
            late[0](9 + index)
            return carry

        lax.fori_loop(0, 3, gradient, 0)

        def back(index, carry):
            cols = pl.ds(pl.multiple_of(index * width, width), width)
            acc_ref[...] += product_back(gproj[:, cols], wq[:, cols])
            return carry

        begin(late, 9, 12)
        lax.fori_loop(0, 3, back, 0)
        normed, inverse = layer_norm(tok_ref[...].astype(jnp.float32))
        grad_hidden = acc_ref[...]
        sums_ref[0:1, :] = jnp.sum(grad_hidden * normed, axis=0, keepdims=True)
        ingrad_ref[...] = ingrad_ref[...] + norm_back(
            grad_hidden * (1.0 + mod_ref[:1, :width]), normed, inverse
        )

    pl.run_scoped(
        closing,
        pltpu.VMEM((BLOCK, 3 * width), jnp.bfloat16),
        pltpu.VMEM((BLOCK, width), jnp.float32),
    )

    def slots(first, count):
        return table_ref.at[pl.ds(first, count)]

    chip_slot = core * 4 * planes + 4 * plane

    def table_row():
        ref = slots(chip_slot + 2 * xbit + row, 1)
        return [remote(ref, ref, s_t.at[0], r_t.at[0], fsdp=other)]

    def table_x():
        ref = slots(chip_slot + 2 * xbit, 2)
        return [remote(ref, ref, s_t.at[1], r_t.at[1], ctx=chip_next)]

    def table_z():
        ref = slots(chip_slot, 4)
        return [
            remote(ref, ref, s_t.at[2 + step], r_t.at[2 + step],
                   ctx=4 * lax.rem(plane + step, planes) + piece)
            for step in range(1, planes)
        ]

    def table_s():
        ref = slots(core * 4 * planes, 4 * planes)
        return [remote(ref, ref, s_t.at[2], r_t.at[2], ctx=sibling)]

    spot = chip_slot + 2 * xbit + row
    for index in range(4):
        table_ref[spot, index : index + 1, :] = sums_ref[index : index + 1, :]
    table_ref[spot, 4:5, :] = emb_ref[:1, :]
    for copy in table_row():
        copy.start()

    begun = FIRST_TICKS + sum(TICKS)

    def finish(time, carry):
        tick(time, carry)

        @pl.when(time == begun + 1)
        def _():
            landed(slots(chip_slot + 2 * xbit + other, 1), r_t.at[0])
            for copy in table_x():
                copy.start()

        @pl.when(time == begun + 3)
        def _():
            landed(slots(chip_slot + 2 * (1 - xbit), 2), r_t.at[1])
            for copy in table_z():
                copy.start()

        @pl.when(time == begun + 5)
        def _():
            for step in range(1, planes):
                goal = lax.rem(plane + planes - step, planes)
                landed(slots(core * 4 * planes + 4 * goal, 4), r_t.at[2 + step])
            for copy in table_s():
                copy.start()

        return carry

    lax.fori_loop(begun, 9 + len(early[3]), finish, 0)
    landed(slots((1 - core) * 4 * planes, 4 * planes), r_t.at[2])
    count = 2 * blocks
    emb_cols = pl.ds(pl.multiple_of(row * (width // 2), 128), width // 2)
    eds = table_ref[:, 4, emb_cols].astype(jnp.bfloat16)
    eds_ref[...] = transposed(jnp.concatenate([eds] * 3, axis=0))
    for index in range(4):
        left = table_ref[:, index, :]
        for third_part in range(3):
            low = left.astype(jnp.bfloat16)
            left = left - low.astype(jnp.float32)
            sds_ref[
                third_part * count : (third_part + 1) * count, index * width : (index + 1) * width
            ] = low
    for copies in (table_row(), table_x(), table_z(), table_s()):
        for copy in copies:
            copy.wait_send()

    def saved(unit, carry):
        for which in range(2):
            pltpu.make_async_copy(
                res_ref.at[unit, :, pl.ds(0, span)], og_out.at[:, pl.ds(0, span)],
                out_sem.at[unit, which],
            ).wait()
        return carry

    lax.fori_loop(0, 12, saved, 0)


def side_by_side(pick, first):
    return jnp.concatenate([pick(first + inner) for inner in range(4)], axis=1)


def seen(shape):
    keys = lax.broadcasted_iota(jnp.int32, shape, 0) // BLOCK
    return keys <= lax.broadcasted_iota(jnp.int32, shape, 1) // BLOCK


FIRST_TICKS = 1
TICKS = (1, 1, 1, 1, 1, 0, 1, 0, 2)
SPLITS = (0, 1, 4)


def widen_kernel(*refs):
    lows, eds_ref, sds_ref = refs[2:6], refs[6], refs[7]
    outs = refs[8:]
    for source, target in zip(refs[:2], outs[:2]):
        target[...] = source[...]
    for source, target in zip(lows, outs[2:6]):
        target[...] = source[...].astype(jnp.float32)
    outs[6][...] = product(eds_ref[...], sds_ref[...])


def widen(result, input_grad, sums, eds, sds):
    steps = WIDEN_STEPS

    def rows_of(array):
        return pl.BlockSpec((array.shape[0] // steps, array.shape[1]), lambda index: (index, 0))

    ada = jax.ShapeDtypeStruct((eds.shape[0], sds.shape[1]), jnp.float32)
    arrays = [result, input_grad, *sums]
    outs = [jax.ShapeDtypeStruct(array.shape, jnp.float32) for array in arrays] + [ada]
    got = pl.pallas_call(
        widen_kernel,
        grid=(steps,),
        out_shape=outs,
        in_specs=[rows_of(array) for array in arrays]
        + [rows_of(eds), pl.BlockSpec(sds.shape, lambda index: (0, 0))],
        out_specs=[rows_of(array) for array in outs],
        compiler_params=pltpu.CompilerParams(vmem_limit_bytes=VMEM_LIMIT),
    )(*arrays, eds, sds)
    return got[0], got[1], got[2:6], got[6]


WIDEN_STEPS = 4


def rope_constants(blocks):
    half = HD // 2
    frequency = rope_base ** (-2.0 * np.arange(half, dtype=np.float64) / HD)
    inner = frequency[:, None] * np.arange(BLOCK, dtype=np.float64)[None, :]
    outer = frequency[:, None] * (BLOCK * np.arange(128, dtype=np.float64))[None, :]
    outer = np.where(np.arange(128)[None, :] < blocks, outer, 0.0)
    return np.concatenate(
        [np.cos(inner), np.sin(inner), np.cos(outer), np.sin(outer)], axis=1
    ).astype(np.float32)


def fast_device(tokens, timestep, time_table, w_qkv, w_out, w_up, w_down, w_ada, cotangent):
    rows, width = tokens.shape[1:]
    heads = width // HD
    blocks = lax.axis_size("ctx")
    planes = blocks // 4
    deep, span = width // 2, width // 2
    embedded = lax.dynamic_slice_in_dim(time_table, timestep[0, 0], 1, 0)
    embedded = embedded.astype(jnp.bfloat16).astype(jnp.float32)
    emb_rows = jnp.broadcast_to(embedded, (8, width))
    hbm = pl.BlockSpec(memory_space=pl.ANY)
    vmem = pl.BlockSpec(memory_space=pltpu.VMEM)
    low, high = jnp.bfloat16, jnp.float32
    dma = pltpu.SemaphoreType.DMA
    steps = planes - 1
    units = 12
    scratch = [
        pltpu.VMEM((width, 3 * width), low),
        pltpu.VMEM((width, width), low),
        pltpu.VMEM((width, 4 * width), low),
        pltpu.VMEM((4 * width, width), low),
        pltpu.VMEM((8, 4 * width), high),
        pltpu.VMEM((8, width), high),
        pltpu.VMEM((8, 4 * width), high),
        pltpu.VMEM((8, 4 * width), high),
        pltpu.VMEM((width, BLOCK), low),
        pltpu.VMEM((BLOCK, width), high),
        pltpu.VMEM((BLOCK, width), high),
        pltpu.VMEM((8, width), high),
        pltpu.VMEM((HD // 2, BLOCK), high),
        pltpu.VMEM((HD // 2, BLOCK), high),
        pltpu.VMEM((heads, 3 * HD, BLOCK), low),
        pltpu.VMEM((blocks, 3 * HD, BLOCK), low),
        pltpu.VMEM((blocks, HD, BLOCK), high),
        pltpu.VMEM((blocks, 8, BLOCK), high),
        pltpu.VMEM((heads, HD, BLOCK), low),
        pltpu.VMEM((heads, HD, BLOCK), low),
        pltpu.VMEM((blocks, HD, BLOCK), low),
        pltpu.VMEM((9, 2, deep, width), low),
        pltpu.VMEM((9, 2, deep, span), low),
        pltpu.VMEM((units, deep, span), low),
        pltpu.VMEM((units, deep // 2, span), low),
        pltpu.VMEM((3, steps, deep // 2 // planes, span), low),
        pltpu.VMEM((9, 2, deep // 4, span), low),
        pltpu.VMEM((units, deep, width), low),
        pltpu.VMEM((2 * blocks, 8, width), high),
    ]
    sems = [
        (5,), (2,), (2,), (6, 4), (6, 4),
        (heads,), (blocks,), (blocks,), (heads,),
        (heads,), (blocks,), (blocks, 2), (heads, 2),
        (units, 2), (units, 2), (units,), (units,), (units,), (units,),
        (units, steps), (units, steps), (units, steps), (units, steps),
        (units,), (units,), (units,), (units,), (planes + 2,), (planes + 2,), (units, 2),
    ]
    scratch += [dma(shape) for shape in sems] + [pltpu.SemaphoreType.REGULAR]
    result, input_grad, eds, sds, *sums = pl.pallas_call(
        functools.partial(layer_kernel, blocks, heads),
        out_shape=[
            jax.ShapeDtypeStruct((rows, width), high),
            jax.ShapeDtypeStruct((rows, width), high),
            jax.ShapeDtypeStruct((deep, 6 * blocks), low),
            jax.ShapeDtypeStruct((6 * blocks, 4 * width), low),
        ]
        + [jax.ShapeDtypeStruct(w.shape, low) for w in (w_qkv, w_out, w_up, w_down)],
        in_specs=[vmem] * 4 + [hbm] * 5,
        out_specs=[vmem] * 4 + [hbm] * 4,
        scratch_shapes=scratch,
        compiler_params=pltpu.CompilerParams(
            collective_id=1, has_side_effects=True, vmem_limit_bytes=VMEM_LIMIT
        ),
    )(tokens[0], cotangent[0], emb_rows, jnp.asarray(rope_constants(blocks)),
      w_ada, w_qkv, w_out, w_up, w_down)
    result, input_grad, totals, ada_total = widen(result, input_grad, sums, eds, sds)
    return (result[None], input_grad[None], *totals, ada_total)


def solution(mesh):
    chosen = fast_device if mesh.shape["ctx"] == 16 else on_device
    return jax.shard_map(
        chosen,
        mesh=mesh,
        in_specs=(
            P("fsdp", "ctx", None),
            P("fsdp", "ctx"),
            P(),
            P("fsdp", None),
            P("fsdp", None),
            P("fsdp", None),
            P("fsdp", None),
            P("fsdp", None),
            P("fsdp", "ctx", None),
        ),
        out_specs=(
            P("fsdp", "ctx", None),
            P("fsdp", "ctx", None),
            P("fsdp", None),
            P("fsdp", None),
            P("fsdp", None),
            P("fsdp", None),
            P("fsdp", None),
        ),
        check_vma=False,
    )
```

```python
import functools
import math

import jax
import jax.numpy as jnp
import numpy as np
from jax import lax
from jax.experimental import pallas as pl
from jax.experimental.pallas import tpu as pltpu
from jax.sharding import PartitionSpec as P

HD = 64
BLOCK = 256
VMEM_LIMIT = 65152 * 1024
MESH = pl.DeviceIdType.MESH


norm_eps = 1e-06
masked_score = -1e30
rope_base = 10000.0


def layer_norm(values):
    center = values - jnp.mean(values, axis=-1, keepdims=True)
    inverse = lax.rsqrt(jnp.mean(center * center, axis=-1, keepdims=True) + norm_eps)
    return (center * inverse, inverse)


def norm_back(grad_norm, normed, inverse):
    mean_grad = jnp.mean(grad_norm, axis=-1, keepdims=True)
    mean_cross = jnp.mean(grad_norm * normed, axis=-1, keepdims=True)
    return inverse * (grad_norm - mean_grad - normed * mean_cross)


def rope_tables(positions, head_size):
    half_size = head_size // 2
    frequency = jnp.exp(
        jnp.arange(half_size, dtype=jnp.float32) * (-2.0 * math.log(rope_base) / head_size)
    )
    angles = positions.astype(jnp.float32)[:, None] * frequency[None, :]
    cosine_table = jnp.concatenate([jnp.cos(angles), jnp.cos(angles)], axis=-1)[:, None, :]
    sine_table = jnp.concatenate([jnp.sin(angles), jnp.sin(angles)], axis=-1)[:, None, :]
    return (cosine_table, sine_table)


def rotate_half(values):
    middle = values.shape[-1] // 2
    return jnp.concatenate([-values[..., middle:], values[..., :middle]], axis=-1)


def rotate(values, cosine_table, sine_table):
    return values * cosine_table + rotate_half(values) * sine_table


def rotate_back(gradient, cosine_table, sine_table):
    return gradient * cosine_table - rotate_half(gradient * sine_table)


def gelu_tanh(values):
    return jax.nn.gelu(values, approximate=True)


def split_rows(array, sub_rows):
    return array.reshape((array.shape[0] // sub_rows, sub_rows) + array.shape[1:])


def part_starts(total_rows, sub_rows):
    return sub_rows * jnp.arange(total_rows // sub_rows, dtype=jnp.int32)


def keep_same(partial_value):
    return partial_value


def attend_forward(partial_value, pieces, queries, query_block, score_scale):
    key_rows, value_rows = pieces
    sub_rows = queries.shape[0]

    def attend_visit(running, scan_item):
        key_part, value_part, part_start = scan_item

        def attend_update(running):
            running_max, running_sum, running_out = running
            key_block = (part_start + jnp.arange(sub_rows, dtype=jnp.int32)) // BLOCK
            allowed = (key_block[None, :] <= query_block[:, None])[None]
            scores = (
                jnp.einsum("qhd,khd->hqk", queries, key_part, preferred_element_type=jnp.float32)
                * score_scale
            )
            scores = jnp.where(allowed, scores, masked_score)
            new_max = jnp.maximum(running_max, jnp.max(scores, axis=-1))
            weights = jnp.where(allowed, jnp.exp(scores - new_max[..., None]), 0.0)
            decay = jnp.exp(running_max - new_max)
            running_sum = running_sum * decay + jnp.sum(weights, axis=-1)
            running_out = running_out * decay[..., None] + jnp.einsum(
                "hqk,khd->hqd",
                weights.astype(jnp.bfloat16),
                value_part,
                preferred_element_type=jnp.float32,
            )
            return (new_max, running_sum, running_out)

        return (
            lax.cond(part_start // BLOCK <= query_block[-1], attend_update, keep_same, running),
            None,
        )

    partial_value, unused = lax.scan(
        attend_visit,
        partial_value,
        (
            split_rows(key_rows, sub_rows),
            split_rows(value_rows, sub_rows),
            part_starts(key_rows.shape[0], sub_rows),
        ),
    )
    return partial_value


def on_device(tokens, timestep, time_table, w_qkv, w_out, w_up, w_down, w_ada, cotangent):
    tok_rows = tokens.shape[1]
    model_width = tokens.shape[2]
    heads = model_width // HD
    score_scale = 1.0 / math.sqrt(HD)
    highest_precision = lax.Precision.HIGHEST
    full_weights = (
        lax.all_gather(w_qkv, "fsdp", axis=0, tiled=True),
        lax.all_gather(w_out, "fsdp", axis=0, tiled=True),
        lax.all_gather(w_up, "fsdp", axis=0, tiled=True),
        lax.all_gather(w_down, "fsdp", axis=0, tiled=True),
        lax.all_gather(w_ada, "fsdp", axis=0, tiled=True),
    )
    qkv_full, out_full, up_full, down_full, ada_full = full_weights
    steps_onehot = (
        timestep[0][:, None] == jnp.arange(time_table.shape[0], dtype=jnp.int32)[None, :]
    ).astype(jnp.float32)
    embedded = jnp.dot(steps_onehot, time_table, precision=highest_precision).astype(jnp.bfloat16)
    modulation = jnp.dot(embedded, ada_full, preferred_element_type=jnp.float32)
    per_token = jnp.repeat(modulation, BLOCK, axis=0)
    scale_attn, gate_attn, scale_mlp, gate_mlp = jnp.split(per_token, 4, axis=1)
    inputs = tokens[0].astype(jnp.float32)
    normed_one, inverse_one = layer_norm(inputs)
    residual_first = (normed_one * (1.0 + scale_attn)).astype(jnp.bfloat16)
    projected_output = jnp.dot(
        residual_first, qkv_full, preferred_element_type=jnp.float32
    ).reshape(tok_rows, 3, heads, HD)
    positions = lax.axis_index("ctx") * tok_rows + jnp.arange(tok_rows, dtype=jnp.int32)
    cosine_table, sine_table = rope_tables(positions, HD)
    queries = rotate(projected_output[:, 0], cosine_table, sine_table).astype(jnp.bfloat16)
    key_own = rotate(projected_output[:, 1], cosine_table, sine_table).astype(jnp.bfloat16)
    value_own = projected_output[:, 2].astype(jnp.bfloat16)
    query_block = positions // BLOCK
    start_state = (
        jnp.full((heads, tok_rows), masked_score, jnp.float32),
        jnp.zeros((heads, tok_rows), jnp.float32),
        jnp.zeros((heads, tok_rows, HD), jnp.float32),
    )
    running_max, running_sum, running_out = attend_forward(
        start_state,
        (
            lax.all_gather(key_own, "ctx", axis=0, tiled=True),
            lax.all_gather(value_own, "ctx", axis=0, tiled=True),
        ),
        queries,
        query_block,
        score_scale,
    )
    attn_rows = jnp.transpose(running_out / running_sum[..., None], (1, 0, 2))
    query_lse = running_max + jnp.log(running_sum)
    attn_low = attn_rows.reshape(tok_rows, model_width).astype(jnp.bfloat16)
    attention_projected = jnp.dot(attn_low, out_full, preferred_element_type=jnp.float32)
    middle = inputs + gate_attn * attention_projected
    normed_two, inverse_two = layer_norm(middle)
    residual_second = (normed_two * (1.0 + scale_mlp)).astype(jnp.bfloat16)
    before_activation = jnp.dot(residual_second, up_full, preferred_element_type=jnp.float32)
    gelu_activated, gelu_back = jax.vjp(gelu_tanh, before_activation)
    act_low = gelu_activated.astype(jnp.bfloat16)
    feedforward_output = jnp.dot(act_low, down_full, preferred_element_type=jnp.float32)
    result = middle + gate_mlp * feedforward_output
    qkv_back, out_back, up_back, down_back = (
        lax.all_gather(w_qkv, "fsdp", axis=0, tiled=True),
        lax.all_gather(w_out, "fsdp", axis=0, tiled=True),
        lax.all_gather(w_up, "fsdp", axis=0, tiled=True),
        lax.all_gather(w_down, "fsdp", axis=0, tiled=True),
    )
    upstream = cotangent[0].astype(jnp.float32)
    grad_gate_mlp = upstream * feedforward_output
    grad_mlp = (upstream * gate_mlp).astype(jnp.bfloat16)
    grad_down = jnp.einsum("tf,td->fd", act_low, grad_mlp, preferred_element_type=jnp.float32)
    grad_act = jnp.einsum("td,fd->tf", grad_mlp, down_back, preferred_element_type=jnp.float32)
    grad_pre = gelu_back(grad_act)[0].astype(jnp.bfloat16)
    grad_up = jnp.einsum("td,tf->df", residual_second, grad_pre, preferred_element_type=jnp.float32)
    grad_hidden_two = jnp.einsum("tf,df->td", grad_pre, up_back, preferred_element_type=jnp.float32)
    grad_scale_mlp = grad_hidden_two * normed_two
    grad_middle = upstream + norm_back(grad_hidden_two * (1.0 + scale_mlp), normed_two, inverse_two)
    grad_gate_attn = grad_middle * attention_projected
    grad_attn_proj = (grad_middle * gate_attn).astype(jnp.bfloat16)
    grad_out = jnp.einsum("td,te->de", attn_low, grad_attn_proj, preferred_element_type=jnp.float32)
    grad_attended = jnp.einsum(
        "te,de->td", grad_attn_proj, out_back, preferred_element_type=jnp.float32
    )
    grad_heads = grad_attended.astype(jnp.bfloat16).reshape(tok_rows, heads, HD)
    delta_rows = jnp.sum(grad_heads.astype(jnp.float32) * attn_rows, axis=-1)
    query_delta = jnp.transpose(delta_rows)
    lse_rows = jnp.transpose(query_lse)
    lse_high = lse_rows.astype(jnp.bfloat16)
    lse_rest = (lse_rows - lse_high.astype(jnp.float32)).astype(jnp.bfloat16)
    delta_high = delta_rows.astype(jnp.bfloat16)
    delta_rest = (delta_rows - delta_high.astype(jnp.float32)).astype(jnp.bfloat16)
    stat_rows = jnp.concatenate([lse_high, lse_rest, delta_high, delta_rest], axis=1)
    zero_heads = jnp.zeros((tok_rows, heads, HD), jnp.float32)
    partial_value = (zero_heads, zero_heads, zero_heads)
    grad_query = partial_value[0]
    key_rows = lax.all_gather(key_own, "ctx", axis=0, tiled=True)

    def query_visit(partial_value, scan_item):
        key_part, value_part, part_start = scan_item

        def query_update(partial_value):
            key_block = (part_start + jnp.arange(tok_rows, dtype=jnp.int32)) // BLOCK
            allowed = (key_block[None, :] <= query_block[:, None])[None]
            scores = (
                jnp.einsum("qhd,khd->hqk", queries, key_part, preferred_element_type=jnp.float32)
                * score_scale
            )
            probs = jnp.where(allowed, jnp.exp(scores - query_lse[..., None]), 0.0)
            grad_prob = jnp.einsum(
                "qhd,khd->hqk", grad_heads, value_part, preferred_element_type=jnp.float32
            )
            grad_score = (probs * (grad_prob - query_delta[..., None]) * score_scale).astype(
                jnp.bfloat16
            )
            return partial_value + jnp.einsum(
                "hqk,khd->qhd", grad_score, key_part, preferred_element_type=jnp.float32
            )

        return (
            lax.cond(
                part_start // BLOCK <= query_block[-1], query_update, keep_same, partial_value
            ),
            None,
        )

    grad_query, unused = lax.scan(
        query_visit,
        grad_query,
        (
            split_rows(key_rows, tok_rows),
            split_rows(lax.all_gather(value_own, "ctx", axis=0, tiled=True), tok_rows),
            part_starts(key_rows.shape[0], tok_rows),
        ),
    )
    key_partial_value = (partial_value[1], partial_value[2])
    query_rows = lax.all_gather(queries, "ctx", axis=0, tiled=True)

    def key_visit(running, scan_item):
        query_part, dout_part, stat_part, part_start = scan_item

        def key_update(running):
            grad_key, grad_value = running
            query_blk = (part_start + jnp.arange(tok_rows, dtype=jnp.int32)) // BLOCK
            allowed = (query_blk[:, None] >= query_block[None, :])[None]
            stat_float = stat_part.astype(jnp.float32)
            lse_part = jnp.transpose(stat_float[:, :heads] + stat_float[:, heads : 2 * heads])
            delta_part = jnp.transpose(
                stat_float[:, 2 * heads : 3 * heads] + stat_float[:, 3 * heads :]
            )
            scores = (
                jnp.einsum("qhd,khd->hqk", query_part, key_own, preferred_element_type=jnp.float32)
                * score_scale
            )
            probs = jnp.where(allowed, jnp.exp(scores - lse_part[..., None]), 0.0)
            grad_value = grad_value + jnp.einsum(
                "hqk,qhd->khd",
                probs.astype(jnp.bfloat16),
                dout_part,
                preferred_element_type=jnp.float32,
            )
            grad_prob = jnp.einsum(
                "qhd,khd->hqk", dout_part, value_own, preferred_element_type=jnp.float32
            )
            grad_score = (probs * (grad_prob - delta_part[..., None]) * score_scale).astype(
                jnp.bfloat16
            )
            grad_key = grad_key + jnp.einsum(
                "hqk,qhd->khd", grad_score, query_part, preferred_element_type=jnp.float32
            )
            return (grad_key, grad_value)

        last_seen = (part_start + tok_rows - 1) // BLOCK
        return (lax.cond(last_seen >= query_block[0], key_update, keep_same, running), None)

    key_partial_value, unused = lax.scan(
        key_visit,
        key_partial_value,
        (
            split_rows(query_rows, tok_rows),
            split_rows(lax.all_gather(grad_heads, "ctx", axis=0, tiled=True), tok_rows),
            split_rows(lax.all_gather(stat_rows, "ctx", axis=0, tiled=True), tok_rows),
            part_starts(query_rows.shape[0], tok_rows),
        ),
    )
    grad_key, grad_value = key_partial_value
    grad_query, grad_key, grad_value = (grad_query, grad_key, grad_value)
    grad_query = rotate_back(grad_query, cosine_table, sine_table)
    grad_key = rotate_back(grad_key, cosine_table, sine_table)
    grad_projected = (
        jnp.stack([grad_query, grad_key, grad_value], axis=1)
        .reshape(tok_rows, 3 * model_width)
        .astype(jnp.bfloat16)
    )
    grad_qkv = jnp.einsum(
        "td,te->de", residual_first, grad_projected, preferred_element_type=jnp.float32
    )
    grad_hidden_one = jnp.einsum(
        "te,de->td", grad_projected, qkv_back, preferred_element_type=jnp.float32
    )
    grad_scale_attn = grad_hidden_one * normed_one
    input_grad = grad_middle + norm_back(
        grad_hidden_one * (1.0 + scale_attn), normed_one, inverse_one
    )
    grad_modulation = jnp.concatenate(
        [grad_scale_attn, grad_gate_attn, grad_scale_mlp, grad_gate_mlp], axis=1
    )
    grad_blocks = jnp.sum(
        grad_modulation.reshape(tok_rows // BLOCK, BLOCK, 4 * model_width), axis=1
    )
    embedded_float = embedded.astype(jnp.float32)
    halves = (
        lax.psum_scatter(
            grad_qkv.astype(jnp.bfloat16), "fsdp", scatter_dimension=0, tiled=True
        ).astype(jnp.float32),
        lax.psum_scatter(
            grad_out.astype(jnp.bfloat16), "fsdp", scatter_dimension=0, tiled=True
        ).astype(jnp.float32),
        lax.psum_scatter(
            grad_up.astype(jnp.bfloat16), "fsdp", scatter_dimension=0, tiled=True
        ).astype(jnp.float32),
        lax.psum_scatter(
            grad_down.astype(jnp.bfloat16), "fsdp", scatter_dimension=0, tiled=True
        ).astype(jnp.float32),
    )
    totals = lax.psum((halves[0], halves[1], halves[2], halves[3]), "ctx")
    all_embedded, all_blocks = (
        lax.all_gather(embedded_float, ("ctx", "fsdp"), axis=0, tiled=True),
        lax.all_gather(grad_blocks, ("ctx", "fsdp"), axis=0, tiled=True),
    )
    shard_width = model_width // lax.axis_size("fsdp")
    row_start = lax.axis_index("fsdp") * shard_width
    embedded_part = lax.dynamic_slice_in_dim(all_embedded, row_start, shard_width, 1)
    ada_total = jnp.dot(jnp.transpose(embedded_part), all_blocks, precision=highest_precision)
    return (result[None], input_grad[None], totals[0], totals[1], totals[2], totals[3], ada_total)


def remote(source, target, send_sem, recv_sem, **where):
    return pltpu.make_async_remote_copy(
        src_ref=source,
        dst_ref=target,
        send_sem=send_sem,
        recv_sem=recv_sem,
        device_id=where,
        device_id_type=MESH,
    )


def landed(ref, sem):
    pltpu.make_async_copy(ref, ref, sem).wait()


def head_place(me):
    plane = me // 4
    spot = lax.rem(me, 4)
    odd = lax.rem(plane, 2)
    idle = 3 - 2 * odd
    head = 3 * plane + spot - odd * (spot // 2)
    return spot != idle, head


def head_owner(head):
    plane = head // 3
    rank = lax.rem(head, 3)
    odd = lax.rem(plane, 2)
    return 4 * plane + rank + odd * ((rank + 1) // 2)


def scatter_sent(me, heads, source, target, send_sem, recv_sem):
    def finish(head, carry):
        owner = head_owner(head)

        @pl.when(owner != me)
        def _():
            remote(
                source.at[head], target.at[me], send_sem.at[head], recv_sem.at[me], ctx=owner
            ).wait_send()

        return carry

    lax.fori_loop(0, heads, finish, 0)


def return_block(me, head, block, source, target, send_sem, recv_sem):
    @pl.when(block != me)
    def _():
        remote(
            source.at[block], target.at[head], send_sem.at[block], recv_sem.at[head], ctx=block
        ).start()

    @pl.when(block == me)
    def _():
        pltpu.make_async_copy(source.at[block], target.at[head], recv_sem.at[head]).start()


def return_sent(me, head, blocks, source, target, send_sem, recv_sem):
    def finish(block, carry):
        @pl.when(block != me)
        def _():
            remote(
                source.at[block], target.at[head], send_sem.at[block], recv_sem.at[head], ctx=block
            ).wait_send()

        return carry

    lax.fori_loop(0, blocks, finish, 0)


def wait_heads(heads, target, recv_sem):
    def finish(head, carry):
        landed(target.at[head], recv_sem.at[head])
        return carry

    lax.fori_loop(0, heads, finish, 0)


def transposed(values):
    return jnp.transpose(values.astype(jnp.float32)).astype(values.dtype)


def add_into(target, left, right, rows):
    step = 48

    def body(index, carry):
        spot = pl.ds(pl.multiple_of(index * step, step), step)
        total = left(spot).astype(jnp.float32) + right(spot).astype(jnp.float32)
        target(spot, total.astype(jnp.bfloat16))
        return carry

    lax.fori_loop(0, rows // step, body, 0)


def product(left, right):
    return jnp.dot(left, right, preferred_element_type=jnp.float32)


def product_back(left, right):
    return lax.dot_general(
        left, right, (((1,), (1,)), ((), ())), preferred_element_type=jnp.float32
    )


def layer_kernel(
    blocks, heads,
    tok_ref, cot_ref, emb_ref, rope_ref, ada_hbm, qkv_hbm, out_hbm, up_hbm, down_hbm,
    result_ref, ingrad_ref, eds_ref, sds_ref, og_qkv, og_out, og_up, og_down,
    wq, wo, wu, wd, mod_ref, emb_other, part_other, part_send,
    hid1_t, mid_ref, ap_ref, sums_ref, cos_ref, sin_ref,
    qs_ref, buf_ref, mix_ref, lse_ref, att_ref, douts_ref, got_ref,
    parts, sib_ref, row_ref, x_ref, z_ref, line_ref, res_ref, table_ref,
    own_sem, small_send, small_recv, w_send, w_recv,
    fs, fr, fbs, fbr, bs, br, bbs, bbr,
    s_sib, r_sib, s_row, r_row, s_x, r_x, s_z, r_z, s_az, r_az, s_ax, r_ax, s_as, r_as,
    s_t, r_t, out_sem, free_sem,
):
    me = lax.axis_index("ctx")
    row = lax.axis_index("fsdp")
    other = 1 - row
    piece = lax.rem(me, 4)
    core = lax.rem(me, 2)
    xbit = lax.rem(me // 2, 2)
    plane = me // 4
    planes = blocks // 4
    chip_next = jnp.bitwise_xor(me, 2)
    sibling = jnp.bitwise_xor(me, 1)
    gland_ref = qs_ref
    owner, head = head_place(me)
    width = tok_ref.shape[1]
    score_scale = 1.0 / math.sqrt(HD)

    barrier = pltpu.get_barrier_semaphore()
    pl.semaphore_signal(barrier, inc=1, device_id={"fsdp": other}, device_id_type=MESH)

    def greet(step, carry):
        pl.semaphore_signal(
            barrier, inc=1, device_id={"ctx": lax.rem(me + step, blocks)}, device_id_type=MESH
        )
        return carry

    lax.fori_loop(1, blocks, greet, 0)
    pl.semaphore_wait(barrier, blocks)

    shards = (qkv_hbm, out_hbm, up_hbm, down_hbm)
    wholes = (wq, wo, wu, wd)
    quarter_rows = [shard.shape[0] // 4 for shard in shards]
    third = quarter_rows[0] // 3
    chunks = [
        (0, 0, third),
        (0, third, third),
        (0, 2 * third, third),
        (1, 0, 2 * quarter_rows[1]),
        (2, 0, 2 * quarter_rows[2]),
        (3, 0, 2 * quarter_rows[3]),
    ]

    def chunk_start(index, half, which):
        weight, first, count = chunks[index]
        if index > 2:
            return pl.multiple_of(half * 2 * count + lax.rem(which, 2) * count, 16)
        return pl.multiple_of((half * 4 + which) * quarter_rows[weight] + first, 16)

    def chunk_ref(index, which):
        weight, first, count = chunks[index]
        return wholes[weight].at[pl.ds(chunk_start(index, other, which), count)]

    def y_copy(index):
        weight, first, count = chunks[index]
        return remote(
            shards[weight].at[pl.ds(chunk_start(index, 0, piece), count)],
            wholes[weight].at[pl.ds(chunk_start(index, row, piece), count)],
            w_send.at[index, 0], w_recv.at[index, 0], fsdp=other,
        )

    def onward(index, which, slot, peer):
        ref = chunk_ref(index, which)
        return remote(ref, ref, w_send.at[index, slot], w_recv.at[index, slot], ctx=peer)

    def pass_on(index):
        landed(chunk_ref(index, piece), w_recv.at[index, 0])
        if index < 3:
            onward(index, piece, 1, chip_next).start()
        onward(index, piece, 2, sibling).start()

    def pass_last(index):
        across = jnp.bitwise_xor(piece, 2)
        landed(chunk_ref(index, across), w_recv.at[index, 1])
        onward(index, across, 3, sibling).start()

    def chunk_done(index):
        landed(chunk_ref(index, jnp.bitwise_xor(piece, 1)), w_recv.at[index, 2])
        if index < 3:
            landed(chunk_ref(index, jnp.bitwise_xor(piece, 3)), w_recv.at[index, 3])

    def chunk_sent(index):
        y_copy(index).wait_send()
        onward(index, piece, 2, sibling).wait_send()
        if index < 3:
            onward(index, piece, 1, chip_next).wait_send()
            onward(index, jnp.bitwise_xor(piece, 2), 3, sibling).wait_send()

    def own_copy(weight):
        half = shards[weight].shape[0]
        start = pl.multiple_of(row * half, 16)
        return pltpu.make_async_copy(
            shards[weight], wholes[weight].at[pl.ds(start, half)], own_sem.at[weight]
        )

    emb_copy = remote(emb_ref, emb_other, small_send.at[0], small_recv.at[0], fsdp=other)
    emb_copy.start()
    for index in range(3):
        y_copy(index).start()

    def opening(ada_ref, hid1):
        ada_copy = pltpu.make_async_copy(ada_hbm, ada_ref, own_sem.at[4])
        ada_copy.start()
        for weight in range(4):
            own_copy(weight).start()
        normed, unused = layer_norm(tok_ref[...].astype(jnp.float32))
        ingrad_ref[...] = normed
        half_width = width // 2
        cols = pl.ds(pl.multiple_of(row * half_width, 128), half_width)
        ada_copy.wait()
        emb_copy.wait()
        both = jnp.concatenate([emb_ref[:, cols], emb_other[:, cols]], axis=0)
        partial = product(both.astype(jnp.bfloat16), ada_ref[...])
        mod_ref[...] = partial[:8]
        part_send[...] = partial[8:]
        part_copy = remote(part_send, part_other, small_send.at[1], small_recv.at[1], fsdp=other)
        part_copy.start()
        for index in (3, 4, 5):
            y_copy(index).start()
        pass_on(0)
        lanes = lax.broadcasted_iota(jnp.int32, (HD // 2, 128), 1)
        pick = lanes == me
        cos_block = jnp.sum(
            jnp.where(pick, rope_ref[:, 2 * BLOCK : 2 * BLOCK + 128], 0.0), axis=1, keepdims=True
        )
        sin_block = jnp.sum(
            jnp.where(pick, rope_ref[:, 2 * BLOCK + 128 :], 0.0), axis=1, keepdims=True
        )
        cos_row = rope_ref[:, :BLOCK]
        sin_row = rope_ref[:, BLOCK : 2 * BLOCK]
        cos_ref[...] = cos_row * cos_block - sin_row * sin_block
        sin_ref[...] = sin_row * cos_block + cos_row * sin_block
        part_copy.wait()
        mod_ref[...] += part_other[...]
        low = (ingrad_ref[...] * (1.0 + mod_ref[:1, :width])).astype(jnp.bfloat16)
        hid1[...] = low
        pass_on(1)
        hid1_t[...] = transposed(low)
        pass_on(2)
        for index in range(3):
            pass_last(index)
        own_copy(0).wait()
        for index in range(3):
            chunk_done(index)

        def project(group, carry):
            spans = []
            for kind in range(3):
                cols = pl.ds(pl.multiple_of(kind * width + group * 4 * HD, 4 * HD), 4 * HD)
                spans.append(jnp.transpose(product(hid1[...], wq[:, cols])))
            cos, sin = cos_ref[...], sin_ref[...]
            for inner in range(4):
                which = group * 4 + inner
                for kind in range(2):
                    top = spans[kind][inner * HD : inner * HD + HD // 2]
                    low_half = spans[kind][inner * HD + HD // 2 : (inner + 1) * HD]
                    turned = jnp.concatenate(
                        [top * cos - low_half * sin, low_half * cos + top * sin], axis=0
                    ).astype(jnp.bfloat16)
                    if kind == 0:
                        turned = turned * jnp.bfloat16(score_scale)
                    qs_ref[which, kind * HD : (kind + 1) * HD, :] = turned
                qs_ref[which, 2 * HD :, :] = spans[2][inner * HD : (inner + 1) * HD].astype(
                    jnp.bfloat16
                )
            return carry

        lax.fori_loop(0, heads // 4, project, 0)

        def send_block(step, carry):
            send_head(lax.rem(step + 3 * (plane + 2), heads), qs_ref, buf_ref, fs, fr)
            return carry

        lax.fori_loop(0, heads, send_block, 0)

    def send_head(which, source, target, send_sem, recv_sem):
        goal = head_owner(which)

        @pl.when(goal != me)
        def _():
            remote(
                source.at[which], target.at[me], send_sem.at[which], recv_sem.at[me], ctx=goal
            ).start()

        @pl.when(goal == me)
        def _():
            pltpu.make_async_copy(source.at[which], target.at[me], recv_sem.at[me]).start()

    pl.run_scoped(
        opening,
        pltpu.VMEM((width // 2, 4 * width), jnp.bfloat16),
        pltpu.VMEM((BLOCK, width), jnp.bfloat16),
    )

    def forward(pair_ref, low_ref):
        def value_of(key):
            ones = jnp.ones((16, BLOCK), jnp.bfloat16)
            return jnp.concatenate([buf_ref[key, 2 * HD :, :], ones], axis=0)

        def attend(group):
            first = 4 * group
            for inner in range(4):
                block = first + inner
                landed(buf_ref.at[block], fr.at[block])
                rows = pl.ds(pl.multiple_of(block * BLOCK, BLOCK), BLOCK)
                pair_ref[rows, :] = transposed(buf_ref[block, HD:, :])
            query = side_by_side(lambda block: buf_ref[block, :HD, :], first)
            query = jnp.concatenate([query, jnp.zeros_like(query)], axis=0)

            def step(state, key, count, skip):
                high, mixed = state
                rows = pl.ds(pl.multiple_of(key * BLOCK, BLOCK), count * BLOCK)
                begin = (skip or 0) * BLOCK
                scores = product(pair_ref[rows, :], query[:, begin:])
                if skip is not None:
                    scores = jnp.where(seen(scores.shape), scores, masked_score)
                new_high = jnp.maximum(high[:, begin:], jnp.max(scores, axis=0, keepdims=True))
                weights = jnp.exp(scores - new_high).astype(jnp.bfloat16)
                values = jnp.concatenate([value_of(key + index) for index in range(count)], axis=1)
                new_mixed = mixed[:, begin:] * jnp.exp(high[:, begin:] - new_high) + product(
                    values, weights
                )
                if begin:
                    new_high = jnp.concatenate([high[:, :begin], new_high], axis=1)
                    new_mixed = jnp.concatenate([mixed[:, :begin], new_mixed], axis=1)
                return new_high, new_mixed

            state = (
                jnp.full((1, 4 * BLOCK), masked_score, jnp.float32),
                jnp.zeros((HD + 16, 4 * BLOCK), jnp.float32),
            )
            state = lax.fori_loop(
                0, group, lambda index, now: step(now, 4 * index, 4, None), state
            )
            state = step(state, first, 2, 0)
            high, mixed = step(state, first + 2, 2, 2)
            total = mixed[HD : HD + 1]
            mixed = mixed[:HD] / total
            lse = high + jnp.log(total)
            for inner in range(4):
                block = first + inner
                cols = slice(inner * BLOCK, (inner + 1) * BLOCK)
                mix_ref[block] = mixed[:, cols]
                low_ref[block] = mixed[:, cols].astype(jnp.bfloat16)
                lse_ref[block] = jnp.broadcast_to(lse[:, cols], (8, BLOCK))
                return_block(me, head, block, low_ref, att_ref, fbs, fbr)

        def visit(group, carry):
            @pl.when(owner)
            def _():
                attend(group)

            for when in range(2):
                @pl.when(group == when)
                def _(when=when):
                    pass_on(3 + when)

            return carry

        lax.fori_loop(0, blocks // 4, visit, 0)
        pass_on(5)

        @pl.when(owner)
        def _():
            return_sent(me, head, blocks, low_ref, att_ref, fbs, fbr)

        scatter_sent(me, heads, qs_ref, buf_ref, fs, fr)
        wait_heads(heads, att_ref, fbr)

    pl.run_scoped(
        forward,
        pltpu.VMEM((blocks * BLOCK, 2 * HD), jnp.bfloat16),
        pltpu.VMEM((blocks, HD, BLOCK), jnp.bfloat16),
    )

    span = width // 2
    mine = pl.ds(pl.multiple_of(core * span, 128), span)
    theirs = pl.ds(pl.multiple_of((1 - core) * span, 128), span)
    deep = width // 2
    half_deep = deep // 2
    small = half_deep // planes

    def part_of(unit, half, cols):
        return parts.at[unit, half, :, cols]

    def qkv_part(unit, half, cols):
        return wd.at[pl.ds(pl.multiple_of(((unit - 9) * 2 + half) * deep, 16), deep), cols]

    def sib_of(unit, half):
        return sib_ref.at[unit, half]

    def qkv_sib(unit, half):
        cols = pl.ds(pl.multiple_of(((unit - 9) * 2 + half) * span, 128), span)
        return wu.at[pl.ds(0, deep), cols]

    def pipeline(part, sib):
        def to_sibling(unit):
            return [
                remote(part(unit, half, theirs), sib(unit, half),
                       s_sib.at[unit, half], r_sib.at[unit, half], ctx=sibling)
                for half in range(2)
            ]

        def to_row(unit):
            return [remote(sib(unit, other), row_ref.at[unit],
                           s_row.at[unit], r_row.at[unit], fsdp=other)]

        def to_x(unit):
            rows = pl.ds(pl.multiple_of((1 - xbit) * half_deep, 16), half_deep)
            return [remote(row_ref.at[unit, rows], x_ref.at[unit],
                           s_x.at[unit], r_x.at[unit], ctx=chip_next)]

        def to_z(unit):
            copies = []
            for step in range(1, planes):
                goal = lax.rem(plane + step, planes)
                rows = pl.ds(pl.multiple_of(goal * small, 16), small)
                copies.append(
                    remote(x_ref.at[unit, rows], z_ref.at[unit - 9, step - 1],
                           s_z.at[unit, step - 1], r_z.at[unit, step - 1], ctx=4 * goal + piece)
                )
            return copies

        def slab(unit, which):
            rows = pl.ds(pl.multiple_of(xbit * half_deep + which * small, 16), small)
            return res_ref.at[unit, rows, mine]

        def along_z(unit):
            return [
                remote(slab(unit, plane), slab(unit, plane),
                       s_az.at[unit, step - 1], r_az.at[unit, step - 1],
                       ctx=4 * lax.rem(plane + step, planes) + piece)
                for step in range(1, planes)
            ]

        def along_x(unit):
            rows = pl.ds(pl.multiple_of(xbit * half_deep, 16), half_deep)
            ref = res_ref.at[unit, rows, mine]
            return [remote(ref, ref, s_ax.at[unit], r_ax.at[unit], ctx=chip_next)]

        def along_s(unit):
            ref = res_ref.at[unit, :, mine]
            return [remote(ref, ref, s_as.at[unit], r_as.at[unit], ctx=sibling)]

        def launch(copies):
            for copy in copies:
                copy.start()

        def write_out(unit, which, cols):
            side = core if which == 0 else 1 - core
            kind = lax.rem(unit, 4)
            order = 2 * (unit // 4) + lax.rem(kind, 2)

            def save(target):
                pltpu.make_async_copy(
                    res_ref.at[unit, :, cols], target, out_sem.at[unit, which]
                ).start()

            @pl.when((unit < 8) & (kind < 2))
            def _():
                save(og_down.at[pl.ds(pl.multiple_of(order * deep, 16), deep),
                                pl.ds(pl.multiple_of(side * span, 128), span)])

            @pl.when((unit < 8) & (kind >= 2))
            def _():
                start = side * 4 * span + order * span
                save(og_up.at[:, pl.ds(pl.multiple_of(start, 128), span)])

            @pl.when(unit == 8)
            def _():
                save(og_out.at[:, pl.ds(pl.multiple_of(side * span, 128), span)])

            @pl.when(unit > 8)
            def _():
                start = (unit - 9) * width + side * span
                save(og_qkv.at[:, pl.ds(pl.multiple_of(start, 128), span)])

        def stage0(unit):
            launch(to_sibling(unit))

        def stage1(unit):
            for half in range(2):
                landed(sib(unit, half), r_sib.at[unit, half])
                ref, part_ref = sib(unit, half), part(unit, half, mine)

                def put(spot, value, ref=ref):
                    ref[spot, :] = value

                add_into(put, lambda spot, ref=ref: ref[spot, :],
                         lambda spot, part_ref=part_ref: part_ref[spot, :], deep)
            launch(to_row(unit))

        def stage2(unit):
            landed(row_ref.at[unit], r_row.at[unit])
            ref = sib(unit, row)

            def put(spot, value):
                row_ref[unit, spot, :] = value

            add_into(put, lambda spot: row_ref[unit, spot, :], lambda spot: ref[spot, :], deep)
            launch(to_x(unit))
            for make in (to_sibling, to_row):
                for copy in make(unit):
                    copy.wait_send()

        def stage3(unit):
            landed(x_ref.at[unit], r_x.at[unit])
            ref = row_ref.at[unit, pl.ds(pl.multiple_of(xbit * half_deep, 16), half_deep)]

            def put(spot, value):
                x_ref[unit, spot, :] = value

            add_into(put, lambda spot: x_ref[unit, spot, :], lambda spot: ref[spot, :], half_deep)

        def stage3_direct(unit):
            stage3(unit)
            launch(to_z(unit))

        def stage4(unit):
            rows = pl.ds(pl.multiple_of(plane * small, 16), small)
            total = x_ref[unit, rows, :].astype(jnp.float32)
            for step in range(1, planes):
                landed(z_ref.at[unit - 9, step - 1], r_z.at[unit, step - 1])
                total += z_ref[unit - 9, step - 1].astype(jnp.float32)
            spots = pl.ds(pl.multiple_of(xbit * half_deep + plane * small, 16), small)
            res_ref[unit, spots, mine] = total.astype(jnp.bfloat16)
            launch(along_z(unit))

        def stage5(unit):
            for step in range(1, planes):
                landed(slab(unit, lax.rem(plane + planes - step, planes)), r_az.at[unit, step - 1])
            launch(along_x(unit))

        def stage6(unit):
            rows = pl.ds(pl.multiple_of((1 - xbit) * half_deep, 16), half_deep)
            landed(res_ref.at[unit, rows, mine], r_ax.at[unit])
            launch(along_s(unit))
            write_out(unit, 0, mine)

        line_rows = half_deep // 2

        def line_spots(way):
            return pl.ds(way * line_rows, line_rows)

        def line_slab(unit, way):
            rows = pl.ds(pl.multiple_of(xbit * half_deep + way * line_rows, 16), line_rows)
            return res_ref.at[unit, rows, mine]

        def line_sum(unit, way):
            goal = me - 4 if way == 0 else me + 4
            return remote(x_ref.at[unit, line_spots(way)], line_ref.at[unit, way],
                          s_z.at[unit, way], r_z.at[unit, way], ctx=goal)

        def line_back(unit, way):
            goal = me + 4 if way == 0 else me - 4
            return remote(line_slab(unit, way), line_slab(unit, way),
                          s_az.at[unit, way], r_az.at[unit, way], ctx=goal)

        def line_place(way):
            return planes - 1 - plane if way == 0 else plane

        def line_add(unit, way):
            landed(line_ref.at[unit, way], r_z.at[unit, way])
            total = x_ref[unit, line_spots(way), :].astype(jnp.float32)
            return (total + line_ref[unit, way].astype(jnp.float32)).astype(jnp.bfloat16)

        def towards(hop):
            def stage(unit):
                if hop == 0:
                    stage3(unit)
                for way in range(2):
                    @pl.when(line_place(way) == hop)
                    def _(way=way):
                        if hop == planes - 1:
                            line_slab(unit, way)[...] = line_add(unit, way)
                            line_back(unit, way).start()
                            return
                        if hop:
                            x_ref[unit, line_spots(way), :] = line_add(unit, way)
                        line_sum(unit, way).start()

            return stage

        def homewards(hop):
            def stage(unit):
                for way in range(2):
                    @pl.when(line_place(way) == planes - 1 - hop)
                    def _(way=way):
                        landed(line_slab(unit, way), r_az.at[unit, way])
                        if hop < planes - 1:
                            line_back(unit, way).start()

                if hop == planes - 1:
                    launch(along_x(unit))

            return stage

        def close(unit):
            landed(res_ref.at[unit, :, theirs], r_as.at[unit])
            write_out(unit, 1, theirs)
            for make in (to_x, along_x, along_s):
                for copy in make(unit):
                    copy.wait_send()

        def line_close(unit):
            close(unit)
            for way in range(2):
                @pl.when(line_place(way) < planes - 1)
                def _(way=way):
                    line_sum(unit, way).wait_send()

                @pl.when(line_place(way) > 0)
                def _(way=way):
                    line_back(unit, way).wait_send()

        def stage7(unit):
            close(unit)
            for make in (to_z, along_z):
                for copy in make(unit):
                    copy.wait_send()

        line = [towards(hop) for hop in range(planes)]
        line += [homewards(hop) for hop in range(1, planes)]
        direct = [stage3_direct, stage4, stage5, stage6, stage7]
        return stage0, stage1, stage2, line + [stage6, line_close], direct

    early = pipeline(part_of, sib_of)
    late = pipeline(qkv_part, qkv_sib)

    def tick(time, carry):
        for lag, stage in enumerate(early[3]):
            unit = time - lag - 1

            @pl.when((unit >= 0) & (unit < 9))
            def _(stage=stage, unit=unit):
                stage(unit)

        for lag, stage in enumerate(late[4]):
            unit = time - lag - 1

            @pl.when((unit >= 9) & (unit < 12))
            def _(stage=stage, unit=unit):
                stage(unit)

        @pl.when((time >= 0) & (time < 9))
        def _():
            early[2](time)

        @pl.when((time >= 9) & (time < 12))
        def _():
            late[2](time)

        return carry

    def begin(stages, first, last):
        def one(unit, carry):
            stages[1](unit)
            return carry

        lax.fori_loop(first, last, one, 0)

    def ticks(first, last):
        lax.fori_loop(first, last, tick, 0)

    def middle_part(act_ref, slope_ref, hid2, hid2_t, low_ref):
        acc_ref = ingrad_ref
        own_copy(1).wait()
        chunk_done(3)
        att_t = att_ref[...].reshape(width, BLOCK)
        ap_ref[...] = product(transposed(att_t), wo[...])
        gate_attn = mod_ref[:1, width : 2 * width]
        scale_mlp = mod_ref[:1, 2 * width : 3 * width]
        gate_mlp = mod_ref[:1, 3 * width :]
        mid_ref[...] = tok_ref[...].astype(jnp.float32) + gate_attn * ap_ref[...]
        normed, unused = layer_norm(mid_ref[...])
        low = (normed * (1.0 + scale_mlp)).astype(jnp.bfloat16)
        hid2[...] = low
        hid2_t[...] = transposed(low)
        acc_ref[...] = jnp.zeros_like(acc_ref)
        own_copy(2).wait()
        chunk_done(4)
        own_copy(3).wait()
        chunk_done(5)
        curve = math.sqrt(2.0 / math.pi)

        def up(index, carry):
            cols = pl.ds(pl.multiple_of(index * width, width), width)
            before = product(hid2[...], wu[:, cols])
            square = before * before
            bent = jnp.tanh(curve * (before + 0.044715 * (square * before)))
            after = (0.5 * before * (1.0 + bent)).astype(jnp.bfloat16)
            act_ref[:, cols] = after
            slope_ref[:, cols] = 0.5 * (1.0 + bent) + 0.5 * before * (1.0 - bent * bent) * (
                curve * (1.0 + 3.0 * 0.044715 * square)
            )
            acc_ref[...] += product(after, wd[cols, :])
            return carry

        lax.fori_loop(0, 4, up, 0)
        grad = cot_ref[...].astype(jnp.float32)
        mlp_out = acc_ref[...]
        result_ref[...] = mid_ref[...] + gate_mlp * mlp_out
        sums_ref[3:4, :] = jnp.sum(grad * mlp_out, axis=0, keepdims=True)
        low_ref[...] = (grad * gate_mlp).astype(jnp.bfloat16)
        acc_ref[...] = jnp.zeros_like(acc_ref)

        def down(index, carry):
            for side in range(2):
                cols = pl.ds(pl.multiple_of(side * 2 * width + index * width, width), width)
                grad_act = product_back(low_ref[...], wd[cols, :])
                grad_pre = (grad_act * slope_ref[:, cols]).astype(jnp.bfloat16)
                grad_down = product(transposed(act_ref[:, cols]), low_ref[...])
                for pick in range(2):
                    parts[4 * index + pick, side] = grad_down[
                        pick * deep : (pick + 1) * deep
                    ].astype(jnp.bfloat16)
                grad_up = product(hid2_t[...], grad_pre).astype(jnp.bfloat16)
                for pick in range(2):
                    for half in range(2):
                        parts[4 * index + 2 + pick, half, :, side * span : (side + 1) * span] = (
                            grad_up[half * deep : (half + 1) * deep, pick * span : (pick + 1) * span]
                        )
                acc_ref[...] += product_back(grad_pre, wu[:, cols])
            for pick in range(4):
                early[0](4 * index + pick)
            begin(early, 0, 4 * index)
            return carry

        lax.fori_loop(0, 2, down, 0)
        for index in range(len(chunks)):
            chunk_sent(index)
        pl.semaphore_signal(free_sem, inc=1, device_id={"ctx": sibling}, device_id_type=MESH)
        grad_hidden = acc_ref[...]
        normed, inverse = layer_norm(mid_ref[...])
        sums_ref[2:3, :] = jnp.sum(grad_hidden * normed, axis=0, keepdims=True)
        grad_mid = cot_ref[...].astype(jnp.float32) + norm_back(
            grad_hidden * (1.0 + scale_mlp), normed, inverse
        )
        ingrad_ref[...] = grad_mid
        sums_ref[1:2, :] = jnp.sum(grad_mid * ap_ref[...], axis=0, keepdims=True)
        gap = (grad_mid * gate_attn).astype(jnp.bfloat16)
        low_ref[...] = gap
        douts_ref[...] = product_back(wo[...], gap).astype(jnp.bfloat16).reshape(
            heads, HD, BLOCK
        )

        def send_dout(step, carry):
            send_head(lax.rem(step + 3 * (plane + 2), heads), douts_ref, got_ref, bs, br)
            return carry

        lax.fori_loop(0, heads, send_dout, 0)
        begin(early, 4, 8)
        grad_out = product(att_ref[...].reshape(width, BLOCK), low_ref[...]).astype(jnp.bfloat16)
        parts[8, 0] = grad_out[:deep]
        parts[8, 1] = grad_out[deep:]
        early[0](8)
        begin(early, 8, 9)
        ticks(0, FIRST_TICKS)

    pl.run_scoped(
        middle_part,
        pltpu.VMEM((BLOCK, 4 * width), jnp.bfloat16),
        pltpu.VMEM((BLOCK, 4 * width), jnp.float32),
        pltpu.VMEM((BLOCK, width), jnp.bfloat16),
        pltpu.VMEM((width, BLOCK), jnp.bfloat16),
        pltpu.VMEM((BLOCK, width), jnp.bfloat16),
    )

    def backward(both_ref, side_ref, grad_ref, lse_wide, delta_wide, low_ref):
        @pl.when(owner)
        def _():
            def prepare(group, carry):
                first = 4 * group
                for inner in range(4):
                    landed(got_ref.at[first + inner], br.at[first + inner])
                dout = side_by_side(lambda block: got_ref[block], first)
                query = side_by_side(lambda block: buf_ref[block, :HD, :], first)
                mixed = side_by_side(lambda block: mix_ref[block], first)
                both = jnp.concatenate([query, dout], axis=0)
                both_ref[group] = both
                side_ref[group] = transposed(both)
                grad_ref[group] = jnp.zeros((HD, 4 * BLOCK), jnp.float32)
                lse_wide[group] = side_by_side(lambda block: lse_ref[block], first)
                delta = jnp.sum(dout.astype(jnp.float32) * mixed, axis=0, keepdims=True)
                delta_wide[group] = jnp.broadcast_to(delta, (8, 4 * BLOCK))
                return carry

            lax.fori_loop(0, blocks // 4, prepare, 0)

        def key_back(group, inner):
            key = 4 * group + inner
            pair = transposed(buf_ref[key, HD:, :])
            left = lax.broadcasted_iota(jnp.int32, pair.shape, 1) < HD
            none = jnp.zeros_like(pair)
            key_side, value_side = jnp.where(left, pair, none), jnp.where(left, none, pair)
            key_low = buf_ref[key, HD : 2 * HD, :]

            def visit_queries(which, skip, state):
                begin = skip * BLOCK
                both = both_ref[which, :, begin:]
                probs = jnp.exp(product(key_side, both) - lse_wide[which, :1, begin:])
                grad_scores = (
                    probs * (product(value_side, both) - delta_wide[which, :1, begin:])
                ).astype(jnp.bfloat16)
                side = side_ref[which, begin:, :]
                grad_ref[which, :, begin:] += product(key_low, grad_scores)
                return (
                    state[0] + product(grad_scores, side),
                    state[1] + product(probs.astype(jnp.bfloat16), side),
                )

            zero = jnp.zeros((BLOCK, 2 * HD), jnp.float32)
            state = visit_queries(group, inner, (zero, zero))
            state = lax.fori_loop(
                group + 1, blocks // 4, lambda which, now: visit_queries(which, 0, now), state
            )
            low_ref[key, HD : 2 * HD, :] = jnp.transpose(state[0])[:HD].astype(jnp.bfloat16)
            low_ref[key, 2 * HD :, :] = jnp.transpose(state[1])[HD:].astype(jnp.bfloat16)
            return_rows(key, HD, 2 * HD, 0)

        def part_copy_of(block, first, count, slot):
            return remote(
                low_ref.at[block, pl.ds(first, count)], gland_ref.at[head, pl.ds(first, count)],
                bbs.at[block, slot], bbr.at[head, slot], ctx=block,
            )

        def return_rows(block, first, count, slot):
            @pl.when(block != me)
            def _():
                part_copy_of(block, first, count, slot).start()

            @pl.when(block == me)
            def _():
                pltpu.make_async_copy(
                    low_ref.at[block, pl.ds(first, count)],
                    gland_ref.at[head, pl.ds(first, count)],
                    bbr.at[head, slot],
                ).start()

        def visit(step, carry):
            for inner in range(4):
                for edge in range(len(SPLITS) - 1):
                    @pl.when(owner & (step == (len(SPLITS) - 1) * inner + edge))
                    def _(inner=inner, edge=edge):
                        def one(group, carry):
                            key_back(group, inner)
                            return carry

                        lax.fori_loop(SPLITS[edge], SPLITS[edge + 1], one, 0)

            low = sum(jnp.where(step > index, count, 0) for index, count in enumerate(TICKS))
            high = sum(jnp.where(step >= index, count, 0) for index, count in enumerate(TICKS))
            ticks(low + FIRST_TICKS, high + FIRST_TICKS)

            @pl.when(owner & (step == len(TICKS) - 2))
            def _():
                finish_queries()

            return carry

        def finish_queries():
            def finish_query(group, carry):
                grad_query = (grad_ref[group] * score_scale).astype(jnp.bfloat16)
                for inner in range(4):
                    block = 4 * group + inner
                    low_ref[block, :HD, :] = grad_query[:, inner * BLOCK : (inner + 1) * BLOCK]
                    return_rows(block, 0, HD, 1)
                return carry

            lax.fori_loop(0, blocks // 4, finish_query, 0)

        lax.fori_loop(0, len(TICKS), visit, 0)

        @pl.when(owner)
        def _():
            def sent(block, carry):
                @pl.when(block != me)
                def _():
                    part_copy_of(block, HD, 2 * HD, 0).wait_send()
                    part_copy_of(block, 0, HD, 1).wait_send()

                return carry

            lax.fori_loop(0, blocks, sent, 0)

        scatter_sent(me, heads, douts_ref, got_ref, bs, br)

        def arrived(which, carry):
            landed(gland_ref.at[which, pl.ds(HD, 2 * HD)], bbr.at[which, 0])
            landed(gland_ref.at[which, pl.ds(0, HD)], bbr.at[which, 1])
            return carry

        lax.fori_loop(0, heads, arrived, 0)

    pl.run_scoped(
        backward,
        pltpu.VMEM((blocks // 4, 2 * HD, 4 * BLOCK), jnp.bfloat16),
        pltpu.VMEM((blocks // 4, 4 * BLOCK, 2 * HD), jnp.bfloat16),
        pltpu.VMEM((blocks // 4, HD, 4 * BLOCK), jnp.float32),
        pltpu.VMEM((blocks // 4, 8, 4 * BLOCK), jnp.float32),
        pltpu.VMEM((blocks // 4, 8, 4 * BLOCK), jnp.float32),
        pltpu.VMEM((blocks, 3 * HD, BLOCK), jnp.bfloat16),
    )

    def closing(gproj, acc_ref):
        def turn_back(group, carry):
            cos, sin = cos_ref[...], sin_ref[...]
            for kind in range(3):
                pieces = []
                for inner in range(4):
                    which = group * 4 + inner
                    if kind == 2:
                        pieces.append(gland_ref[which, 2 * HD :, :])
                        continue
                    top = gland_ref[which, kind * HD : kind * HD + HD // 2, :].astype(jnp.float32)
                    bottom = gland_ref[
                        which, kind * HD + HD // 2 : (kind + 1) * HD, :
                    ].astype(jnp.float32)
                    pieces.append((top * cos + bottom * sin).astype(jnp.bfloat16))
                    pieces.append((bottom * cos - top * sin).astype(jnp.bfloat16))
                cols = pl.ds(pl.multiple_of(kind * width + group * 4 * HD, 4 * HD), 4 * HD)
                gproj[:, cols] = transposed(jnp.concatenate(pieces, axis=0))
            return carry

        lax.fori_loop(0, heads // 4, turn_back, 0)
        acc_ref[...] = jnp.zeros_like(acc_ref)
        pl.semaphore_wait(free_sem, 1)

        def gradient(index, carry):
            cols = pl.ds(pl.multiple_of(index * width, width), width)
            low = product(hid1_t[...], gproj[:, cols]).astype(jnp.bfloat16)
            wd[pl.ds(pl.multiple_of(index * width, width), width), :] = low
            late[0](9 + index)
            begin(late, 8 + jnp.maximum(index, 1), 9 + index)
            return carry

        lax.fori_loop(0, 3, gradient, 0)

        def back(index, carry):
            cols = pl.ds(pl.multiple_of(index * width, width), width)
            acc_ref[...] += product_back(gproj[:, cols], wq[:, cols])
            return carry

        begin(late, 11, 12)
        lax.fori_loop(0, 3, back, 0)
        normed, inverse = layer_norm(tok_ref[...].astype(jnp.float32))
        grad_hidden = acc_ref[...]
        sums_ref[0:1, :] = jnp.sum(grad_hidden * normed, axis=0, keepdims=True)
        ingrad_ref[...] = ingrad_ref[...] + norm_back(
            grad_hidden * (1.0 + mod_ref[:1, :width]), normed, inverse
        )

    pl.run_scoped(
        closing,
        pltpu.VMEM((BLOCK, 3 * width), jnp.bfloat16),
        pltpu.VMEM((BLOCK, width), jnp.float32),
    )

    def slots(first, count):
        return table_ref.at[pl.ds(first, count)]

    chip_slot = core * 4 * planes + 4 * plane

    def table_row():
        ref = slots(chip_slot + 2 * xbit + row, 1)
        return [remote(ref, ref, s_t.at[0], r_t.at[0], fsdp=other)]

    def table_x():
        ref = slots(chip_slot + 2 * xbit, 2)
        return [remote(ref, ref, s_t.at[1], r_t.at[1], ctx=chip_next)]

    def table_z():
        ref = slots(chip_slot, 4)
        return [
            remote(ref, ref, s_t.at[2 + step], r_t.at[2 + step],
                   ctx=4 * lax.rem(plane + step, planes) + piece)
            for step in range(1, planes)
        ]

    def table_s():
        ref = slots(core * 4 * planes, 4 * planes)
        return [remote(ref, ref, s_t.at[2], r_t.at[2], ctx=sibling)]

    spot = chip_slot + 2 * xbit + row
    for index in range(4):
        table_ref[spot, index : index + 1, :] = sums_ref[index : index + 1, :]
    table_ref[spot, 4:5, :] = emb_ref[:1, :]
    for copy in table_row():
        copy.start()

    begun = FIRST_TICKS + sum(TICKS)

    def finish(time, carry):
        tick(time, carry)

        @pl.when(time == begun + 1)
        def _():
            landed(slots(chip_slot + 2 * xbit + other, 1), r_t.at[0])
            for copy in table_x():
                copy.start()

        @pl.when(time == begun + 3)
        def _():
            landed(slots(chip_slot + 2 * (1 - xbit), 2), r_t.at[1])
            for copy in table_z():
                copy.start()

        @pl.when(time == begun + 5)
        def _():
            for step in range(1, planes):
                goal = lax.rem(plane + planes - step, planes)
                landed(slots(core * 4 * planes + 4 * goal, 4), r_t.at[2 + step])
            for copy in table_s():
                copy.start()

        return carry

    lax.fori_loop(begun, 9 + len(early[3]), finish, 0)
    landed(slots((1 - core) * 4 * planes, 4 * planes), r_t.at[2])
    count = 2 * blocks
    emb_cols = pl.ds(pl.multiple_of(row * (width // 2), 128), width // 2)
    eds = table_ref[:, 4, emb_cols].astype(jnp.bfloat16)
    eds_ref[...] = transposed(jnp.concatenate([eds] * 3, axis=0))
    for index in range(4):
        left = table_ref[:, index, :]
        for third_part in range(3):
            low = left.astype(jnp.bfloat16)
            left = left - low.astype(jnp.float32)
            sds_ref[
                third_part * count : (third_part + 1) * count, index * width : (index + 1) * width
            ] = low
    for copies in (table_row(), table_x(), table_z(), table_s()):
        for copy in copies:
            copy.wait_send()

    def saved(unit, carry):
        for which in range(2):
            pltpu.make_async_copy(
                res_ref.at[unit, :, pl.ds(0, span)], og_out.at[:, pl.ds(0, span)],
                out_sem.at[unit, which],
            ).wait()
        return carry

    lax.fori_loop(0, 12, saved, 0)


def side_by_side(pick, first):
    return jnp.concatenate([pick(first + inner) for inner in range(4)], axis=1)


def seen(shape):
    keys = lax.broadcasted_iota(jnp.int32, shape, 0) // BLOCK
    return keys <= lax.broadcasted_iota(jnp.int32, shape, 1) // BLOCK


FIRST_TICKS = 1
TICKS = (1, 1, 1, 1, 1, 0, 1, 0, 2)
SPLITS = (0, 1, 4)


def widen_kernel(*refs):
    lows, eds_ref, sds_ref = refs[2:6], refs[6], refs[7]
    outs = refs[8:]
    for source, target in zip(refs[:2], outs[:2]):
        target[...] = source[...]
    for source, target in zip(lows, outs[2:6]):
        target[...] = source[...].astype(jnp.float32)
    outs[6][...] = product(eds_ref[...], sds_ref[...])


def widen(result, input_grad, sums, eds, sds):
    steps = WIDEN_STEPS

    def rows_of(array):
        return pl.BlockSpec((array.shape[0] // steps, array.shape[1]), lambda index: (index, 0))

    ada = jax.ShapeDtypeStruct((eds.shape[0], sds.shape[1]), jnp.float32)
    arrays = [result, input_grad, *sums]
    outs = [jax.ShapeDtypeStruct(array.shape, jnp.float32) for array in arrays] + [ada]
    got = pl.pallas_call(
        widen_kernel,
        grid=(steps,),
        out_shape=outs,
        in_specs=[rows_of(array) for array in arrays]
        + [rows_of(eds), pl.BlockSpec(sds.shape, lambda index: (0, 0))],
        out_specs=[rows_of(array) for array in outs],
        compiler_params=pltpu.CompilerParams(vmem_limit_bytes=VMEM_LIMIT),
    )(*arrays, eds, sds)
    return got[0], got[1], got[2:6], got[6]


WIDEN_STEPS = 4


def rope_constants(blocks):
    half = HD // 2
    frequency = rope_base ** (-2.0 * np.arange(half, dtype=np.float64) / HD)
    inner = frequency[:, None] * np.arange(BLOCK, dtype=np.float64)[None, :]
    outer = frequency[:, None] * (BLOCK * np.arange(128, dtype=np.float64))[None, :]
    outer = np.where(np.arange(128)[None, :] < blocks, outer, 0.0)
    return np.concatenate(
        [np.cos(inner), np.sin(inner), np.cos(outer), np.sin(outer)], axis=1
    ).astype(np.float32)


def fast_device(tokens, timestep, time_table, w_qkv, w_out, w_up, w_down, w_ada, cotangent):
    rows, width = tokens.shape[1:]
    heads = width // HD
    blocks = lax.axis_size("ctx")
    planes = blocks // 4
    deep, span = width // 2, width // 2
    embedded = lax.dynamic_slice_in_dim(time_table, timestep[0, 0], 1, 0)
    embedded = embedded.astype(jnp.bfloat16).astype(jnp.float32)
    emb_rows = jnp.broadcast_to(embedded, (8, width))
    hbm = pl.BlockSpec(memory_space=pl.ANY)
    vmem = pl.BlockSpec(memory_space=pltpu.VMEM)
    low, high = jnp.bfloat16, jnp.float32
    dma = pltpu.SemaphoreType.DMA
    steps = planes - 1
    units = 12
    scratch = [
        pltpu.VMEM((width, 3 * width), low),
        pltpu.VMEM((width, width), low),
        pltpu.VMEM((width, 4 * width), low),
        pltpu.VMEM((4 * width, width), low),
        pltpu.VMEM((8, 4 * width), high),
        pltpu.VMEM((8, width), high),
        pltpu.VMEM((8, 4 * width), high),
        pltpu.VMEM((8, 4 * width), high),
        pltpu.VMEM((width, BLOCK), low),
        pltpu.VMEM((BLOCK, width), high),
        pltpu.VMEM((BLOCK, width), high),
        pltpu.VMEM((8, width), high),
        pltpu.VMEM((HD // 2, BLOCK), high),
        pltpu.VMEM((HD // 2, BLOCK), high),
        pltpu.VMEM((heads, 3 * HD, BLOCK), low),
        pltpu.VMEM((blocks, 3 * HD, BLOCK), low),
        pltpu.VMEM((blocks, HD, BLOCK), high),
        pltpu.VMEM((blocks, 8, BLOCK), high),
        pltpu.VMEM((heads, HD, BLOCK), low),
        pltpu.VMEM((heads, HD, BLOCK), low),
        pltpu.VMEM((blocks, HD, BLOCK), low),
        pltpu.VMEM((9, 2, deep, width), low),
        pltpu.VMEM((9, 2, deep, span), low),
        pltpu.VMEM((units, deep, span), low),
        pltpu.VMEM((units, deep // 2, span), low),
        pltpu.VMEM((3, steps, deep // 2 // planes, span), low),
        pltpu.VMEM((9, 2, deep // 4, span), low),
        pltpu.VMEM((units, deep, width), low),
        pltpu.VMEM((2 * blocks, 8, width), high),
    ]
    sems = [
        (5,), (2,), (2,), (6, 4), (6, 4),
        (heads,), (blocks,), (blocks,), (heads,),
        (heads,), (blocks,), (blocks, 2), (heads, 2),
        (units, 2), (units, 2), (units,), (units,), (units,), (units,),
        (units, steps), (units, steps), (units, steps), (units, steps),
        (units,), (units,), (units,), (units,), (planes + 2,), (planes + 2,), (units, 2),
    ]
    scratch += [dma(shape) for shape in sems] + [pltpu.SemaphoreType.REGULAR]
    result, input_grad, eds, sds, *sums = pl.pallas_call(
        functools.partial(layer_kernel, blocks, heads),
        out_shape=[
            jax.ShapeDtypeStruct((rows, width), high),
            jax.ShapeDtypeStruct((rows, width), high),
            jax.ShapeDtypeStruct((deep, 6 * blocks), low),
            jax.ShapeDtypeStruct((6 * blocks, 4 * width), low),
        ]
        + [jax.ShapeDtypeStruct(w.shape, low) for w in (w_qkv, w_out, w_up, w_down)],
        in_specs=[vmem] * 4 + [hbm] * 5,
        out_specs=[vmem] * 4 + [hbm] * 4,
        scratch_shapes=scratch,
        compiler_params=pltpu.CompilerParams(
            collective_id=1, has_side_effects=True, vmem_limit_bytes=VMEM_LIMIT
        ),
    )(tokens[0], cotangent[0], emb_rows, jnp.asarray(rope_constants(blocks)),
      w_ada, w_qkv, w_out, w_up, w_down)
    result, input_grad, totals, ada_total = widen(result, input_grad, sums, eds, sds)
    return (result[None], input_grad[None], *totals, ada_total)


def solution(mesh):
    chosen = fast_device if mesh.shape["ctx"] == 16 else on_device
    return jax.shard_map(
        chosen,
        mesh=mesh,
        in_specs=(
            P("fsdp", "ctx", None),
            P("fsdp", "ctx"),
            P(),
            P("fsdp", None),
            P("fsdp", None),
            P("fsdp", None),
            P("fsdp", None),
            P("fsdp", None),
            P("fsdp", "ctx", None),
        ),
        out_specs=(
            P("fsdp", "ctx", None),
            P("fsdp", "ctx", None),
            P("fsdp", None),
            P("fsdp", None),
            P("fsdp", None),
            P("fsdp", None),
            P("fsdp", None),
        ),
        check_vma=False,
    )
```
